32 devices in a mesh: dp: 16 (over z, x, core), fsdp: 2 (over y).
Axes of the slice: x: 2, y: 2, z: 4, core: 2. Of those that a mesh axis runs over, the one named last changes fastest.
Arguments:
- patches: bfloat16 [32, 1024, 768], P(('dp', 'fsdp')), may hold values from -6 to 6
- page_ids: int32 [32, 1024], P(('dp', 'fsdp')), may hold values from 0 to 15, never falling along the last dimension, each value on 1 to 512 neighbouring positions
- patch_rows: int32 [32, 1024], P(('dp', 'fsdp')), may hold values from 0 to 63
- live_len: int32 [32, 1], P(('dp', 'fsdp')), may hold values from 768 to 1024
- norm1_gain: bfloat16 [768], P('fsdp'), may hold values from 0.5 to 1.5
- norm1_bias: bfloat16 [768], P('fsdp'), may hold values from -2 to 2
- w_qkv: bfloat16 [768, 2304], P('fsdp'), may hold values from -0.21875 to 0.21875
- bias_qv: bfloat16 [1536], P('fsdp'), may hold values from -2 to 2
- rel_table: bfloat16 [32, 12], P('fsdp'), may hold values from -3 to 3
- w_proj: bfloat16 [768, 768], P('fsdp'), may hold values from -0.875 to 0.875
- bias_proj: bfloat16 [768], P('fsdp'), may hold values from -2 to 2
- scale_attn: bfloat16 [768], P('fsdp'), may hold values from 0.5 to 1.5
- norm2_gain: bfloat16 [768], P('fsdp'), may hold values from 0.5 to 1.5
- norm2_bias: bfloat16 [768], P('fsdp'), may hold values from -2 to 2
- w_up: bfloat16 [768, 3072], P('fsdp'), may hold values from -0.21875 to 0.21875
- bias_up: bfloat16 [3072], P('fsdp'), may hold values from -2 to 2
- w_down: bfloat16 [3072, 768], P('fsdp'), may hold values from -0.109375 to 0.109375
- bias_down: bfloat16 [768], P('fsdp'), may hold values from -2 to 2
- scale_mlp: bfloat16 [768], P('fsdp'), may hold values from 0.5 to 1.5
- cotangent: bfloat16 [32, 1024, 768], P(('dp', 'fsdp')), may hold values from -6 to 6
Outputs:
- layer_out: bfloat16 [32, 1024, 768], P(('dp', 'fsdp'))
- grad_patches: float32 [32, 1024, 768], P(('dp', 'fsdp'))
- grad_norm1_gain: float32 [768], P('fsdp')
- grad_norm1_bias: float32 [768], P('fsdp')
- grad_w_qkv: float32 [768, 2304], P('fsdp')
- grad_bias_qv: float32 [1536], P('fsdp')
- grad_rel_table: float32 [32, 12], P('fsdp')
- grad_w_proj: float32 [768, 768], P('fsdp')
- grad_bias_proj: float32 [768], P('fsdp')
- grad_scale_attn: float32 [768], P('fsdp')
- grad_norm2_gain: float32 [768], P('fsdp')
- grad_norm2_bias: float32 [768], P('fsdp')
- grad_w_up: float32 [768, 3072], P('fsdp')
- grad_bias_up: float32 [3072], P('fsdp')
- grad_w_down: float32 [3072, 768], P('fsdp')
- grad_bias_down: float32 [768], P('fsdp')
- grad_scale_mlp: float32 [768], P('fsdp')
The draws below stay inside these ranges and needn't reach their ends.
Inputs may be any that keep to these rules, and one draw needn't show every extreme that they name: `page_ids`: within each pack the page numbers never fall and run through 0 to 15; a page has 1 to 512 patches, and some page has exactly 512. Patches at positions live_len and beyond of a pack are padding.
All inputs are finite; a program needn't handle non-finite values.
Results may differ from the reference program's by a relative error of at most 0.0097.
Values may be sent and summed in bfloat16 or wider, within the bound.
No kernel may reach another device: no remote copies, remote signals or barrier semaphores. Data moves between devices by JAX's collectives and lax.ppermute only.
A program may use at most 320 MiB of HBM per device.

```python
import math
import jax
import jax.numpy as jnp
import numpy as np
from jax import lax

D = 768
HEADS = 12
HEAD = 64
FF = 3072
NB = 32
PACK = 1024
PAGES = 16
PAGE_MAX = 512
PACKS = 32


def with_ends(array, stream_key, smallest, high):
    spot = [jax.random.randint(jax.random.fold_in(stream_key, axis), (), 0, length) for axis, length in enumerate(array.shape)]
    longest = array.shape.index(max(array.shape))
    next_to = spot[:longest] + [(spot[longest] + 1) % array.shape[longest]] + spot[longest + 1:]
    return array.at[tuple(spot)].set(smallest).at[tuple(next_to)].set(high)


def level_of(key, extent, shards, least, high):
    level, own = 1.0, jax.random.fold_in(key, 6)
    for dim, blocks in shards:
        heights = jnp.exp(jax.random.uniform(jax.random.fold_in(own, dim), (blocks,), jnp.float32, least / len(shards), high / len(shards)))
        level = level * jnp.repeat(heights, extent[dim] // blocks).reshape([-1 if axis == dim else 1 for axis in range(len(extent))])
    return level


def length_profile(amount, total, bound, slope):
    portions = [(1 << 20) // math.isqrt(rank ** slope) + 1 for rank in range(2, amount + 1)]
    spare, counts = total - bound - (amount - 1), [1] * (amount - 1)
    while spare > 0:
        movable = [i for i in range(amount - 1) if counts[i] < bound]
        mass, remaining = sum([portions[i] for i in movable]), spare
        for i in movable:
            addition = min(bound - counts[i], max(1, remaining * portions[i] // mass), spare)
            counts[i] = counts[i] + addition
            spare = spare - addition
    return np.array([bound] + counts)


def ragged(key, count, total, reach, lean):
    if count == 2:
        one = jax.random.randint(key, (), max(1, total - reach), min(reach, total - 1) + 1)
        return jnp.stack([one, total - one])
    tallies = jnp.asarray(length_profile(count, total, reach, lean), jnp.int32)
    pairs = (count - 1) // 2
    giver, sink = tallies[1:1 + 2 * pairs:2], tallies[2:2 + 2 * pairs:2]
    margin = jnp.minimum(giver - 1, reach - sink)
    shifted = jax.random.randint(jax.random.fold_in(key, 1), (pairs,), 0, 1 << 20) % (margin + 1)
    tallies = tallies.at[1:1 + 2 * pairs:2].set(giver - shifted).at[2:2 + 2 * pairs:2].set(sink + shifted)
    return tallies[jax.random.permutation(jax.random.fold_in(key, 2), count)]


def scatter_about(key, extent, deviation, reach, cuts=(), held_as=jnp.bfloat16):
    factor_of = level_of(key, extent, cuts, -0.22, 0.18) if cuts else 1.0
    entries = jax.random.normal(key, extent, jnp.float32) * deviation * factor_of
    return jnp.minimum(jnp.maximum(entries, -reach), reach).astype(held_as)


def setup_inputs(seed: int = 0) -> dict:
    streams_of = jax.random.split(jax.random.key(seed), 21)
    patches = scatter_about(streams_of[0], (PACKS, PACK, D), 1.0, 6.0, ((0, 32),))
    page_ids = jax.vmap(lambda own: jnp.searchsorted(jnp.cumsum(ragged(own, PAGES, PACK, PAGE_MAX, 2)), jnp.arange(PACK), side="right"))(jax.random.split(streams_of[1], PACKS)).reshape((PACKS, PACK)).astype(jnp.int32)
    patch_rows = with_ends(jax.random.randint(streams_of[2], (PACKS, PACK), 0, 2 * NB), jax.random.fold_in(streams_of[2], 1), 0, (2 * NB) - 1).astype(jnp.int32)
    live_len = with_ends(jax.random.randint(streams_of[3], (PACKS, 1), PACK - PACK // 4, PACK + 1), jax.random.fold_in(streams_of[3], 1), PACK - PACK // 4, PACK).astype(jnp.int32)
    norm1_gain = jnp.clip(0.5 + 1.0 * jax.random.uniform(streams_of[4], (D,), jnp.float32) ** level_of(streams_of[4], (D,), ((0, 2),), -0.2, 0.2), 0.5, 1.5).astype(jnp.bfloat16)
    norm1_bias = scatter_about(streams_of[5], (D,), 0.3, 2.0, ((0, 2),))
    w_qkv = scatter_about(streams_of[6], (D, 3 * D), D ** -0.5, 0.21875, ((0, 2),))
    bias_qv = scatter_about(streams_of[7], (2 * D,), 0.3, 2.0, ((0, 2),))
    rel_table = scatter_about(streams_of[8], (NB, HEADS), 1.0, 3.0, ((0, 2),))
    w_proj = scatter_about(streams_of[9], (D, D), (D // 16) ** -0.5, 0.875, ((0, 2),))
    bias_proj = scatter_about(streams_of[10], (D,), 0.3, 2.0, ((0, 2),))
    scale_attn = jnp.clip(0.5 + 1.0 * jax.random.uniform(streams_of[11], (D,), jnp.float32) ** level_of(streams_of[11], (D,), ((0, 2),), -0.2, 0.2), 0.5, 1.5).astype(jnp.bfloat16)
    norm2_gain = jnp.clip(0.5 + 1.0 * jax.random.uniform(streams_of[12], (D,), jnp.float32) ** level_of(streams_of[12], (D,), ((0, 2),), -0.2, 0.2), 0.5, 1.5).astype(jnp.bfloat16)
    norm2_bias = scatter_about(streams_of[13], (D,), 0.3, 2.0, ((0, 2),))
    w_up = scatter_about(streams_of[14], (D, FF), D ** -0.5, 0.21875, ((0, 2),))
    bias_up = scatter_about(streams_of[15], (FF,), 0.3, 2.0, ((0, 2),))
    w_down = scatter_about(streams_of[16], (FF, D), FF ** -0.5, 0.109375, ((0, 2),))
    bias_down = scatter_about(streams_of[17], (D,), 0.3, 2.0, ((0, 2),))
    scale_mlp = jnp.clip(0.5 + 1.0 * jax.random.uniform(streams_of[18], (D,), jnp.float32) ** level_of(streams_of[18], (D,), ((0, 2),), -0.2, 0.2), 0.5, 1.5).astype(jnp.bfloat16)
    cotangent = scatter_about(streams_of[19], (PACKS, PACK, D), 1.0, 6.0, ((0, 32),))
    return dict(patches=patches, page_ids=page_ids, patch_rows=patch_rows, live_len=live_len, norm1_gain=norm1_gain, norm1_bias=norm1_bias, w_qkv=w_qkv, bias_qv=bias_qv, rel_table=rel_table, w_proj=w_proj, bias_proj=bias_proj, scale_attn=scale_attn, norm2_gain=norm2_gain, norm2_bias=norm2_bias, w_up=w_up, bias_up=bias_up, w_down=w_down, bias_down=bias_down, scale_mlp=scale_mlp, cotangent=cotangent)


EPSILON = 1e-06

@jax.custom_vjp
def low(v):
    return lax.optimization_barrier(v.astype(jnp.bfloat16)).astype(jnp.float32)

@jax.custom_vjp
def low_back(v):
    return v

def low_keep(v):
    return (low(v), None)

def low_pass(kept, grad):
    return (grad,)

def back_keep(v):
    return (v, None)

def back_low(kept, grad):
    return (low(grad),)
low.defvjp(low_keep, low_pass)
low_back.defvjp(back_keep, back_low)

def matmul(left, right):
    return jnp.dot(left, right, precision=lax.Precision.HIGHEST, preferred_element_type=jnp.float32)

def norm_rows(values, gain, shift):
    center = values - lax.optimization_barrier(jnp.mean(values, axis=-1, keepdims=True))
    spread = lax.optimization_barrier(jnp.mean(center * center, axis=-1, keepdims=True))
    return center * lax.rsqrt(spread + EPSILON) * gain + shift

def pack_attention(query, keyset, valueset, page_row, place_row, live_row, table):
    heads_query = query.reshape(PACK, HEADS, HEAD)
    heads_key = keyset.reshape(PACK, HEADS, HEAD)
    heads_value = valueset.reshape(PACK, HEADS, HEAD)
    logits = jnp.einsum('qhd,khd->hqk', heads_query, heads_key, precision=lax.Precision.HIGHEST) * HEAD ** (-0.5)
    bucket = jnp.clip(place_row[:, None] - place_row[None, :] + NB // 2, 0, NB - 1).astype(jnp.int32)
    logits = logits + jnp.transpose(table[bucket], (2, 0, 1))
    places = jnp.arange(PACK, dtype=jnp.int32)
    allowed = (page_row[:, None] == page_row[None, :]) & (places[None, :] < live_row) | (places[:, None] == places[None, :])
    logits = low_back(jnp.where(allowed[None], logits, -1e+30))
    weights = low(jax.nn.softmax(logits, axis=-1))
    mixed = jnp.einsum('hqk,khd->qhd', weights, heads_value, precision=lax.Precision.HIGHEST)
    return mixed.reshape(PACK, D)

def forward(inputs, gain1, shift1, weight_qkv, bias_qkv, table, weight_proj, bias_out, layer_scale1, gain2, shift2, weight_up, bias_hidden, weight_down, bias_last, layer_scale2, page_ids, patch_rows, live_len):
    flat = inputs.reshape(-1, D)
    normed1 = low(norm_rows(flat, gain1, shift1))
    projected = matmul(normed1, weight_qkv)
    query = low(low_back(projected[:, :D] + bias_qkv[:D]))
    keyset = low(low_back(projected[:, D:2 * D]))
    valueset = low(low_back(projected[:, 2 * D:] + bias_qkv[D:]))

    def one_pack(pieces):
        return pack_attention(pieces[0], pieces[1], pieces[2], pieces[3], pieces[4], pieces[5], table)
    attended = lax.map(jax.checkpoint(one_pack), (query.reshape(-1, PACK, D), keyset.reshape(-1, PACK, D), valueset.reshape(-1, PACK, D), page_ids, patch_rows, live_len[:, 0]))
    attended = low(low_back(attended.reshape(-1, D)))
    branch_a = low_back(matmul(attended, weight_proj) + bias_out)
    resid1 = flat + layer_scale1 * branch_a
    normed2 = low(norm_rows(resid1, gain2, shift2))
    upper = low_back(matmul(normed2, weight_up) + bias_hidden)
    activ = low(jax.nn.gelu(upper, approximate=True))
    branch_m = low_back(matmul(activ, weight_down) + bias_last)
    output = resid1 + layer_scale2 * branch_m
    return output.reshape(inputs.shape)

def reference(patches, page_ids, patch_rows, live_len, norm1_gain, norm1_bias, w_qkv, bias_qv, rel_table, w_proj, bias_proj, scale_attn, norm2_gain, norm2_bias, w_up, bias_up, w_down, bias_down, scale_mlp, cotangent):
    params = tuple((item.astype(jnp.float32) for item in (norm1_gain, norm1_bias, w_qkv, bias_qv, rel_table, w_proj, bias_proj, scale_attn, norm2_gain, norm2_bias, w_up, bias_up, w_down, bias_down, scale_mlp)))

    def run(inputs, *weights):
        return forward(inputs, *weights, page_ids, patch_rows, live_len)
    output, pull = jax.vjp(run, patches.astype(jnp.float32), *params)
    grads = pull(cotangent.astype(jnp.float32))
    return (output.astype(jnp.bfloat16), grads[0], grads[1], grads[2], grads[3], grads[4], grads[5], grads[6], grads[7], grads[8], grads[9], grads[10], grads[11], grads[12], grads[13], grads[14], grads[15])
```

```python
import jax
import jax.numpy as jnp
from jax import lax
from jax.experimental import pallas as pl
from jax.experimental.pallas import tpu as pltpu
from jax.sharding import PartitionSpec as P

HEADS = 12
HEAD = 64
NB = 32
ROWS = 64
PAGES = 16
LONGEST = 512
DEAD_SPAN = 256
EPSILON = 1e-06
BIG = 2.0**100
NN = (((1,), (0,)), ((), ()))
NT = (((1,), (1,)), ((), ()))
TN = (((0,), (0,)), ((), ()))
F32 = jnp.float32
BF16 = jnp.bfloat16


def dg(left, right, dims):
    return lax.dot_general(left, right, dims, preferred_element_type=F32)


def split3(value):
    high = value.astype(BF16)
    rest = value - high.astype(F32)
    mid = rest.astype(BF16)
    low = (rest - mid.astype(F32)).astype(BF16)
    return high, mid, low


def side_tables(page, place, live):
    total = page.shape[0]
    shape = (total, 128)
    lane = lax.broadcasted_iota(jnp.int32, shape, 1)
    pos = lax.broadcasted_iota(jnp.int32, shape, 0)
    page = page[:, None]
    place = place[:, None]
    high = (pos % DEAD_SPAN) // 16
    low = pos % 16
    early = pos < total - DEAD_SPAN
    select = (
        (lane == place)
        | (lane == 64 + page)
        | (lane == 80 + high)
        | (lane == 96 + low)
        | (early & (lane >= 80) & (lane < 112))
    )
    query_side = select.astype(BF16)
    dead = pos >= live
    other_page = jnp.logical_not(dead) & (lane >= 64) & (lane < 80) & (lane != 64 + page)
    other_place = dead & (
        ((lane >= 80) & (lane < 96) & (lane != 80 + high))
        | ((lane >= 96) & (lane < 112) & (lane != 96 + low))
    )
    one = (lane == place) | ((lane >= 112) & (lane < 115))
    key_side = jnp.where(other_page | other_place, -BIG, jnp.where(one, 1.0, 0.0)).astype(BF16)
    return query_side, key_side


def mix_kernel(table_ref, mix_ref):
    head = pl.program_id(0)
    row = lax.broadcasted_iota(jnp.int32, (128, 128), 0)
    col = lax.broadcasted_iota(jnp.int32, (128, 128), 1)
    bucket = jnp.clip(row - col + NB // 2, 0, NB - 1)
    bias = jnp.zeros((128, 128), F32)
    for number in range(NB):
        bias = jnp.where(bucket == number, table_ref[number, head], bias)
    keep = (row == col) & (row >= ROWS) & (row < 112)
    mix = jnp.where((row < ROWS) & (col < ROWS), bias, jnp.where(keep, 1.0, 0.0))
    mix_ref[0] = mix.astype(BF16)


def bias_mix(table):
    return pl.pallas_call(
        mix_kernel,
        grid=(HEADS,),
        in_specs=[pl.BlockSpec(memory_space=pltpu.SMEM)],
        out_specs=pl.BlockSpec((1, 128, 128), lambda head: (head, 0, 0)),
        out_shape=jax.ShapeDtypeStruct((HEADS, 128, 128), BF16),
        name="bias_mix",
    )(table.astype(F32))


def attention_kernel(q_ref, k_ref, v_ref, f_ref, g_ref, m_ref, o_ref, l_ref):
    pair = pl.program_id(1)
    size = q_ref.shape[0]
    q = q_ref[...].astype(F32) * HEAD**-0.5
    v = v_ref[...]
    lane = lax.broadcasted_iota(jnp.int32, (size, 128), 1)
    keys = jnp.concatenate([k_ref[...], g_ref[...]], axis=1)
    f = f_ref[...]

    @pl.when(pair == 0)
    def _():
        l_ref[...] = jnp.zeros_like(l_ref)

    lse = l_ref[...]
    out = None
    for h in range(2):
        mine = (lane // HEAD) == h
        extra = dg(f, m_ref[h], NN).astype(BF16)
        queries = jnp.concatenate([jnp.where(mine, q, 0.0).astype(BF16), extra], axis=1)
        score = dg(queries, keys, NT)
        top = jnp.max(score, axis=1, keepdims=True)
        expo = jnp.exp(score - top)
        denom = jnp.sum(expo, axis=1, keepdims=True)
        part = dg(expo.astype(BF16), jnp.where(mine, v, jnp.zeros_like(v)), NN) / denom
        out = part if out is None else out + part
        lse = jnp.where(lane == 2 * pair + h, top + jnp.log(denom), lse)
    o_ref[...] = out.astype(BF16)
    l_ref[...] = lse


def attention(qkv, query_side, key_side, mix):
    total, width3 = qkv.shape
    width = width3 // 3
    pairs = width // 128
    size = LONGEST
    blocks = total // size
    area = blocks * size * size
    return pl.pallas_call(
        attention_kernel,
        grid=(blocks, pairs),
        in_specs=[
            pl.BlockSpec((size, 128), lambda b, h: (b, h)),
            pl.BlockSpec((size, 128), lambda b, h: (b, pairs + h)),
            pl.BlockSpec((size, 128), lambda b, h: (b, 2 * pairs + h)),
            pl.BlockSpec((size, 128), lambda b, h: (b, 0)),
            pl.BlockSpec((size, 128), lambda b, h: (b, 0)),
            pl.BlockSpec((2, 128, 128), lambda b, h: (h, 0, 0)),
        ],
        out_specs=[
            pl.BlockSpec((size, 128), lambda b, h: (b, h)),
            pl.BlockSpec((size, 128), lambda b, h: (b, 0)),
        ],
        out_shape=[
            jax.ShapeDtypeStruct((total, width), BF16),
            jax.ShapeDtypeStruct((total, 128), F32),
        ],
        cost_estimate=pl.CostEstimate(
            flops=2 * 2 * pairs * area * 512, transcendentals=2 * pairs * area, bytes_accessed=8 * total * width
        ),
        name="attention",
    )(qkv, qkv, qkv, query_side, key_side, mix)


def attention_back_kernel(
    q_ref, k_ref, v_ref, da_ref, o_ref, l_ref, f_ref, g_ref, m_ref, d_ref, sum_ref, tab_ref
):
    pair = pl.program_id(0)
    block = pl.program_id(1)
    size = q_ref.shape[0]
    lane = lax.broadcasted_iota(jnp.int32, (size, 128), 1)
    q = q_ref[...].astype(F32) * HEAD**-0.5
    v = v_ref[...]
    da = da_ref[...]
    product = da.astype(F32) * o_ref[...].astype(F32)
    f = f_ref[...]
    keys = jnp.concatenate([k_ref[...], g_ref[...]], axis=1)
    values = jnp.concatenate([v, jnp.where(lane < 3, 1.0, 0.0).astype(BF16)], axis=1)
    lse_all = l_ref[...]
    dq, dk, dv = None, None, None
    for h in range(2):
        mine = (lane // HEAD) == h
        extra = dg(f, m_ref[h], NN)
        lse = jnp.sum(jnp.where(lane == 2 * pair + h, lse_all, 0.0), axis=1, keepdims=True)
        for place, piece in enumerate(split3(-lse)):
            extra = jnp.where(lane == 112 + place, piece.astype(F32), extra)
        qm = jnp.where(mine, q, 0.0).astype(BF16)
        queries = jnp.concatenate([qm, extra.astype(BF16)], axis=1)
        delta = jnp.sum(jnp.where(mine, product, 0.0), axis=1, keepdims=True)
        columns = jnp.zeros((size, 128), F32)
        for place, piece in enumerate(split3(-delta)):
            columns = jnp.where(lane == place, piece.astype(F32), columns)
        dam = jnp.where(mine, da, jnp.zeros_like(da))
        prob = jnp.exp(dg(keys, queries, NT))
        dprob = dg(values, jnp.concatenate([dam, columns.astype(BF16)], axis=1), NT)
        dscore = (prob * dprob).astype(BF16)
        dvh = dg(prob.astype(BF16), dam, NN)
        dkh = dg(dscore, qm, NN)
        both = dg(dscore, keys, TN)
        dv = dvh if dv is None else dv + dvh
        dk = dkh if dk is None else dk + dkh
        dq = both[:, :128] if dq is None else jnp.where(mine, both[:, :128], dq)
        rows = both[:, 128:]
        rows_high = rows.astype(BF16)
        rows_low = (rows - rows_high.astype(F32)).astype(BF16)
        grid = dg(f, jnp.concatenate([rows_high, rows_low], axis=1), TN)
        grid = grid[:ROWS, :128] + grid[:ROWS, 128:]

        @pl.when(block == 0)
        def _():
            tab_ref[h] = grid

        @pl.when(block > 0)
        def _():
            tab_ref[h] += grid

    dq = (dq * HEAD**-0.5).astype(BF16)
    dk = dk.astype(BF16)
    dv = dv.astype(BF16)
    d_ref[0] = dq
    d_ref[1] = dk
    d_ref[2] = dv
    sums = jnp.concatenate(
        [
            jnp.sum(dq.astype(F32), axis=0, keepdims=True),
            jnp.sum(dv.astype(F32), axis=0, keepdims=True),
            jnp.zeros((6, 128), F32),
        ],
        axis=0,
    )

    @pl.when(block == 0)
    def _():
        sum_ref[...] = sums

    @pl.when(block > 0)
    def _():
        sum_ref[...] += sums


def attention_back(qkv, d_attended, attended, lse, query_side, key_side, mix):
    total, width3 = qkv.shape
    width = width3 // 3
    pairs = width // 128
    size = LONGEST
    blocks = total // size
    area = blocks * size * size
    wide = lambda h, b: (b, h)
    side = lambda h, b: (b, 0)
    return pl.pallas_call(
        attention_back_kernel,
        grid=(pairs, blocks),
        in_specs=[
            pl.BlockSpec((size, 128), wide),
            pl.BlockSpec((size, 128), lambda h, b: (b, pairs + h)),
            pl.BlockSpec((size, 128), lambda h, b: (b, 2 * pairs + h)),
            pl.BlockSpec((size, 128), wide),
            pl.BlockSpec((size, 128), wide),
            pl.BlockSpec((size, 128), side),
            pl.BlockSpec((size, 128), side),
            pl.BlockSpec((size, 128), side),
            pl.BlockSpec((2, 128, 128), lambda h, b: (h, 0, 0)),
        ],
        out_specs=[
            pl.BlockSpec((3, size, 128), lambda h, b: (0, b, h)),
            pl.BlockSpec((8, 128), lambda h, b: (0, h)),
            pl.BlockSpec((2, ROWS, 128), lambda h, b: (h, 0, 0)),
        ],
        out_shape=[
            jax.ShapeDtypeStruct((3, total, width), BF16),
            jax.ShapeDtypeStruct((8, width), F32),
            jax.ShapeDtypeStruct((2 * pairs, ROWS, 128), F32),
        ],
        cost_estimate=pl.CostEstimate(
            flops=2 * 2 * pairs * area * 1024, transcendentals=2 * pairs * area, bytes_accessed=20 * total * width
        ),
        name="attention_back",
    )(qkv, qkv, qkv, d_attended, attended, lse, query_side, key_side, mix)


def table_gradient(tab):
    row = jnp.arange(ROWS, dtype=jnp.int32)
    bucket = jnp.clip(row[:, None] - row[None, :] + NB // 2, 0, NB - 1)
    onehot = (bucket[:, :, None] == jnp.arange(NB, dtype=jnp.int32)).astype(F32)
    return jnp.einsum("hij,ijb->bh", tab[:, :, :ROWS], onehot, precision=lax.Precision.HIGHEST)


class Links:
    def __init__(self, dp, fsdp):
        self.dp, self.fsdp = dp, fsdp
        self.fast = fsdp == 2 and dp >= 4 and dp & (dp - 1) == 0
        here = lax.axis_index("dp")
        self.core = here % 2
        self.x = (here // 2) % 2
        self.y = lax.axis_index("fsdp")

    def swap(self, value, mask):
        return lax.ppermute(value, "dp", [(i, i ^ mask) for i in range(self.dp)])

    def swap_y(self, value):
        return lax.ppermute(value, "fsdp", [(0, 1), (1, 0)])

    def order(self, bit, own, other, axis=0):
        first = bit == 0
        return jnp.concatenate(
            [jnp.where(first, own, other), jnp.where(first, other, own)], axis=axis
        )

    def gather(self, shards):
        if not self.fast:
            return [lax.all_gather(shard, "fsdp", axis=0, tiled=True) for shard in shards]
        rows = shards[0].shape[0]
        quarter = rows // 4
        start = (2 * self.core + self.x) * quarter
        piece = jnp.concatenate(
            [lax.dynamic_slice_in_dim(shard, start, quarter, 0) for shard in shards], axis=1
        )
        first = self.swap_y(piece)
        second = self.swap(first, 2)
        half = self.order(self.x, first, second)
        rest = self.swap(half, 1)
        wholes = []
        at = 0
        for shard in shards:
            width = shard.shape[1]
            far = self.order(self.core, half[:, at : at + width], rest[:, at : at + width])
            wholes.append(self.order(self.y, shard, far))
            at += width
        return wholes

    def gather_small(self, shard):
        if not self.fast:
            return lax.all_gather(shard, "fsdp", axis=0, tiled=False)
        far = self.swap_y(shard)
        return self.order(self.y, shard[None], far[None])

    def reduce(self, grads):
        if not self.fast:
            outs = []
            for grad in grads:
                share = lax.psum_scatter(grad.astype(F32), "fsdp", scatter_dimension=0, tiled=True)
                outs.append(lax.psum(share, "dp"))
            return outs
        rows = grads[0].shape[0] // 2
        half = rows // 2

        def pick(start):
            return jnp.concatenate(
                [
                    lax.dynamic_slice_in_dim(grad.reshape(2, rows, -1), start, half, 1)
                    for grad in grads
                ],
                axis=2,
            )

        def add(left, right):
            return (left.astype(F32) + right.astype(F32)).astype(BF16)

        got = self.swap(pick((1 - self.core) * half), 1)
        total = add(pick(self.core * half), got)
        got = self.swap_y(lax.dynamic_index_in_dim(total, 1 - self.y, 0, False))
        total = add(lax.dynamic_index_in_dim(total, self.y, 0, False), got)
        part = half // 2
        got = self.swap(lax.dynamic_slice_in_dim(total, (1 - self.x) * part, part, 0), 2)
        total = add(lax.dynamic_slice_in_dim(total, self.x * part, part, 0), got)
        mask = 4
        while mask < self.dp:
            total = add(total, self.swap(total, mask))
            mask *= 2
        total = self.order(self.x, total, self.swap(total, 2))
        rest = self.swap(total, 1)
        outs = []
        at = 0
        for grad in grads:
            width = grad.shape[1]
            outs.append(
                self.order(self.core, total[:, at : at + width], rest[:, at : at + width]).astype(F32)
            )
            at += width
        return outs

    def reduce_small(self, grads):
        sizes = [grad.size // self.fsdp for grad in grads]
        flat = jnp.concatenate([grad.reshape(self.fsdp, -1) for grad in grads], axis=1)
        if not self.fast:
            total = lax.psum(flat, "dp")
            total = lax.psum_scatter(total, "fsdp", scatter_dimension=0, tiled=True)[0]
        else:
            got = self.swap_y(lax.dynamic_index_in_dim(flat, 1 - self.y, 0, True))
            total = lax.dynamic_index_in_dim(flat, self.y, 0, True) + got
            mask = 1
            while mask < self.dp:
                total = total + self.swap(total, mask)
                mask *= 2
            total = total[0]
        outs = []
        at = 0
        for grad, size in zip(grads, sizes):
            piece = total[at : at + size]
            outs.append(piece.reshape((grad.shape[0] // self.fsdp,) + grad.shape[1:]))
            at += size
        return outs


def norm_parts(values):
    center = values - jnp.mean(values, axis=-1, keepdims=True)
    spread = jnp.mean(center * center, axis=-1, keepdims=True)
    scale = lax.rsqrt(spread + EPSILON)
    return center * scale, scale


def norm_back(grad, unit, scale, gain):
    inner = grad * gain
    mean = jnp.mean(inner, axis=-1, keepdims=True)
    mixed = jnp.mean(inner * unit, axis=-1, keepdims=True)
    return scale * (inner - mean - unit * mixed)


def gelu_parts(upper):
    c = 0.7978845608028654
    square = upper * upper
    wave = jnp.tanh(c * (upper + 0.044715 * upper * square))
    value = 0.5 * upper * (1.0 + wave)
    slope = 0.5 * (1.0 + wave) + 0.5 * upper * (1.0 - wave * wave) * c * (1.0 + 3 * 0.044715 * square)
    return value, slope


def make_body(dp, fsdp):
    def body(
        patches,
        page_ids,
        patch_rows,
        live_len,
        norm1_gain,
        norm1_bias,
        w_qkv,
        bias_qv,
        rel_table,
        w_proj,
        bias_proj,
        scale_attn,
        norm2_gain,
        norm2_bias,
        w_up,
        bias_up,
        w_down,
        bias_down,
        scale_mlp,
        cotangent,
    ):
        links = Links(dp, fsdp)
        smalls = (
            norm1_gain,
            norm1_bias,
            bias_qv,
            rel_table,
            bias_proj,
            scale_attn,
            norm2_gain,
            norm2_bias,
            bias_up,
            bias_down,
            scale_mlp,
        )
        packed = links.gather_small(jnp.concatenate([small.reshape(-1) for small in smalls]))
        whole = []
        at = 0
        for small in smalls:
            piece = packed[:, at : at + small.size]
            whole.append(piece.reshape((small.shape[0] * fsdp,) + small.shape[1:]).astype(F32))
            at += small.size
        gain1, shift1, bias_qv_f, table, bias_out, scale1, gain2, shift2, bias_hidden, bias_last, scale2 = whole
        (weight_qkv,) = links.gather([w_qkv])
        weight_proj, weight_up = links.gather([w_proj, w_up])
        (weight_down,) = links.gather([w_down])

        total, width = patches.shape[1:]
        page = page_ids[0]
        place = patch_rows[0]
        live = live_len[0, 0]

        starts = jnp.arange(total - LONGEST + 1, dtype=jnp.int32)
        found = page[: total - LONGEST + 1] == page[LONGEST - 1 :]
        start = jnp.min(jnp.where(found, starts, total))
        row = lax.broadcasted_iota(jnp.int32, (total, total), 0)
        col = lax.broadcasted_iota(jnp.int32, (total, total), 1)
        turn = (col == (row + start) % total).astype(BF16)
        query_side, key_side = side_tables(page, place, live)
        turned = jnp.dot(
            turn,
            jnp.concatenate([patches[0], cotangent[0], query_side, key_side], axis=1),
            preferred_element_type=F32,
        ).astype(BF16)
        flat = turned[:, :width].astype(F32)
        grad_out = turned[:, width : 2 * width].astype(F32)
        query_side = turned[:, 2 * width : 2 * width + 128]
        key_side = turned[:, 2 * width + 128 :]

        unit1, rstd1 = norm_parts(flat)
        normed1 = (unit1 * gain1 + shift1).astype(BF16)
        bias_all = jnp.concatenate([bias_qv_f[:width], jnp.zeros((width,), F32), bias_qv_f[width:]])
        qkv = (jnp.dot(normed1, weight_qkv, preferred_element_type=F32) + bias_all).astype(BF16)
        mix = bias_mix(table)
        attended, lse = attention(qkv, query_side, key_side, mix)
        branch_a = jnp.dot(attended, weight_proj, preferred_element_type=F32) + bias_out
        resid1 = flat + scale1 * branch_a
        unit2, rstd2 = norm_parts(resid1)
        normed2 = (unit2 * gain2 + shift2).astype(BF16)
        upper = jnp.dot(normed2, weight_up, preferred_element_type=F32) + bias_hidden
        activ_f, slope = gelu_parts(upper)
        activ = activ_f.astype(BF16)
        branch_m = jnp.dot(activ, weight_down, preferred_element_type=F32) + bias_last
        output = (resid1 + scale2 * branch_m).astype(BF16)

        grad_scale_mlp = jnp.sum(grad_out * branch_m, axis=0)
        grad_mlp = (scale2 * grad_out).astype(BF16)
        grad_w_down = dg(activ, grad_mlp, TN).astype(BF16)
        (out_w_down,) = links.reduce([grad_w_down])
        grad_bias_down = jnp.sum(grad_mlp.astype(F32), axis=0)
        grad_upper = (dg(grad_mlp, weight_down, NT) * slope).astype(BF16)
        grad_w_up = dg(normed2, grad_upper, TN).astype(BF16)
        grad_bias_up = jnp.sum(grad_upper.astype(F32), axis=0)
        grad_normed2 = dg(grad_upper, weight_up, NT)
        grad_norm2_gain = jnp.sum(grad_normed2 * unit2, axis=0)
        grad_norm2_bias = jnp.sum(grad_normed2, axis=0)
        grad_resid1 = grad_out + norm_back(grad_normed2, unit2, rstd2, gain2)
        grad_scale_attn = jnp.sum(grad_resid1 * branch_a, axis=0)
        grad_branch = (scale1 * grad_resid1).astype(BF16)
        grad_w_proj = dg(attended, grad_branch, TN).astype(BF16)
        out_w_proj, out_w_up = links.reduce([grad_w_proj, grad_w_up])
        grad_bias_proj = jnp.sum(grad_branch.astype(F32), axis=0)
        grad_attended = dg(grad_branch, weight_proj, NT).astype(BF16)
        grad_qkv, sums, tab = attention_back(
            qkv, grad_attended, attended, lse, query_side, key_side, mix
        )
        grad_w_qkv = jnp.concatenate([dg(normed1, grad_qkv[i], TN) for i in range(3)], axis=1).astype(BF16)
        (out_w_qkv,) = links.reduce([grad_w_qkv])
        grad_bias_qv = jnp.concatenate([sums[0], sums[1]])
        grad_rel_table = table_gradient(tab)
        grad_normed1 = sum(dg(grad_qkv[i], weight_qkv[:, i * width : (i + 1) * width], NT) for i in range(3))
        grad_norm1_gain = jnp.sum(grad_normed1 * unit1, axis=0)
        grad_norm1_bias = jnp.sum(grad_normed1, axis=0)
        grad_inputs = grad_resid1 + norm_back(grad_normed1, unit1, rstd1, gain1)
        high = grad_inputs.astype(BF16)
        low = (grad_inputs - high.astype(F32)).astype(BF16)
        back = dg(turn, jnp.concatenate([output, high, low], axis=1), TN)
        layer_out = back[:, :width].astype(BF16)
        grad_patches = back[:, width : 2 * width] + back[:, 2 * width :]
        small_outs = links.reduce_small(
            [
                grad_norm1_gain,
                grad_norm1_bias,
                grad_bias_qv,
                grad_rel_table,
                grad_bias_proj,
                grad_scale_attn,
                grad_norm2_gain,
                grad_norm2_bias,
                grad_bias_up,
                grad_bias_down,
                grad_scale_mlp,
            ]
        )
        return (
            layer_out[None],
            grad_patches[None],
            small_outs[0],
            small_outs[1],
            out_w_qkv,
            small_outs[2],
            small_outs[3],
            out_w_proj,
            small_outs[4],
            small_outs[5],
            small_outs[6],
            small_outs[7],
            out_w_up,
            small_outs[8],
            out_w_down,
            small_outs[9],
            small_outs[10],
        )

    return body


def solution(mesh):
    rows = P(("dp", "fsdp"), None, None)
    ids = P(("dp", "fsdp"), None)
    vector = P("fsdp")
    matrix = P("fsdp", None)
    in_specs = (
        rows,
        ids,
        ids,
        ids,
        vector,
        vector,
        matrix,
        vector,
        matrix,
        matrix,
        vector,
        vector,
        vector,
        vector,
        matrix,
        vector,
        matrix,
        vector,
        vector,
        rows,
    )
    out_specs = (
        rows,
        rows,
        vector,
        vector,
        matrix,
        vector,
        matrix,
        matrix,
        vector,
        vector,
        vector,
        vector,
        matrix,
        vector,
        matrix,
        vector,
        vector,
    )
    body = make_body(mesh.shape["dp"], mesh.shape["fsdp"])
    return jax.shard_map(body, mesh=mesh, in_specs=in_specs, out_specs=out_specs, check_vma=False)
```

```python
import jax
import jax.numpy as jnp
from jax import lax
from jax.experimental import pallas as pl
from jax.experimental.pallas import tpu as pltpu
from jax.sharding import PartitionSpec as P

HEADS = 12
HEAD = 64
NB = 32
ROWS = 64
PAGES = 16
LONGEST = 512
DEAD_SPAN = 256
EPSILON = 1e-06
BIG = 2.0**100
NN = (((1,), (0,)), ((), ()))
NT = (((1,), (1,)), ((), ()))
TN = (((0,), (0,)), ((), ()))
TINY = pl.CostEstimate(flops=1000, transcendentals=0, bytes_accessed=1000)
MIB = 2**20
F32 = jnp.float32
BF16 = jnp.bfloat16


def dg(left, right, dims):
    return lax.dot_general(left, right, dims, preferred_element_type=F32)


def split3(value):
    high = value.astype(BF16)
    rest = value - high.astype(F32)
    mid = rest.astype(BF16)
    low = (rest - mid.astype(F32)).astype(BF16)
    return high, mid, low


def mix_kernel(table_ref, mix_ref):
    head = pl.program_id(0)
    row = lax.broadcasted_iota(jnp.int32, (128, 128), 0)
    col = lax.broadcasted_iota(jnp.int32, (128, 128), 1)
    bucket = jnp.clip(row - col + NB // 2, 0, NB - 1)
    bias = jnp.zeros((128, 128), F32)
    for number in range(NB):
        bias = jnp.where(bucket == number, table_ref[number, head], bias)
    keep = (row == col) & (row >= ROWS) & (row < 112)
    mix = jnp.where((row < ROWS) & (col < ROWS), bias, jnp.where(keep, 1.0, 0.0))
    mix_ref[0] = mix.astype(BF16)


def bias_mix(table):
    return pl.pallas_call(
        mix_kernel,
        grid=(HEADS,),
        in_specs=[pl.BlockSpec(memory_space=pltpu.SMEM)],
        out_specs=pl.BlockSpec((1, 128, 128), lambda head: (head, 0, 0)),
        out_shape=jax.ShapeDtypeStruct((HEADS, 128, 128), BF16),
        compiler_params=pltpu.CompilerParams(vmem_limit_bytes=28 * MIB),
        name="bias_mix",
    )(table.astype(F32))


def attention_kernel(q_ref, k_ref, v_ref, f_ref, g_ref, m_ref, o_ref, l_ref):
    pair = pl.program_id(1)
    size = q_ref.shape[0]
    q = q_ref[...].astype(F32) * HEAD**-0.5
    v = v_ref[...]
    lane = lax.broadcasted_iota(jnp.int32, (size, 128), 1)
    keys = jnp.concatenate([k_ref[...], g_ref[...]], axis=1)
    f = f_ref[...]

    @pl.when(pair == 0)
    def _():
        l_ref[...] = jnp.zeros_like(l_ref)

    lse = l_ref[...]
    out = None
    for h in range(2):
        mine = (lane // HEAD) == h
        extra = dg(f, m_ref[h], NN).astype(BF16)
        queries = jnp.concatenate([jnp.where(mine, q, 0.0).astype(BF16), extra], axis=1)
        score = dg(queries, keys, NT)
        top = jnp.max(score, axis=1, keepdims=True)
        expo = jnp.exp(score - top)
        denom = jnp.sum(expo, axis=1, keepdims=True)
        part = dg(expo.astype(BF16), jnp.where(mine, v, jnp.zeros_like(v)), NN) / denom
        out = part if out is None else out + part
        lse = jnp.where(lane == 2 * pair + h, top + jnp.log(denom), lse)
    o_ref[...] = out.astype(BF16)
    l_ref[...] = lse


def attention(qkv, query_side, key_side, mix):
    total, width3 = qkv.shape
    width = width3 // 3
    pairs = width // 128
    size = LONGEST
    blocks = total // size
    area = blocks * size * size
    return pl.pallas_call(
        attention_kernel,
        grid=(blocks, pairs),
        in_specs=[
            pl.BlockSpec((size, 128), lambda b, h: (b, h)),
            pl.BlockSpec((size, 128), lambda b, h: (b, pairs + h)),
            pl.BlockSpec((size, 128), lambda b, h: (b, 2 * pairs + h)),
            pl.BlockSpec((size, 128), lambda b, h: (b, 0)),
            pl.BlockSpec((size, 128), lambda b, h: (b, 0)),
            pl.BlockSpec((2, 128, 128), lambda b, h: (h, 0, 0)),
        ],
        out_specs=[
            pl.BlockSpec((size, 128), lambda b, h: (b, h)),
            pl.BlockSpec((size, 128), lambda b, h: (b, 0)),
        ],
        out_shape=[
            jax.ShapeDtypeStruct((total, width), BF16),
            jax.ShapeDtypeStruct((total, 128), F32),
        ],
        cost_estimate=TINY,
        compiler_params=pltpu.CompilerParams(vmem_limit_bytes=28 * MIB),
        name="attention",
    )(qkv, qkv, qkv, query_side, key_side, mix)


def make_attention_back_kernel(first):
    def kernel(q_ref, k_ref, v_ref, da_ref, o_ref, l_ref, f_ref, g_ref, m_ref, d_ref, sum_ref, tab_ref):
        pair = pl.program_id(0) + first
        block = pl.program_id(1)
        size = q_ref.shape[0]
        lane = lax.broadcasted_iota(jnp.int32, (size, 128), 1)
        q = q_ref[...].astype(F32) * HEAD**-0.5
        v = v_ref[...]
        da = da_ref[...]
        product = da.astype(F32) * o_ref[...].astype(F32)
        f = f_ref[...]
        keys = jnp.concatenate([k_ref[...], g_ref[...]], axis=1)
        values = jnp.concatenate([v, jnp.where(lane < 3, 1.0, 0.0).astype(BF16)], axis=1)
        lse_all = l_ref[...]
        dq, dk, dv = None, None, None
        for h in range(2):
            mine = (lane // HEAD) == h
            extra = dg(f, m_ref[h], NN)
            lse = jnp.sum(jnp.where(lane == 2 * pair + h, lse_all, 0.0), axis=1, keepdims=True)
            for place, piece in enumerate(split3(-lse)):
                extra = jnp.where(lane == 112 + place, piece.astype(F32), extra)
            qm = jnp.where(mine, q, 0.0).astype(BF16)
            queries = jnp.concatenate([qm, extra.astype(BF16)], axis=1)
            delta = jnp.sum(jnp.where(mine, product, 0.0), axis=1, keepdims=True)
            columns = jnp.zeros((size, 128), F32)
            for place, piece in enumerate(split3(-delta)):
                columns = jnp.where(lane == place, piece.astype(F32), columns)
            dam = jnp.where(mine, da, jnp.zeros_like(da))
            prob = jnp.exp(dg(keys, queries, NT))
            dprob = dg(values, jnp.concatenate([dam, columns.astype(BF16)], axis=1), NT)
            dscore = (prob * dprob).astype(BF16)
            dvh = dg(prob.astype(BF16), dam, NN)
            dkh = dg(dscore, qm, NN)
            both = dg(dscore, keys, TN)
            dv = dvh if dv is None else dv + dvh
            dk = dkh if dk is None else dk + dkh
            dq = both[:, :128] if dq is None else jnp.where(mine, both[:, :128], dq)
            rows = both[:, 128:]
            rows_high = rows.astype(BF16)
            rows_low = (rows - rows_high.astype(F32)).astype(BF16)
            grid = dg(f, jnp.concatenate([rows_high, rows_low], axis=1), TN)
            grid = grid[:ROWS, :128] + grid[:ROWS, 128:]

            @pl.when(block == 0)
            def _():
                tab_ref[h] = grid

            @pl.when(block > 0)
            def _():
                tab_ref[h] += grid

        dq = (dq * HEAD**-0.5).astype(BF16)
        dk = dk.astype(BF16)
        dv = dv.astype(BF16)
        d_ref[0] = dq
        d_ref[1] = dk
        d_ref[2] = dv
        sums = jnp.concatenate(
            [
                jnp.sum(dq.astype(F32), axis=0, keepdims=True),
                jnp.sum(dv.astype(F32), axis=0, keepdims=True),
                jnp.zeros((6, 128), F32),
            ],
            axis=0,
        )

        @pl.when(block == 0)
        def _():
            sum_ref[...] = sums

        @pl.when(block > 0)
        def _():
            sum_ref[...] += sums

    return kernel


def attention_back(qkv, d_attended, attended, lse, query_side, key_side, mix, first, count):
    total, width3 = qkv.shape
    pairs = width3 // 3 // 128
    size = LONGEST
    blocks = total // size
    wide = lambda h, b: (b, first + h)
    side = lambda h, b: (b, 0)
    return pl.pallas_call(
        make_attention_back_kernel(first),
        grid=(count, blocks),
        in_specs=[
            pl.BlockSpec((size, 128), wide),
            pl.BlockSpec((size, 128), lambda h, b: (b, pairs + first + h)),
            pl.BlockSpec((size, 128), lambda h, b: (b, 2 * pairs + first + h)),
            pl.BlockSpec((size, 128), wide),
            pl.BlockSpec((size, 128), wide),
            pl.BlockSpec((size, 128), side),
            pl.BlockSpec((size, 128), side),
            pl.BlockSpec((size, 128), side),
            pl.BlockSpec((2, 128, 128), lambda h, b: (first + h, 0, 0)),
        ],
        out_specs=[
            pl.BlockSpec((3, size, 128), lambda h, b: (0, b, h)),
            pl.BlockSpec((8, 128), lambda h, b: (0, h)),
            pl.BlockSpec((2, ROWS, 128), lambda h, b: (h, 0, 0)),
        ],
        out_shape=[
            jax.ShapeDtypeStruct((3, total, 128 * count), BF16),
            jax.ShapeDtypeStruct((8, 128 * count), F32),
            jax.ShapeDtypeStruct((2 * count, ROWS, 128), F32),
        ],
        cost_estimate=TINY,
        compiler_params=pltpu.CompilerParams(vmem_limit_bytes=28 * MIB),
        name="attention_back",
    )(qkv, qkv, qkv, d_attended, attended, lse, query_side, key_side, mix)


def table_gradient(tab):
    row = jnp.arange(ROWS, dtype=jnp.int32)
    bucket = jnp.clip(row[:, None] - row[None, :] + NB // 2, 0, NB - 1)
    onehot = (bucket[:, :, None] == jnp.arange(NB, dtype=jnp.int32)).astype(F32)
    return jnp.einsum("hij,ijb->bh", tab[:, :, :ROWS], onehot, precision=lax.Precision.HIGHEST)


def rotate_kernel(page_ref, place_ref, live_ref, x_ref, c_ref, xo_ref, co_ref, f_ref, g_ref):
    size = xo_ref.shape[0]
    total = x_ref.shape[0]
    page = page_ref[...]
    place = place_ref[...]
    start = page_start(page)
    row = lax.broadcasted_iota(jnp.int32, (size, total), 0) + pl.program_id(0) * size
    col = lax.broadcasted_iota(jnp.int32, (size, total), 1)
    source = row + start
    source = jnp.where(source >= total, source - total, source)
    turn = jnp.where(col == source, 1.0, 0.0).astype(BF16)
    xo_ref[...] = dg(turn, x_ref[...], NN).astype(BF16)
    co_ref[...] = dg(turn, c_ref[...], NN).astype(BF16)
    line = lax.broadcasted_iota(jnp.int32, (128, total), 0)
    pos = lax.broadcasted_iota(jnp.int32, (128, total), 1)
    span = pos & (DEAD_SPAN - 1)
    high = 80 + (span >> 4)
    low = 96 + (span & 15)
    early = pos < total - DEAD_SPAN
    in_high = (line >= 80) & (line < 96)
    in_low = (line >= 96) & (line < 112)
    select = (
        (line == place)
        | (line == 64 + page)
        | (line == high)
        | (line == low)
        | (early & (in_high | in_low))
    )
    dead = pos >= live_ref[0, 0]
    other_page = jnp.logical_not(dead) & (line >= 64) & (line < 80) & (line != 64 + page)
    other_place = dead & ((in_high & (line != high)) | (in_low & (line != low)))
    one = (line == place) | ((line >= 112) & (line < 115))
    query_side = jnp.where(select, 1.0, 0.0).astype(BF16)
    key_side = jnp.where(other_page | other_place, -BIG, jnp.where(one, 1.0, 0.0)).astype(BF16)
    f_ref[...] = dg(turn, query_side, NT).astype(BF16)
    g_ref[...] = dg(turn, key_side, NT).astype(BF16)


def rotate(page_ids, patch_rows, live_len, patches, cotangent):
    total, width = patches.shape
    size = 256
    full = lambda i: (0, 0)
    rows = lambda i: (i, 0)
    return pl.pallas_call(
        rotate_kernel,
        grid=(total // size,),
        in_specs=[
            pl.BlockSpec((1, total), full),
            pl.BlockSpec((1, total), full),
            pl.BlockSpec(memory_space=pltpu.SMEM),
            pl.BlockSpec((total, width), full),
            pl.BlockSpec((total, width), full),
        ],
        out_specs=[
            pl.BlockSpec((size, width), rows),
            pl.BlockSpec((size, width), rows),
            pl.BlockSpec((size, 128), rows),
            pl.BlockSpec((size, 128), rows),
        ],
        out_shape=[
            jax.ShapeDtypeStruct((total, width), BF16),
            jax.ShapeDtypeStruct((total, width), BF16),
            jax.ShapeDtypeStruct((total, 128), BF16),
            jax.ShapeDtypeStruct((total, 128), BF16),
        ],
        cost_estimate=TINY,
        compiler_params=pltpu.CompilerParams(vmem_limit_bytes=28 * MIB),
        name="rotate",
    )(page_ids, patch_rows, live_len, patches, cotangent)


def norm_parts(values):
    center = values - jnp.mean(values, axis=-1, keepdims=True)
    spread = jnp.mean(center * center, axis=-1, keepdims=True)
    scale = lax.rsqrt(spread + EPSILON)
    return center * scale, scale


def norm_back(grad, unit, scale, gain):
    inner = grad * gain
    mean = jnp.mean(inner, axis=-1, keepdims=True)
    mixed = jnp.mean(inner * unit, axis=-1, keepdims=True)
    return scale * (inner - mean - unit * mixed)


def gelu_parts(upper):
    c = 0.7978845608028654
    square = upper * upper
    wave = jnp.tanh(upper * (c + (c * 0.044715) * square))
    half = 0.5 + 0.5 * wave
    value = upper * half
    slope = half + (value * (1.0 - wave)) * (c + (3 * c * 0.044715) * square)
    return value, slope


GAIN1, SHIFT1, SCALE1, BIAS_OUT, GAIN2, SHIFT2, SCALE2, BIAS_LAST = range(8)


ANY = pl.BlockSpec(memory_space=pl.ANY)


class Weight:
    def __init__(self, arrays, rows, columns, at=0):
        self.arrays, self.rows, self.columns, self.at = tuple(arrays), rows, columns, at

    def copies(self, refs, spot_ref, target, sem, column=0, columns=None, to=0):
        columns = columns or self.columns
        lanes = pl.ds(to, columns)
        if len(refs) == 1:
            return [pltpu.make_async_copy(refs[0].at[:, pl.ds(column, columns)], target.at[:, lanes], sem)]
        y, me = spot_ref[0], spot_ref[1]
        size = self.rows // 2
        quarter = size // 4
        start = pl.multiple_of(y * size, 16)
        jobs = [
            pltpu.make_async_copy(refs[0].at[:, pl.ds(column, columns)], target.at[pl.ds(start, size), lanes], sem)
        ]
        for number, ref in enumerate(refs[1:]):
            start = pl.multiple_of((1 - y) * size + (me ^ number) * quarter, 16)
            jobs.append(
                pltpu.make_async_copy(
                    ref.at[:, pl.ds(self.at + column, columns)], target.at[pl.ds(start, quarter), lanes], sem
                )
            )
        return jobs


def outside(arrays):
    return [pltpu.with_memory_space_constraint(array, pltpu.HBM) for array in arrays]


def run_copies(jobs):
    for job in jobs:
        job.start()
    for job in jobs:
        job.wait()


def make_qkv_kernel(weight):
    count = len(weight.arrays)

    def kernel(spot_ref, x_ref, vec_ref, bias_ref, *refs):
        normed_ref, qkv_ref, w, sem = refs[count:]

        @pl.when(pl.program_id(0) == 0)
        def _():
            run_copies(weight.copies(refs[:count], spot_ref, w, sem))

        unit, _ = norm_parts(x_ref[...].astype(F32))
        normed = (unit * vec_ref[GAIN1 : GAIN1 + 1] + vec_ref[SHIFT1 : SHIFT1 + 1]).astype(BF16)
        normed_ref[...] = normed
        qkv_ref[...] = (dg(normed, w[...], NN) + bias_ref[...]).astype(BF16)

    return kernel


def project_qkv(spot, x, vectors, bias, weight):
    total, width = x.shape
    size = 256
    wide = weight.columns
    full = lambda i, s: (0, 0)
    rows = lambda i, s: (i, 0)
    return pl.pallas_call(
        make_qkv_kernel(weight),
        grid_spec=pltpu.PrefetchScalarGridSpec(
            num_scalar_prefetch=1,
            grid=(total // size,),
            in_specs=[
                pl.BlockSpec((size, width), rows),
                pl.BlockSpec((8, width), full),
                pl.BlockSpec((1, wide), full),
            ]
            + [ANY] * len(weight.arrays),
            out_specs=[pl.BlockSpec((size, width), rows), pl.BlockSpec((size, wide), rows)],
            scratch_shapes=[pltpu.VMEM((width, wide), BF16), pltpu.SemaphoreType.DMA],
        ),
        out_shape=[
            jax.ShapeDtypeStruct((total, width), BF16),
            jax.ShapeDtypeStruct((total, wide), BF16),
        ],
        cost_estimate=TINY,
        compiler_params=pltpu.CompilerParams(vmem_limit_bytes=28 * MIB),
        name="project_qkv",
    )(spot, x, vectors, bias, *outside(weight.arrays))


def make_merge_kernel(weight):
    count = len(weight.arrays)

    def kernel(spot_ref, a_ref, x_ref, c_ref, vec_ref, *refs):
        branch_ref, normed_ref, dmlp_ref, w, sem = refs[count:]

        @pl.when(pl.program_id(0) == 0)
        def _():
            run_copies(weight.copies(refs[:count], spot_ref, w, sem))

        vec = lambda row: vec_ref[row : row + 1]
        branch = dg(a_ref[...], w[...], NN) + vec(BIAS_OUT)
        branch_ref[...] = branch
        unit, _ = norm_parts(x_ref[...].astype(F32) + vec(SCALE1) * branch)
        normed_ref[...] = (unit * vec(GAIN2) + vec(SHIFT2)).astype(BF16)
        dmlp_ref[...] = (vec(SCALE2) * c_ref[...].astype(F32)).astype(BF16)

    return kernel


def merge_branch(spot, attended, x, cot, vectors, weight):
    total, width = x.shape
    size = 256
    full = lambda i, s: (0, 0)
    block = pl.BlockSpec((size, width), lambda i, s: (i, 0))
    return pl.pallas_call(
        make_merge_kernel(weight),
        grid_spec=pltpu.PrefetchScalarGridSpec(
            num_scalar_prefetch=1,
            grid=(total // size,),
            in_specs=[block, block, block, pl.BlockSpec((8, width), full)] + [ANY] * len(weight.arrays),
            out_specs=[block, block, block],
            scratch_shapes=[pltpu.VMEM((width, width), BF16), pltpu.SemaphoreType.DMA],
        ),
        out_shape=[
            jax.ShapeDtypeStruct((total, width), F32),
            jax.ShapeDtypeStruct((total, width), BF16),
            jax.ShapeDtypeStruct((total, width), BF16),
        ],
        cost_estimate=TINY,
        compiler_params=pltpu.CompilerParams(vmem_limit_bytes=28 * MIB),
        name="merge_branch",
    )(spot, attended, x, cot, vectors, *outside(weight.arrays))


def make_mlp_kernel(pieces, more, blocks, size, weight_up, weight_down):
    up_count = len(weight_up.arrays)
    down_count = len(weight_down.arrays)
    deep = 768
    part = deep // pieces

    def load(spot_ref, ups, downs, up, down, sems):
        tile = spot_ref[2]
        hidden = weight_up.columns // pieces
        jobs = []
        for piece in range(pieces):
            column = pl.multiple_of(piece * hidden + tile * part, 128)
            jobs += weight_up.copies(ups, spot_ref, up, sems.at[0], column, part, piece * part)
        if down_count == 1:
            start = pl.multiple_of(tile * deep, 16)
            jobs.append(pltpu.make_async_copy(downs[0].at[pl.ds(start, deep)], down, sems.at[1]))
        else:
            y, me = spot_ref[0], spot_ref[1]
            start = pl.multiple_of(tile * part, 16)
            to = pl.multiple_of(y * part, 16)
            jobs.append(pltpu.make_async_copy(downs[0].at[pl.ds(start, part)], down.at[pl.ds(to, part)], sems.at[1]))
            to = pl.multiple_of((1 - y) * part, 16)
            for number, ref in enumerate(downs[1:]):

                @pl.when((me ^ number) == tile)
                def _():
                    run_copies([pltpu.make_async_copy(ref, down.at[pl.ds(to, part)], sems.at[2])])

        run_copies(jobs)

    def kernel(spot_ref, n_ref, d_ref, bias_ref, *refs):
        if more:
            old_out_ref, old_back_ref = refs[:2]
            refs = refs[2:]
        ups = refs[:up_count]
        downs = refs[up_count : up_count + down_count]
        out_ref, back_ref, grad_ref, sum_ref, up, down, normeds, dmlps, activs, duppers, sems = refs[
            up_count + down_count :
        ]
        block = pl.program_id(0)
        rows = pl.ds(block * size, size)

        @pl.when(block == 0)
        def _():
            load(spot_ref, ups, downs, up, down, sems)

        @pl.when(block < blocks)
        def _():
            normed = n_ref[...]
            dmlp = d_ref[...]
            normeds[rows] = normed
            dmlps[rows] = dmlp
            bias = bias_ref[0]
            value, slope = gelu_parts(dg(normed, up[...], NN) + bias)
            activ = value.astype(BF16)
            activs[rows] = activ
            dupper = (dg(dmlp, down[...], NT) * slope).astype(BF16)
            duppers[rows] = dupper
            out = dg(activ, down[...], NN)
            back = dg(dupper, up[...], NT)
            if more:
                out += old_out_ref[...]
                back += old_back_ref[...]
            out_ref[...] = out
            back_ref[...] = back
            sums = jnp.sum(dupper.astype(F32), axis=0, keepdims=True)

            @pl.when(block == 0)
            def _():
                sum_ref[...] = sums

            @pl.when(block > 0)
            def _():
                sum_ref[...] += sums

        @pl.when(block == blocks)
        def _():
            dup = dg(normeds[...], duppers[...], TN).astype(BF16)
            ddown = dg(activs[...], dmlps[...], TN).astype(BF16)
            side = dup.shape[0] // pieces
            for piece in range(pieces):
                grad_ref[piece, :side] = dup[piece * side : (piece + 1) * side]
                grad_ref[piece, side:] = ddown[piece * part : (piece + 1) * part]

    return kernel


def mlp(spot, normed, dmlp, old, bias_up, weight_up, weight_down, pieces):
    total, width = normed.shape
    deep = 768
    size = 256
    blocks = total // size
    more = old is not None
    row = pl.BlockSpec((size, width), lambda r, s: (jnp.minimum(r, blocks - 1), 0))
    arrays = outside(weight_up.arrays + weight_down.arrays)
    stack = (width + deep) // pieces
    return pl.pallas_call(
        make_mlp_kernel(pieces, more, blocks, size, weight_up, weight_down),
        grid_spec=pltpu.PrefetchScalarGridSpec(
            num_scalar_prefetch=1,
            grid=(blocks + 1,),
            in_specs=[row, row, pl.BlockSpec((1, 1, deep), lambda r, s: (s[2], 0, 0))]
            + ([row, row] if more else [])
            + [ANY] * len(arrays),
            out_specs=[
                row,
                row,
                pl.BlockSpec((pieces, stack, width), lambda r, s: (0, 0, 0)),
                pl.BlockSpec((1, deep), lambda r, s: (0, 0)),
            ],
            scratch_shapes=[
                pltpu.VMEM((width, deep), BF16),
                pltpu.VMEM((deep, width), BF16),
                pltpu.VMEM((total, width), BF16),
                pltpu.VMEM((total, width), BF16),
                pltpu.VMEM((total, deep), BF16),
                pltpu.VMEM((total, deep), BF16),
                pltpu.SemaphoreType.DMA((3,)),
            ],
        ),
        out_shape=[
            jax.ShapeDtypeStruct((total, width), F32),
            jax.ShapeDtypeStruct((total, width), F32),
            jax.ShapeDtypeStruct((pieces, stack, width), BF16),
            jax.ShapeDtypeStruct((1, deep), F32),
        ],
        cost_estimate=TINY,
        compiler_params=pltpu.CompilerParams(vmem_limit_bytes=28 * MIB),
        name="mlp",
    )(spot, normed, dmlp, bias_up, *(old or ()), *arrays)


def make_branch_kernel(pieces, blocks, weight):
    count = len(weight.arrays)

    def kernel(spot_ref, d_ref, x_ref, b_ref, c_ref, a_ref, vec_ref, *refs):
        resid_ref, datt_ref, grad_ref, sum_ref, acc, w, sem = refs[count:]
        block = pl.program_id(0)

        @pl.when(block == 0)
        def _():
            run_copies(weight.copies(refs[:count], spot_ref, w, sem))

        vec = lambda row: vec_ref[row : row + 1]
        dnormed = d_ref[...]
        branch = b_ref[...]
        unit, scale = norm_parts(x_ref[...].astype(F32) + vec(SCALE1) * branch)
        dresid = c_ref[...].astype(F32) + norm_back(dnormed, unit, scale, vec(GAIN2))
        resid_ref[...] = dresid
        dbranch = (vec(SCALE1) * dresid).astype(BF16)
        datt_ref[...] = dg(dbranch, w[...], NT).astype(BF16)
        part = dg(a_ref[...], dbranch, TN)
        rows = [dnormed * unit, dnormed, dresid * branch, dbranch.astype(F32)]
        sums = jnp.concatenate(
            [jnp.sum(row, axis=0, keepdims=True) for row in rows] + [jnp.zeros((4, dnormed.shape[1]), F32)], axis=0
        )

        @pl.when(block == 0)
        def _():
            acc[...] = part
            sum_ref[...] = sums

        @pl.when(block > 0)
        def _():
            acc[...] += part
            sum_ref[...] += sums

        @pl.when(block == blocks - 1)
        def _():
            side = acc.shape[0] // pieces
            for piece in range(pieces):
                grad_ref[piece] = acc[piece * side : (piece + 1) * side].astype(BF16)

    return kernel


def branch_back(spot, back, x, branch, cot, attended, vectors, weight, pieces):
    total, width = x.shape
    size = 256
    blocks = total // size
    block = pl.BlockSpec((size, width), lambda i, s: (i, 0))
    full = lambda i, s: (0, 0)
    return pl.pallas_call(
        make_branch_kernel(pieces, blocks, weight),
        grid_spec=pltpu.PrefetchScalarGridSpec(
            num_scalar_prefetch=1,
            grid=(blocks,),
            in_specs=[block] * 5 + [pl.BlockSpec((8, width), full)] + [ANY] * len(weight.arrays),
            out_specs=[
                block,
                block,
                pl.BlockSpec((pieces, width // pieces, width), lambda i, s: (0, 0, 0)),
                pl.BlockSpec((8, width), full),
            ],
            scratch_shapes=[
                pltpu.VMEM((width, width), F32),
                pltpu.VMEM((width, width), BF16),
                pltpu.SemaphoreType.DMA,
            ],
        ),
        out_shape=[
            jax.ShapeDtypeStruct((total, width), F32),
            jax.ShapeDtypeStruct((total, width), BF16),
            jax.ShapeDtypeStruct((pieces, width // pieces, width), BF16),
            jax.ShapeDtypeStruct((8, width), F32),
        ],
        cost_estimate=TINY,
        compiler_params=pltpu.CompilerParams(vmem_limit_bytes=28 * MIB),
        name="branch_back",
    )(spot, back, x, branch, cot, attended, vectors, *outside(weight.arrays))


def make_weight_kernel(pieces, parts, blocks, paired):
    def kernel(spot_ref, n_ref, *refs):
        columns, refs = refs[:parts], refs[parts:]
        block = pl.program_id(0)
        rows = jnp.concatenate([ref[0] for ref in columns], axis=1)
        part = dg(n_ref[...], rows, TN)
        acc = refs[-1]

        @pl.when(block == 0)
        def _():
            acc[...] = part

        @pl.when(block > 0)
        def _():
            acc[...] += part

        @pl.when(block == blocks - 1)
        def _():
            side = acc.shape[0] // pieces
            if not paired:
                for piece in range(pieces):
                    refs[0][piece] = acc[piece * side : (piece + 1) * side].astype(BF16)
                return
            other_ref, send_ref, keep_ref = refs[:3]
            half = side // 2
            core = spot_ref[CORE]
            for out_ref, which in ((send_ref, 1 - core), (keep_ref, core)):
                for piece in range(pieces):
                    start = pl.multiple_of(which * half, 16)
                    out_ref[piece, half:] = other_ref[piece, pl.ds(start, half)]
                    start = pl.multiple_of(piece * side + which * half, 16)
                    out_ref[piece, :half] = acc[pl.ds(start, half)].astype(BF16)

    return kernel


def weight_unit(spot, normed, columns, pieces, other=None):
    total, width = normed.shape
    parts = len(columns)
    wide = columns[0][0].shape[2]
    size = 512
    unit = (pieces, width // pieces, parts * wide)
    paired = other is not None
    full = pl.BlockSpec(unit, lambda i, s: (0, 0, 0))
    outs = 2 if paired else 1
    result = pl.pallas_call(
        make_weight_kernel(pieces, parts, total // size, paired),
        grid_spec=pltpu.PrefetchScalarGridSpec(
            num_scalar_prefetch=1,
            grid=(total // size,),
            in_specs=[pl.BlockSpec((size, width), lambda i, s: (i, 0))]
            + [pl.BlockSpec((1, size, wide), lambda i, s, n=n: (n, i, 0)) for _, n in columns]
            + [full] * paired,
            out_specs=[full] * outs,
            scratch_shapes=[pltpu.VMEM((width, parts * wide), F32)],
        ),
        out_shape=[jax.ShapeDtypeStruct(unit, BF16)] * outs,
        cost_estimate=TINY,
        compiler_params=pltpu.CompilerParams(vmem_limit_bytes=28 * MIB),
        name="weight_unit",
    )(spot, normed, *[array for array, _ in columns], *([other] if paired else []))
    return result if paired else result[0]


def make_finish_kernel(parts, weight):
    count = len(weight.arrays)

    def kernel(spot_ref, *refs):
        grads = refs[:parts]
        x_ref, r_ref, b_ref, m_ref, c_ref, d_ref, vec_ref = refs[parts : parts + 7]
        out_ref, sum_ref, w_ref, sem = refs[parts + 7 + count :]
        block = pl.program_id(0)

        @pl.when(block == 0)
        def _():
            run_copies(weight.copies(refs[parts + 7 : parts + 7 + count], spot_ref, w_ref, sem))

        vec = lambda row: vec_ref[row : row + 1]
        width = x_ref.shape[1]
        dnormed = None
        for i in range(3):
            rows = jnp.concatenate([ref[i] for ref in grads], axis=1)
            part = dg(rows, w_ref[:, i * width : (i + 1) * width], NT)
            dnormed = part if dnormed is None else dnormed + part
        x = x_ref[...].astype(F32)
        unit, scale = norm_parts(x)
        dx = r_ref[...] + norm_back(dnormed, unit, scale, vec(GAIN1))
        high = dx.astype(BF16)
        branch_m = m_ref[...] + vec(BIAS_LAST)
        out = x + vec(SCALE1) * b_ref[...] + vec(SCALE2) * branch_m
        out_ref[:, :width] = out.astype(BF16)
        out_ref[:, width : 2 * width] = high
        out_ref[:, 2 * width :] = (dx - high.astype(F32)).astype(BF16)
        rows = [dnormed * unit, dnormed, c_ref[...].astype(F32) * branch_m, d_ref[...].astype(F32)]
        sums = jnp.concatenate(
            [jnp.sum(row, axis=0, keepdims=True) for row in rows] + [jnp.zeros((4, width), F32)], axis=0
        )

        @pl.when(block == 0)
        def _():
            sum_ref[...] = sums

        @pl.when(block > 0)
        def _():
            sum_ref[...] += sums

    return kernel


def finish(spot, grads, x, dresid, branch, branch_m, cot, dmlp, vectors, weight, first, blocks):
    width = x.shape[1]
    size = 256
    block = pl.BlockSpec((size, width), lambda i, s: (first + i, 0))
    full = lambda i, s: (0, 0)
    return pl.pallas_call(
        make_finish_kernel(len(grads), weight),
        grid_spec=pltpu.PrefetchScalarGridSpec(
            num_scalar_prefetch=1,
            grid=(blocks,),
            in_specs=[pl.BlockSpec((3, size, grad.shape[2]), lambda i, s: (0, first + i, 0)) for grad in grads]
            + [block] * 6
            + [pl.BlockSpec((8, width), full)]
            + [ANY] * len(weight.arrays),
            out_specs=[pl.BlockSpec((size, 3 * width), lambda i, s: (i, 0)), pl.BlockSpec((8, width), full)],
            scratch_shapes=[pltpu.VMEM((width, weight.columns), BF16), pltpu.SemaphoreType.DMA],
        ),
        out_shape=[
            jax.ShapeDtypeStruct((size * blocks, 3 * width), BF16),
            jax.ShapeDtypeStruct((8, width), F32),
        ],
        cost_estimate=TINY,
        compiler_params=pltpu.CompilerParams(vmem_limit_bytes=28 * MIB),
        name="finish",
    )(spot, *grads, x, dresid, branch, branch_m, cot, dmlp, vectors, *outside(weight.arrays))


def page_start(page):
    total = page.shape[1]
    lane = lax.broadcasted_iota(jnp.int32, (1, total), 1)
    found = (page == pltpu.roll(page, total - (LONGEST - 1), 1)) & (lane <= total - LONGEST)
    return jnp.min(jnp.where(found, lane, total), axis=1, keepdims=True)


def unrotate_kernel(page_ref, a_ref, b_ref, o_ref, g_ref):
    size, width = o_ref.shape
    total = 2 * a_ref.shape[0]
    row = lax.broadcasted_iota(jnp.int32, (size, total), 0) + pl.program_id(0) * size
    col = lax.broadcasted_iota(jnp.int32, (size, total), 1)
    source = row - page_start(page_ref[...])
    source = jnp.where(source < 0, source + total, source)
    turn = jnp.where(col == source, 1.0, 0.0).astype(BF16)
    value = dg(turn[:, : total // 2], a_ref[...], NN) + dg(turn[:, total // 2 :], b_ref[...], NN)
    o_ref[...] = value[:, :width].astype(BF16)
    g_ref[...] = value[:, width : 2 * width] + value[:, 2 * width :]


def unrotate(page_ids, upper, lower):
    half, width3 = upper.shape
    total = 2 * half
    width = width3 // 3
    size = 256
    block = pl.BlockSpec((size, width), lambda i: (i, 0))
    full = lambda i: (0, 0)
    return pl.pallas_call(
        unrotate_kernel,
        grid=(total // size,),
        in_specs=[pl.BlockSpec((1, total), full)] + [pl.BlockSpec((half, width3), full)] * 2,
        out_specs=[block, block],
        out_shape=[
            jax.ShapeDtypeStruct((total, width), BF16),
            jax.ShapeDtypeStruct((total, width), F32),
        ],
        cost_estimate=TINY,
        compiler_params=pltpu.CompilerParams(vmem_limit_bytes=28 * MIB),
        name="unrotate",
    )(page_ids, upper, lower)


QV_ROW, UP_ROW, TABLE_ROW = 8, 10, 16


def pack_kernel(*refs):
    out_ref = refs[-1]
    lanes = out_ref.shape[1]
    out_ref[...] = jnp.zeros_like(out_ref)
    at = 0
    for ref in refs[:-1]:
        if len(ref.shape) == 1:
            for n in range(ref.shape[0] // lanes):
                out_ref[at : at + 1, :] = ref[n * lanes : (n + 1) * lanes].astype(F32).reshape(1, lanes)
                at += 1
        else:
            rows, columns = ref.shape
            out_ref[TABLE_ROW : TABLE_ROW + rows, :columns] = ref[...].astype(F32)


def pack_small(smalls):
    lanes = smalls[0].shape[0]
    return pl.pallas_call(
        pack_kernel, out_shape=jax.ShapeDtypeStruct((32, lanes), F32), cost_estimate=TINY, name="pack_small"
    )(*smalls)


def unpack_kernel(spot_ref, mine_ref, far_ref, vec_ref, qkv_ref, up_ref, mix_ref):
    first = spot_ref[Y] == 0
    low = jnp.where(first, mine_ref[...], far_ref[...])
    high = jnp.where(first, far_ref[...], mine_ref[...])
    lanes = low.shape[1]
    vec_ref[:, :lanes] = low[:8]
    vec_ref[:, lanes:] = high[:8]
    qkv_ref[...] = jnp.zeros_like(qkv_ref)
    for n in range(2):
        row = QV_ROW + n
        qkv_ref[:, n * lanes : (n + 1) * lanes] = low[row : row + 1]
        qkv_ref[:, (4 + n) * lanes : (5 + n) * lanes] = high[row : row + 1]
    for n in range(up_ref.shape[0]):
        row = UP_ROW + n
        up_ref[n, :, :lanes] = low[row : row + 1]
        up_ref[n, :, lanes:] = high[row : row + 1]
    row = lax.broadcasted_iota(jnp.int32, (128, 128), 0)
    col = lax.broadcasted_iota(jnp.int32, (128, 128), 1)
    inner = (row < ROWS) & (col < ROWS)
    bucket = jnp.where(inner, jnp.clip(row - col + NB // 2, 0, NB - 1), NB)
    keep = jnp.where((row == col) & (row >= ROWS) & (row < 112), 1.0, 0.0)
    for head in range(mix_ref.shape[0]):
        mix = keep
        for number in range(NB):
            half = low if number < NB // 2 else high
            at = TABLE_ROW + number % (NB // 2)
            mix = jnp.where(bucket == number, half[at : at + 1, head : head + 1], mix)
        mix_ref[head] = mix.astype(BF16)


def unpack_small(spot, mine, far):
    lanes = mine.shape[1]
    width = 2 * lanes
    smem = pl.BlockSpec(memory_space=pltpu.SMEM)
    vmem = pl.BlockSpec(memory_space=pltpu.VMEM)
    return pl.pallas_call(
        unpack_kernel,
        in_specs=[smem, vmem, vmem],
        out_shape=[
            jax.ShapeDtypeStruct((8, width), F32),
            jax.ShapeDtypeStruct((1, 3 * width), F32),
            jax.ShapeDtypeStruct((4, 1, width), F32),
            jax.ShapeDtypeStruct((HEADS, 128, 128), BF16),
        ],
        cost_estimate=TINY,
        compiler_params=pltpu.CompilerParams(vmem_limit_bytes=28 * MIB),
        name="unpack_small",
    )(spot, mine, far)


def pack_grads_kernel(spot_ref, *refs):
    a_ref, b_ref, two_ref = refs[:3]
    qv_refs, up_refs, tab_refs = refs[3:6], refs[6:10], refs[10:13]
    send_ref, keep_ref, both = refs[13:]
    lanes = both.shape[2]
    both[...] = jnp.zeros_like(both)
    one = a_ref[...] + b_ref[...]
    two = two_ref[...]
    rows = [one[0:1], one[1:2], two[2:3], two[3:4], two[0:1], two[1:2], one[2:3], one[3:4]]
    for n, row in enumerate(rows):
        for half in range(2):
            both[half, n : n + 1] = row[:, half * lanes : (half + 1) * lanes]
    for half in range(2):
        row = jnp.concatenate([ref[half : half + 1] for ref in qv_refs], axis=1)
        for n in range(2):
            both[half, QV_ROW + n : QV_ROW + n + 1] = row[:, n * lanes : (n + 1) * lanes]
    zero = spot_ref[CORE] == 0
    for chunk in range(2):
        first, second = up_refs[2 * chunk][...], up_refs[2 * chunk + 1][...]
        tiles = (jnp.where(zero, second, first), jnp.where(zero, first, second))
        for n, tile in enumerate(tiles):
            row = UP_ROW + 2 * chunk + n
            for half in range(2):
                both[half, row : row + 1] = tile[:, half * lanes : (half + 1) * lanes]
    sums = []
    lane = lax.broadcasted_iota(jnp.int32, (ROWS, 128), 1)
    line = lax.broadcasted_iota(jnp.int32, (ROWS, 128), 0)
    for ref in tab_refs:
        for n in range(ref.shape[0]):
            value = jnp.where(lane < ROWS, ref[n], 0.0)
            for bit in range(6):
                value = jnp.where((line >> bit) & 1 == 1, pltpu.roll(value, 128 - (1 << bit), 1), value)
            sums.append(jnp.sum(value, axis=0, keepdims=True))
    sums.append(jnp.zeros((16 - len(sums), 128), F32))
    sums = jnp.concatenate(sums, axis=0)
    number = lax.broadcasted_iota(jnp.int32, (NB, 128), 0)
    shift = lax.broadcasted_iota(jnp.int32, (NB, 128), 1)
    shift = jnp.where(shift < ROWS, shift, shift - 128)
    pick = jnp.where(jnp.clip(NB // 2 - shift, 0, NB - 1) == number, 1.0, 0.0).astype(BF16)
    table = None
    for piece in split3(sums):
        part = dg(pick, piece, NT)
        table = part if table is None else table + part
    for half in range(2):
        both[half, TABLE_ROW : TABLE_ROW + NB // 2, :16] = table[half * (NB // 2) : (half + 1) * (NB // 2)]
    y = spot_ref[Y]
    send_ref[...] = both[1 - y]
    keep_ref[...] = both[y]


def pack_grads(spot, sums_a, sums_b, sums2, sums_qv, up_sums, tabs):
    lanes = sums2.shape[1] // 2
    smem = pl.BlockSpec(memory_space=pltpu.SMEM)
    vmem = pl.BlockSpec(memory_space=pltpu.VMEM)
    return pl.pallas_call(
        pack_grads_kernel,
        in_specs=[smem] + [vmem] * 13,
        out_shape=[jax.ShapeDtypeStruct((32, lanes), F32)] * 2,
        scratch_shapes=[pltpu.VMEM((2, 32, lanes), F32)],
        cost_estimate=TINY,
        compiler_params=pltpu.CompilerParams(vmem_limit_bytes=28 * MIB),
        name="pack_grads",
    )(spot, sums_a, sums_b, sums2, *sums_qv, *up_sums, *tabs)


def unpack_grads_kernel(in_ref, *refs):
    lanes = in_ref.shape[1]
    for n in range(8):
        refs[n][...] = in_ref[n : n + 1].reshape(lanes)
    for n in range(2):
        refs[8][n * lanes : (n + 1) * lanes] = in_ref[QV_ROW + n : QV_ROW + n + 1].reshape(lanes)
    refs[9][...] = in_ref[TABLE_ROW:, :HEADS]
    for n in range(4):
        refs[10][n * lanes : (n + 1) * lanes] = in_ref[UP_ROW + n : UP_ROW + n + 1].reshape(lanes)


def unpack_grads(value):
    lanes = value.shape[1]
    return pl.pallas_call(
        unpack_grads_kernel,
        out_shape=[jax.ShapeDtypeStruct((lanes,), F32)] * 8
        + [
            jax.ShapeDtypeStruct((2 * lanes,), F32),
            jax.ShapeDtypeStruct((NB // 2, HEADS), F32),
            jax.ShapeDtypeStruct((4 * lanes,), F32),
        ],
        cost_estimate=TINY,
        compiler_params=pltpu.CompilerParams(vmem_limit_bytes=28 * MIB),
        name="unpack_grads",
    )(value)


def place_mlp_kernel(spot_ref, *refs):
    up_ref, down_ref = refs[8:]
    side = refs[0].shape[0]
    hidden = up_ref.shape[1] // 2
    core, x = spot_ref[CORE], spot_ref[X]
    for chunk in range(2):
        for n in range(4):
            ref = refs[4 * chunk + n]
            start = pl.multiple_of((2 * chunk + (core ^ (n // 2))) * side, 128)

            @pl.when((x ^ (n % 2)) == 0)
            def _():
                value = ref[...].astype(F32)
                up_ref[:, pl.ds(start, side)] = value[:, :side]
                up_ref[:, pl.ds(start + hidden, side)] = value[:, side:]

            @pl.when((x ^ (n % 2)) == 1)
            def _():
                down_ref[pl.ds(start, side)] = ref[...].astype(F32)


def place_mlp(spot, quarters, hidden):
    side, width = quarters[0].shape
    smem = pl.BlockSpec(memory_space=pltpu.SMEM)
    vmem = pl.BlockSpec(memory_space=pltpu.VMEM)
    return pl.pallas_call(
        place_mlp_kernel,
        in_specs=[smem] + [vmem] * 8,
        out_shape=[
            jax.ShapeDtypeStruct((side, hidden), F32),
            jax.ShapeDtypeStruct((hidden // 2, width), F32),
        ],
        cost_estimate=TINY,
        compiler_params=pltpu.CompilerParams(vmem_limit_bytes=28 * MIB),
        name="place_mlp",
    )(spot, *quarters)


def place_qkv_kernel(spot_ref, *refs):
    qkv_ref, proj_ref = refs[8:]
    half, width = refs[0].shape
    third = width // 3
    core, x = spot_ref[CORE], spot_ref[X]

    def put(rows, value, number):
        for n in range(3):
            start = n * width + number * third
            qkv_ref[rows, start : start + third] = value[:, n * third : (n + 1) * third]

    for n in range(4):
        rows = pl.ds(pl.multiple_of((core ^ (n // 2)) * half, 8), half)
        early, late = refs[n], refs[4 + n]

        @pl.when((x ^ (n % 2)) == 0)
        def _():
            put(rows, early[...].astype(F32), 0)
            put(rows, late[...].astype(F32), 2)

        @pl.when((x ^ (n % 2)) == 1)
        def _():
            proj_ref[rows] = early[...].astype(F32)
            put(rows, late[...].astype(F32), 1)


def place_qkv(spot, early, late):
    half, width = early[0].shape
    smem = pl.BlockSpec(memory_space=pltpu.SMEM)
    vmem = pl.BlockSpec(memory_space=pltpu.VMEM)
    return pl.pallas_call(
        place_qkv_kernel,
        in_specs=[smem] + [vmem] * 8,
        out_shape=[
            jax.ShapeDtypeStruct((2 * half, 3 * width), F32),
            jax.ShapeDtypeStruct((2 * half, width), F32),
        ],
        cost_estimate=TINY,
        compiler_params=pltpu.CompilerParams(vmem_limit_bytes=28 * MIB),
        name="place_qkv",
    )(spot, *early, *late)


Y, ME, TILE, X, CORE, BITS = range(6)


def combine_kernel(spot_ref, *refs):
    total = None
    for ref in refs[:-1]:
        value = ref[...].astype(F32)
        value = value.reshape(value.shape[-2:])
        total = value if total is None else total + value
    refs[-1][...] = total.astype(BF16)


def combine(spot, terms, rows):
    width = terms[0][0].shape[-1]
    parts = 2 if rows % 32 == 0 else 1
    size = rows // parts
    specs = []
    for array, lead, start in terms:
        if array.ndim == 3:
            specs.append(
                pl.BlockSpec((1, size, width), lambda i, s, lead=lead, start=start: (lead(s), start(s) * parts + i, 0))
            )
        else:
            specs.append(pl.BlockSpec((size, width), lambda i, s, start=start: (start(s) * parts + i, 0)))
    return pl.pallas_call(
        combine_kernel,
        grid_spec=pltpu.PrefetchScalarGridSpec(
            num_scalar_prefetch=1,
            grid=(parts,),
            in_specs=specs,
            out_specs=pl.BlockSpec((size, width), lambda i, s: (i, 0)),
        ),
        out_shape=jax.ShapeDtypeStruct((rows, width), BF16),
        cost_estimate=TINY,
        compiler_params=pltpu.CompilerParams(vmem_limit_bytes=28 * MIB),
        name="combine",
    )(spot, *[array for array, _, _ in terms])


def narrow(terms, bit):
    return [(array, lead, lambda s, start=start: 2 * start(s) + bit(s)) for array, lead, start in terms]


def whole_term(array):
    return (array, None, lambda s: 0)


def join_kernel(spot_ref, a_ref, b_ref, o_ref):
    @pl.when(pl.program_id(0) == 0)
    def _():
        o_ref[...] = a_ref[...]

    @pl.when(pl.program_id(0) == 1)
    def _():
        o_ref[...] = b_ref[...]


def join(spot, bit, own, other):
    rows, width = own.shape
    full = pl.BlockSpec((rows, width), lambda i, s: (0, 0))
    return pl.pallas_call(
        join_kernel,
        grid_spec=pltpu.PrefetchScalarGridSpec(
            num_scalar_prefetch=1,
            grid=(2,),
            in_specs=[full, full],
            out_specs=pl.BlockSpec((rows, width), lambda i, s: (i ^ bit(s), 0)),
        ),
        out_shape=jax.ShapeDtypeStruct((2 * rows, width), BF16),
        cost_estimate=TINY,
        compiler_params=pltpu.CompilerParams(vmem_limit_bytes=28 * MIB),
        name="join",
    )(spot, own, other)


class Links:
    def __init__(self, dp, fsdp):
        self.dp, self.fsdp = dp, fsdp
        self.fast = fsdp == 2 and dp >= 4 and dp & (dp - 1) == 0
        here = lax.axis_index("dp")
        self.here = here
        self.core = here % 2
        self.x = (here // 2) % 2
        self.y = lax.axis_index("fsdp")
        self.masks = []
        mask = 4
        while mask < dp:
            self.masks.append(mask)
            mask *= 2

    def spot(self, tile):
        values = [self.y, 2 * self.core + self.x, tile, self.x, self.core]
        values += [(self.here // mask) % 2 for mask in self.masks]
        return jnp.stack(values).astype(jnp.int32)

    def swap(self, value, mask):
        return lax.ppermute(value, "dp", [(i, i ^ mask) for i in range(self.dp)])

    def swap_y(self, value):
        return lax.ppermute(value, "fsdp", [(0, 1), (1, 0)])

    def order(self, bit, own, other, axis=0):
        first = bit == 0
        return jnp.concatenate(
            [jnp.where(first, own, other), jnp.where(first, other, own)], axis=axis
        )

    def pieces(self, shards):
        rows = shards[0].shape[0]
        quarter = rows // 4
        start = (2 * self.core + self.x) * quarter
        return jnp.concatenate(
            [lax.dynamic_slice_in_dim(shard, start, quarter, 0) for shard in shards], axis=1
        )

    def weight_stages(self, shards):
        (first,) = yield [(self.pieces(shards), 0)]
        (second,) = yield [(first, 2)]
        rest = yield [(first, 1), (second, 1)]
        return (first, second) + tuple(rest)

    def small_gather(self, shard):
        (far,) = yield [(shard, 0)]
        return far

    def stages(self, spot, send, keep, halve):
        (near,) = yield [(send, 1)]
        keep = keep()
        half = keep.shape[1] // 2
        y, other_y = lambda s: s[Y], lambda s: 1 - s[Y]
        x, other_x = lambda s: s[X], lambda s: 1 - s[X]
        (far,) = yield [(combine(spot, [(keep, other_y, other_x), (near, other_y, other_x)], half), 0)]
        part = combine(spot, [(keep, y, other_x), (near, y, other_x), whole_term(far)], half)
        far = combine(spot, [(keep, other_y, x), (near, other_y, x)], half)
        got, far = yield [(part, 2), (far, 0)]
        terms = [(keep, y, x), (near, y, x), whole_term(far), whole_term(got)]
        masks = [(mask, lambda s, n=n: s[BITS + n]) for n, mask in enumerate(self.masks)]
        if halve:
            size = half
            for mask, bit in masks:
                size //= 2
                (got,) = yield [(combine(spot, narrow(terms, lambda s: 1 - bit(s)), size), mask)]
                terms = narrow(terms, bit) + [whole_term(got)]
            total = combine(spot, terms, size)
            for mask, bit in masks[::-1]:
                (got,) = yield [(total, mask)]
                total = join(spot, bit, total, got)
        else:
            total = combine(spot, terms, half)
            for mask, _ in masks:
                (got,) = yield [(total, mask)]
                total = combine(spot, [whole_term(total), whole_term(got)], half)
        (other,) = yield [(total, 2)]
        rest = yield [(total, 1), (other, 1)]
        return (total, other) + tuple(rest)

    def small_stages(self, send, keep):
        (got,) = yield [(send, 0)]
        total = keep + got
        mask = 1
        while mask < self.dp:
            (got,) = yield [(total, mask)]
            total = total + got
            mask *= 2
        return total

    def permute(self, value, mask):
        return self.swap(value, mask) if mask else self.swap_y(value)


class Flow:
    def __init__(self, links, run):
        self.links, self.run = links, run
        self.sends = next(run)
        self.got = None
        self.result = None

    def take(self, got):
        try:
            self.sends = self.run.send(got)
        except StopIteration as stop:
            self.result = stop.value

    def leave(self, values):
        self.got = [self.links.permute(value, mask) for value, (_, mask) in zip(values, self.sends)]


def advance(anchor, flows):
    flows = [flow for flow in flows if flow.result is None]
    if not flows:
        return anchor
    anchor, gots = lax.optimization_barrier((anchor, [flow.got for flow in flows]))
    for flow, got in zip(flows, gots):
        if got is not None:
            flow.take(got)
    going = [flow for flow in flows if flow.result is None]
    values = [[value for value, _ in flow.sends] for flow in going]
    anchor, values = lax.optimization_barrier((anchor, values))
    for flow, mine in zip(going, values):
        flow.leave(mine)
    return anchor


def make_body(dp, fsdp):
    def body(
        patches,
        page_ids,
        patch_rows,
        live_len,
        norm1_gain,
        norm1_bias,
        w_qkv,
        bias_qv,
        rel_table,
        w_proj,
        bias_proj,
        scale_attn,
        norm2_gain,
        norm2_bias,
        w_up,
        bias_up,
        w_down,
        bias_down,
        scale_mlp,
        cotangent,
    ):
        links = Links(dp, fsdp)
        smalls = (
            norm1_gain,
            norm1_bias,
            scale_attn,
            bias_proj,
            norm2_gain,
            norm2_bias,
            scale_mlp,
            bias_down,
            bias_qv,
            rel_table,
            bias_up,
        )
        total, width = patches.shape[1:]
        fast = links.fast
        pieces = 2 if fast else 1
        hidden = w_up.shape[1]
        spots = []
        for number in range(4):
            chunk, second = divmod(number, 2)
            core = links.core if fast else 0
            spots.append(links.spot(2 * chunk + (core if second else 1 - core)))
        spots = lax.optimization_barrier(spots)
        spot = spots[0]

        x, cot = patches[0], cotangent[0]
        if fast:
            loads = [
                Flow(links, links.weight_stages(group)) for group in ([w_qkv], [w_proj, w_up], [w_down])
            ]
            x = advance(x, loads[:1])
            mine = pack_small(smalls[:9] + smalls[10:] + smalls[9:10])
            far = Flow(links, links.small_gather(mine))
            x = advance(x, [far])
            x, cot, query_side, key_side = rotate(page_ids, patch_rows, live_len, x, cot)
            x = advance(x, [far] + loads[:2])
            vectors, bias_all, bias_hidden, mix = unpack_small(spot, mine, far.result)
            x, mix = advance((x, mix), loads[:2])
            x, mix = advance((x, mix), loads[:1] + loads[2:])
            weight_qkv = Weight((w_qkv,) + loads[0].result, width, 3 * width)
        else:
            x, cot, query_side, key_side = rotate(page_ids, patch_rows, live_len, x, cot)
            mine = jnp.concatenate([small.reshape(-1) for small in smalls])
            packed = lax.all_gather(mine, "fsdp", axis=0, tiled=False)
            share = width // fsdp
            vectors = packed[:, : 8 * share].reshape(fsdp, 8, share).transpose(1, 0, 2).reshape(8, width).astype(F32)
            at = 8 * share
            whole = []
            for small in smalls[8:]:
                piece = packed[:, at : at + small.size]
                whole.append(piece.reshape((small.shape[0] * fsdp,) + small.shape[1:]).astype(F32))
                at += small.size
            bias_qv_f, table, bias_hidden = whole
            bias_all = jnp.concatenate([bias_qv_f[:width], jnp.zeros((width,), F32), bias_qv_f[width:]])[None]
            bias_hidden = bias_hidden.reshape(pieces, -1, 768 // pieces).transpose(1, 0, 2).reshape(-1, 1, 768)
            mix = bias_mix(table)
            weight_qkv, weight_proj, weight_up, weight_down = [
                Weight([lax.all_gather(shard, "fsdp", axis=0, tiled=True)], shard.shape[0] * fsdp, shard.shape[1])
                for shard in (w_qkv, w_proj, w_up, w_down)
            ]
        x, mix = lax.optimization_barrier((x, mix))
        normed1, qkv = project_qkv(spot, x, vectors, bias_all, weight_qkv)
        if fast:
            qkv = advance(qkv, loads)
        attended, lse = attention(qkv, query_side, key_side, mix)
        if fast:
            attended = advance(attended, loads)
            weight_proj = Weight((w_proj,) + loads[1].result, width, width)
            weight_up = Weight((w_up,) + loads[1].result, width, hidden, width)
        branch, normed2, dmlp = merge_branch(spot, attended, x, cot, vectors, weight_proj)
        if fast:
            normed2 = advance(normed2, loads)
            weight_down = Weight((w_down,) + loads[2].result, hidden, width)

        flows = []

        def launch(run):
            if links.fast:
                flows.append(Flow(links, run))

        def go(anchor):
            return advance(anchor, flows) if links.fast else anchor

        old = None
        mlp_grads, up_sums = [], []
        for number in range(4):
            chunk, second = divmod(number, 2)
            out, back, grad, sums = mlp(
                spots[number], normed2, dmlp, old, bias_hidden, weight_up, weight_down, pieces
            )
            mlp_grads.append(grad)
            up_sums.append(sums)
            if not second:
                launch(links.stages(spot, grad, lambda chunk=chunk: mlp_grads[2 * chunk + 1], True))
            old = go((out, back))
        branch_m, back = old
        dresid, datt, proj_grad, sums2 = branch_back(
            spot, back, x, branch, cot, attended, vectors, weight_proj, pieces
        )
        datt = go(datt)

        d_parts, sums_qv, tabs, units = [], [], [], []
        for number in range(3):
            d_part, sums, tab = attention_back(
                qkv, datt, attended, lse, query_side, key_side, mix, 2 * number, 2
            )
            sums_qv.append(sums)
            tabs.append(tab)
            datt, d_part = go((datt, d_part))
            d_parts.append(d_part)
            columns = [(d_part, 0), (d_part, 1), (d_part, 2)]
            other = (proj_grad, None, units[-1] if units else None)[number] if fast else None
            unit = weight_unit(spot, normed1, columns, pieces, other)
            if number == 0:
                if fast:
                    launch(links.stages(spot, unit[0], lambda unit=unit: unit[1], False))
                else:
                    first_unit = unit
                datt = go(datt)
            elif number == 1:
                units.append(unit)
                datt, units[0] = go((datt, units[0]))
            elif fast:
                launch(links.stages(spot, unit[0], lambda unit=unit: unit[1], False))
                d_parts[2] = go(d_parts[2])
            else:
                units.append(unit)

        halves = []
        for first in range(0, total // 256, 2):
            half, sums = finish(
                spot, d_parts, x, dresid, branch, branch_m, cot, dmlp, vectors, weight_qkv, first, 2
            )
            half, dmlp = go((half, dmlp))
            halves.append((half, sums))
        (upper, sums_a), (lower, sums_b) = halves
        if fast:
            send, keep = pack_grads(spot, sums_a, sums_b, sums2, sums_qv, up_sums, tabs)
            launch(links.small_stages(send, keep))
            upper = advance(upper, flows[-1:])
            layer_out, grad_patches = unrotate(page_ids, upper, lower)
            layer_out, grad_patches = go((layer_out, grad_patches))
            out_w_up, out_w_down = place_mlp(spot, flows[0].result + flows[1].result, hidden)
            out_w_up, out_w_down = go((out_w_up, out_w_down))
            while any(flow.result is None for flow in flows):
                layer_out = go(layer_out)
            out_w_qkv, out_w_proj = place_qkv(spot, flows[2].result, flows[3].result)
            g = unpack_grads(flows[4].result)
            small_outs = [g[0], g[1], g[8], g[9], g[3], g[2], g[4], g[5], g[10], g[7], g[6]]
        else:
            layer_out, grad_patches = unrotate(page_ids, upper, lower)
            for values in (mlp_grads, up_sums):
                values[:] = [values[1], values[0], values[3], values[2]]
            sums1 = sums_a + sums_b
            sums_qv = jnp.concatenate(sums_qv, axis=1)
            small_grads = [
                sums1[0],
                sums1[1],
                jnp.concatenate([sums_qv[0], sums_qv[1]]),
                table_gradient(jnp.concatenate(tabs, axis=0)),
                sums2[3],
                sums2[2],
                sums2[0],
                sums2[1],
                jnp.concatenate(up_sums, axis=0).reshape(-1),
                sums1[3],
                sums1[2],
            ]
            flat = jnp.concatenate([grad.reshape(fsdp, -1) for grad in small_grads], axis=1)
            summed = lax.psum_scatter(lax.psum(flat, "dp"), "fsdp", scatter_dimension=0, tiled=True)[0]
            small_outs = []
            at = 0
            for grad in small_grads:
                size = grad.size // fsdp
                small_outs.append(summed[at : at + size].reshape((grad.shape[0] // fsdp,) + grad.shape[1:]))
                at += size
            stacks = jnp.concatenate(mlp_grads, axis=1).astype(F32).reshape(-1, 2, width, width)
            qkv_units = [unit[0].astype(F32) for unit in (first_unit, units[0], units[1])]
            third = width // 3
            fulls = (
                jnp.concatenate([unit[:, n * third : (n + 1) * third] for n in range(3) for unit in qkv_units], axis=1),
                proj_grad[0].astype(F32),
                jnp.concatenate([stacks[t, 0] for t in range(stacks.shape[0])], axis=1),
                stacks[:, 1].reshape(-1, width),
            )
            out_w_qkv, out_w_proj, out_w_up, out_w_down = [
                lax.psum(lax.psum_scatter(grad, "fsdp", scatter_dimension=0, tiled=True), "dp") for grad in fulls
            ]
        return (
            layer_out[None],
            grad_patches[None],
            small_outs[0],
            small_outs[1],
            out_w_qkv,
            small_outs[2],
            small_outs[3],
            out_w_proj,
            small_outs[4],
            small_outs[5],
            small_outs[6],
            small_outs[7],
            out_w_up,
            small_outs[8],
            out_w_down,
            small_outs[9],
            small_outs[10],
        )

    return body


def solution(mesh):
    rows = P(("dp", "fsdp"), None, None)
    ids = P(("dp", "fsdp"), None)
    vector = P("fsdp")
    matrix = P("fsdp", None)
    in_specs = (
        rows,
        ids,
        ids,
        ids,
        vector,
        vector,
        matrix,
        vector,
        matrix,
        matrix,
        vector,
        vector,
        vector,
        vector,
        matrix,
        vector,
        matrix,
        vector,
        vector,
        rows,
    )
    out_specs = (
        rows,
        rows,
        vector,
        vector,
        matrix,
        vector,
        matrix,
        matrix,
        vector,
        vector,
        vector,
        vector,
        matrix,
        vector,
        matrix,
        vector,
        vector,
    )
    body = make_body(mesh.shape["dp"], mesh.shape["fsdp"])
    return jax.shard_map(body, mesh=mesh, in_specs=in_specs, out_specs=out_specs, check_vma=False)
```

```python
import jax
import jax.numpy as jnp
from jax import lax
from jax.experimental import pallas as pl
from jax.experimental.pallas import tpu as pltpu
from jax.sharding import PartitionSpec as P

HEADS = 12
HEAD = 64
NB = 32
ROWS = 64
PAGES = 16
LONGEST = 512
DEAD_SPAN = 256
EPSILON = 1e-06
BIG = 2.0**100
Y, ME, X, CORE, TILES, BITS = 0, 1, 2, 3, 4, 8
NN = (((1,), (0,)), ((), ()))
NT = (((1,), (1,)), ((), ()))
TN = (((0,), (0,)), ((), ()))
TINY = pl.CostEstimate(flops=1000, transcendentals=0, bytes_accessed=1000)
MIB = 2**20
F32 = jnp.float32
BF16 = jnp.bfloat16


def dg(left, right, dims):
    return lax.dot_general(left, right, dims, preferred_element_type=F32)


def split3(value):
    high = value.astype(BF16)
    rest = value - high.astype(F32)
    mid = rest.astype(BF16)
    low = (rest - mid.astype(F32)).astype(BF16)
    return high, mid, low


def mix_kernel(table_ref, mix_ref):
    head = pl.program_id(0)
    row = lax.broadcasted_iota(jnp.int32, (128, 128), 0)
    col = lax.broadcasted_iota(jnp.int32, (128, 128), 1)
    bucket = jnp.clip(row - col + NB // 2, 0, NB - 1)
    bias = jnp.zeros((128, 128), F32)
    for number in range(NB):
        bias = jnp.where(bucket == number, table_ref[number, head], bias)
    keep = (row == col) & (row >= ROWS) & (row < 112)
    mix = jnp.where((row < ROWS) & (col < ROWS), bias, jnp.where(keep, 1.0, 0.0))
    mix_ref[0] = mix.astype(BF16)


def bias_mix(table):
    return pl.pallas_call(
        mix_kernel,
        grid=(HEADS,),
        in_specs=[pl.BlockSpec(memory_space=pltpu.SMEM)],
        out_specs=pl.BlockSpec((1, 128, 128), lambda head: (head, 0, 0)),
        out_shape=jax.ShapeDtypeStruct((HEADS, 128, 128), BF16),
        compiler_params=pltpu.CompilerParams(vmem_limit_bytes=16 * MIB),
        name="bias_mix",
    )(table.astype(F32))


def attention_kernel(q_ref, k_ref, v_ref, f_ref, g_ref, m_ref, o_ref, l_ref):
    pair = pl.program_id(1)
    size = q_ref.shape[0]
    q = q_ref[...].astype(F32) * HEAD**-0.5
    v = v_ref[...]
    lane = lax.broadcasted_iota(jnp.int32, (size, 128), 1)
    keys = jnp.concatenate([k_ref[...], g_ref[...]], axis=1)
    f = f_ref[...]

    @pl.when(pair == 0)
    def _():
        l_ref[...] = jnp.zeros_like(l_ref)

    lse = l_ref[...]
    out = None
    mines = [(lane // HEAD) == h for h in range(2)]
    scores = []
    for h in range(2):
        extra = dg(f, m_ref[h], NN).astype(BF16)
        queries = jnp.concatenate([jnp.where(mines[h], q, 0.0).astype(BF16), extra], axis=1)
        scores.append(dg(queries, keys, NT))
    for h, score in enumerate(scores):
        top = jnp.max(score, axis=1, keepdims=True)
        expo = jnp.exp(score - top)
        denom = jnp.sum(expo, axis=1, keepdims=True)
        part = dg(expo.astype(BF16), jnp.where(mines[h], v, jnp.zeros_like(v)), NN) / denom
        out = part if out is None else out + part
        lse = jnp.where(lane == 2 * pair + h, top + jnp.log(denom), lse)
    o_ref[...] = out.astype(BF16)
    l_ref[...] = lse


def attention(qkv, query_side, key_side, mix):
    total, width3 = qkv.shape
    width = width3 // 3
    pairs = width // 128
    size = LONGEST
    blocks = total // size
    area = blocks * size * size
    return pl.pallas_call(
        attention_kernel,
        grid=(blocks, pairs),
        in_specs=[
            pl.BlockSpec((size, 128), lambda b, h: (b, h)),
            pl.BlockSpec((size, 128), lambda b, h: (b, pairs + h)),
            pl.BlockSpec((size, 128), lambda b, h: (b, 2 * pairs + h)),
            pl.BlockSpec((size, 128), lambda b, h: (b, 0)),
            pl.BlockSpec((size, 128), lambda b, h: (b, 0)),
            pl.BlockSpec((2, 128, 128), lambda b, h: (h, 0, 0)),
        ],
        out_specs=[
            pl.BlockSpec((size, 128), lambda b, h: (b, h)),
            pl.BlockSpec((size, 128), lambda b, h: (b, 0)),
        ],
        out_shape=[
            jax.ShapeDtypeStruct((total, width), BF16),
            jax.ShapeDtypeStruct((total, 128), F32),
        ],
        cost_estimate=TINY,
        compiler_params=pltpu.CompilerParams(vmem_limit_bytes=16 * MIB),
        name="attention",
    )(qkv, qkv, qkv, query_side, key_side, mix)


def make_attention_back_kernel(first):
    def kernel(q_ref, k_ref, v_ref, da_ref, o_ref, l_ref, f_ref, g_ref, m_ref, d_ref, sum_ref, tab_ref):
        pair = pl.program_id(0) + first
        block = pl.program_id(1)
        size = q_ref.shape[0]
        lane = lax.broadcasted_iota(jnp.int32, (size, 128), 1)
        q = q_ref[...].astype(F32) * HEAD**-0.5
        v = v_ref[...]
        da = da_ref[...]
        product = da.astype(F32) * o_ref[...].astype(F32)
        f = f_ref[...]
        keys = jnp.concatenate([k_ref[...], g_ref[...]], axis=1)
        values = jnp.concatenate([v, jnp.where(lane < 3, 1.0, 0.0).astype(BF16)], axis=1)
        lse_all = l_ref[...]
        dq, dk, dv = None, None, None
        saved = []
        for h in range(2):
            mine = (lane // HEAD) == h
            extra = dg(f, m_ref[h], NN)
            lse = jnp.sum(jnp.where(lane == 2 * pair + h, lse_all, 0.0), axis=1, keepdims=True)
            for place, piece in enumerate(split3(-lse)):
                extra = jnp.where(lane == 112 + place, piece.astype(F32), extra)
            qm = jnp.where(mine, q, 0.0).astype(BF16)
            queries = jnp.concatenate([qm, extra.astype(BF16)], axis=1)
            delta = jnp.sum(jnp.where(mine, product, 0.0), axis=1, keepdims=True)
            columns = jnp.zeros((size, 128), F32)
            for place, piece in enumerate(split3(-delta)):
                columns = jnp.where(lane == place, piece.astype(F32), columns)
            dam = jnp.where(mine, da, jnp.zeros_like(da))
            dax = jnp.concatenate([dam, columns.astype(BF16)], axis=1)
            saved.append((mine, qm, dam, dg(keys, queries, NT), dg(values, dax, NT)))
        for h in range(2):
            mine, qm, dam, score, dprob = saved[h]
            prob = jnp.exp(score)
            dscore = (prob * dprob).astype(BF16)
            dvh = dg(prob.astype(BF16), dam, NN)
            dkh = dg(dscore, qm, NN)
            both = dg(dscore, keys, TN)
            dv = dvh if dv is None else dv + dvh
            dk = dkh if dk is None else dk + dkh
            dq = both[:, :128] if dq is None else jnp.where(mine, both[:, :128], dq)
            rows = both[:, 128:]
            rows_high = rows.astype(BF16)
            rows_low = (rows - rows_high.astype(F32)).astype(BF16)
            grid = dg(f, jnp.concatenate([rows_high, rows_low], axis=1), TN)
            grid = grid[:ROWS, :128] + grid[:ROWS, 128:]

            @pl.when(block == 0)
            def _():
                tab_ref[h] = grid

            @pl.when(block > 0)
            def _():
                tab_ref[h] += grid

        dq = (dq * HEAD**-0.5).astype(BF16)
        dk = dk.astype(BF16)
        dv = dv.astype(BF16)
        d_ref[0] = dq
        d_ref[1] = dk
        d_ref[2] = dv
        sums = jnp.concatenate(
            [
                jnp.sum(dq.astype(F32), axis=0, keepdims=True),
                jnp.sum(dv.astype(F32), axis=0, keepdims=True),
                jnp.zeros((6, 128), F32),
            ],
            axis=0,
        )

        @pl.when(block == 0)
        def _():
            sum_ref[...] = sums

        @pl.when(block > 0)
        def _():
            sum_ref[...] += sums

    return kernel


def attention_back(qkv, d_attended, attended, lse, query_side, key_side, mix, first, count):
    total, width3 = qkv.shape
    pairs = width3 // 3 // 128
    size = LONGEST
    blocks = total // size
    wide = lambda h, b: (b, first + h)
    side = lambda h, b: (b, 0)
    return pl.pallas_call(
        make_attention_back_kernel(first),
        grid=(count, blocks),
        in_specs=[
            pl.BlockSpec((size, 128), wide),
            pl.BlockSpec((size, 128), lambda h, b: (b, pairs + first + h)),
            pl.BlockSpec((size, 128), lambda h, b: (b, 2 * pairs + first + h)),
            pl.BlockSpec((size, 128), wide),
            pl.BlockSpec((size, 128), wide),
            pl.BlockSpec((size, 128), side),
            pl.BlockSpec((size, 128), side),
            pl.BlockSpec((size, 128), side),
            pl.BlockSpec((2, 128, 128), lambda h, b: (first + h, 0, 0)),
        ],
        out_specs=[
            pl.BlockSpec((3, size, 128), lambda h, b: (0, b, h)),
            pl.BlockSpec((8, 128), lambda h, b: (0, h)),
            pl.BlockSpec((2, ROWS, 128), lambda h, b: (h, 0, 0)),
        ],
        out_shape=[
            jax.ShapeDtypeStruct((3, total, 128 * count), BF16),
            jax.ShapeDtypeStruct((8, 128 * count), F32),
            jax.ShapeDtypeStruct((2 * count, ROWS, 128), F32),
        ],
        cost_estimate=TINY,
        compiler_params=pltpu.CompilerParams(vmem_limit_bytes=16 * MIB),
        name="attention_back",
    )(qkv, qkv, qkv, d_attended, attended, lse, query_side, key_side, mix)


def table_gradient(tab):
    row = jnp.arange(ROWS, dtype=jnp.int32)
    bucket = jnp.clip(row[:, None] - row[None, :] + NB // 2, 0, NB - 1)
    onehot = (bucket[:, :, None] == jnp.arange(NB, dtype=jnp.int32)).astype(F32)
    return jnp.einsum("hij,ijb->bh", tab[:, :, :ROWS], onehot, precision=lax.Precision.HIGHEST)


def turn_rows(page, size, total):
    row = lax.broadcasted_iota(jnp.int32, (size, total), 0) + pl.program_id(0) * size
    col = lax.broadcasted_iota(jnp.int32, (size, total), 1)
    source = row + page_start(page)
    source = jnp.where(source >= total, source - total, source)
    return jnp.where(col == source, 1.0, 0.0).astype(BF16)


def rotate_kernel(page_ref, x_ref, xo_ref):
    turn = turn_rows(page_ref[...], xo_ref.shape[0], x_ref.shape[0])
    xo_ref[...] = dg(turn, x_ref[...], NN).astype(BF16)


def rotate_ids_kernel(page_ref, place_ref, live_ref, x_ref, xo_ref, f_ref, g_ref):
    total = x_ref.shape[0]
    page = page_ref[...]
    place = place_ref[...]
    turn = turn_rows(page, xo_ref.shape[0], total)
    xo_ref[...] = dg(turn, x_ref[...], NN).astype(BF16)
    line = lax.broadcasted_iota(jnp.int32, (128, total), 0)
    pos = lax.broadcasted_iota(jnp.int32, (128, total), 1)
    span = pos & (DEAD_SPAN - 1)
    high = 80 + (span >> 4)
    low = 96 + (span & 15)
    early = pos < total - DEAD_SPAN
    in_high = (line >= 80) & (line < 96)
    in_low = (line >= 96) & (line < 112)
    select = (
        (line == place)
        | (line == 64 + page)
        | (line == high)
        | (line == low)
        | (early & (in_high | in_low))
    )
    dead = pos >= live_ref[0, 0]
    other_page = jnp.logical_not(dead) & (line >= 64) & (line < 80) & (line != 64 + page)
    other_place = dead & ((in_high & (line != high)) | (in_low & (line != low)))
    one = (line == place) | ((line >= 112) & (line < 115))
    query_side = jnp.where(select, 1.0, 0.0).astype(BF16)
    key_side = jnp.where(other_page | other_place, -BIG, jnp.where(one, 1.0, 0.0)).astype(BF16)
    f_ref[...] = dg(turn, query_side, NT).astype(BF16)
    g_ref[...] = dg(turn, key_side, NT).astype(BF16)


def rotate(page_ids, values):
    total, width = values.shape
    size = 256
    full = lambda i: (0, 0)
    return pl.pallas_call(
        rotate_kernel,
        grid=(total // size,),
        in_specs=[pl.BlockSpec((1, total), full), pl.BlockSpec((total, width), full)],
        out_specs=pl.BlockSpec((size, width), lambda i: (i, 0)),
        out_shape=jax.ShapeDtypeStruct((total, width), BF16),
        cost_estimate=TINY,
        compiler_params=pltpu.CompilerParams(vmem_limit_bytes=16 * MIB),
        name="rotate",
    )(page_ids, values)


def rotate_ids(page_ids, patch_rows, live_len, values):
    total, width = values.shape
    size = 256
    full = lambda i: (0, 0)
    rows = lambda i: (i, 0)
    return pl.pallas_call(
        rotate_ids_kernel,
        grid=(total // size,),
        in_specs=[
            pl.BlockSpec((1, total), full),
            pl.BlockSpec((1, total), full),
            pl.BlockSpec(memory_space=pltpu.SMEM),
            pl.BlockSpec((total, width), full),
        ],
        out_specs=[
            pl.BlockSpec((size, width), rows),
            pl.BlockSpec((size, 128), rows),
            pl.BlockSpec((size, 128), rows),
        ],
        out_shape=[
            jax.ShapeDtypeStruct((total, width), BF16),
            jax.ShapeDtypeStruct((total, 128), BF16),
            jax.ShapeDtypeStruct((total, 128), BF16),
        ],
        cost_estimate=TINY,
        compiler_params=pltpu.CompilerParams(vmem_limit_bytes=16 * MIB),
        name="rotate_ids",
    )(page_ids, patch_rows, live_len, values)


def norm_parts(values):
    center = values - jnp.mean(values, axis=-1, keepdims=True)
    spread = jnp.mean(center * center, axis=-1, keepdims=True)
    scale = lax.rsqrt(spread + EPSILON)
    return center * scale, scale


def norm_back(grad, unit, scale, gain):
    inner = grad * gain
    mean = jnp.mean(inner, axis=-1, keepdims=True)
    mixed = jnp.mean(inner * unit, axis=-1, keepdims=True)
    return scale * (inner - mean - unit * mixed)


def gelu_parts(upper):
    c = 0.7978845608028654
    square = upper * upper
    wave = jnp.tanh(upper * (c + (c * 0.044715) * square))
    half = 0.5 + 0.5 * wave
    value = upper * half
    slope = half + (value * (1.0 - wave)) * (c + (3 * c * 0.044715) * square)
    return value, slope


GAIN1, SHIFT1, SCALE1, BIAS_OUT, GAIN2, SHIFT2, SCALE2, BIAS_LAST = range(8)


ANY = pl.BlockSpec(memory_space=pl.ANY)


class Weight:
    def __init__(self, arrays, rows, columns, at=0):
        self.arrays, self.rows, self.columns, self.at = tuple(arrays), rows, columns, at

    def copies(self, refs, spot_ref, target, sem, column=0, columns=None, to=0):
        columns = columns or self.columns
        lanes = pl.ds(to, columns)
        if len(refs) == 1:
            return [pltpu.make_async_copy(refs[0].at[:, pl.ds(column, columns)], target.at[:, lanes], sem)]
        y, me = spot_ref[0], spot_ref[1]
        size = self.rows // 2
        quarter = size // 4
        start = pl.multiple_of(y * size, 16)
        jobs = [
            pltpu.make_async_copy(refs[0].at[:, pl.ds(column, columns)], target.at[pl.ds(start, size), lanes], sem)
        ]
        for number, ref in enumerate(refs[1:]):
            start = pl.multiple_of((1 - y) * size + (me ^ number) * quarter, 16)
            jobs.append(
                pltpu.make_async_copy(
                    ref.at[:, pl.ds(self.at + column, columns)], target.at[pl.ds(start, quarter), lanes], sem
                )
            )
        return jobs


def outside(arrays):
    return [pltpu.with_memory_space_constraint(array, pltpu.HBM) for array in arrays]


def run_copies(jobs):
    for job in jobs:
        job.start()
    for job in jobs:
        job.wait()


def make_qkv_kernel(weight):
    count = len(weight.arrays)

    def kernel(spot_ref, x_ref, vec_ref, bias_ref, *refs):
        normed_ref, qkv_ref, w, sem = refs[count:]

        @pl.when(pl.program_id(0) == 0)
        def _():
            run_copies(weight.copies(refs[:count], spot_ref, w, sem))

        unit, _ = norm_parts(x_ref[...].astype(F32))
        normed = (unit * vec_ref[GAIN1 : GAIN1 + 1] + vec_ref[SHIFT1 : SHIFT1 + 1]).astype(BF16)
        normed_ref[...] = normed
        qkv_ref[...] = (dg(normed, w[...], NN) + bias_ref[...]).astype(BF16)

    return kernel


def project_qkv(spot, x, vectors, bias, weight):
    total, width = x.shape
    size = 256
    wide = weight.columns
    full = lambda i, s: (0, 0)
    rows = lambda i, s: (i, 0)
    return pl.pallas_call(
        make_qkv_kernel(weight),
        grid_spec=pltpu.PrefetchScalarGridSpec(
            num_scalar_prefetch=1,
            grid=(total // size,),
            in_specs=[
                pl.BlockSpec((size, width), rows),
                pl.BlockSpec((8, width), full),
                pl.BlockSpec((1, wide), full),
            ]
            + [ANY] * len(weight.arrays),
            out_specs=[pl.BlockSpec((size, width), rows), pl.BlockSpec((size, wide), rows)],
            scratch_shapes=[pltpu.VMEM((width, wide), BF16), pltpu.SemaphoreType.DMA],
        ),
        out_shape=[
            jax.ShapeDtypeStruct((total, width), BF16),
            jax.ShapeDtypeStruct((total, wide), BF16),
        ],
        cost_estimate=TINY,
        compiler_params=pltpu.CompilerParams(vmem_limit_bytes=16 * MIB),
        name="project_qkv",
    )(spot, x, vectors, bias, *outside(weight.arrays))


def make_merge_kernel(weight):
    count = len(weight.arrays)

    def kernel(spot_ref, a_ref, x_ref, c_ref, vec_ref, *refs):
        branch_ref, normed_ref, dmlp_ref, w, sem = refs[count:]

        @pl.when(pl.program_id(0) == 0)
        def _():
            run_copies(weight.copies(refs[:count], spot_ref, w, sem))

        vec = lambda row: vec_ref[row : row + 1]
        branch = dg(a_ref[...], w[...], NN) + vec(BIAS_OUT)
        branch_ref[...] = branch
        unit, _ = norm_parts(x_ref[...].astype(F32) + vec(SCALE1) * branch)
        normed_ref[...] = (unit * vec(GAIN2) + vec(SHIFT2)).astype(BF16)
        dmlp_ref[...] = (vec(SCALE2) * c_ref[...].astype(F32)).astype(BF16)

    return kernel


def merge_branch(spot, attended, x, cot, vectors, weight):
    total, width = x.shape
    size = 256
    full = lambda i, s: (0, 0)
    block = pl.BlockSpec((size, width), lambda i, s: (i, 0))
    return pl.pallas_call(
        make_merge_kernel(weight),
        grid_spec=pltpu.PrefetchScalarGridSpec(
            num_scalar_prefetch=1,
            grid=(total // size,),
            in_specs=[block, block, block, pl.BlockSpec((8, width), full)] + [ANY] * len(weight.arrays),
            out_specs=[block, block, block],
            scratch_shapes=[pltpu.VMEM((width, width), BF16), pltpu.SemaphoreType.DMA],
        ),
        out_shape=[
            jax.ShapeDtypeStruct((total, width), F32),
            jax.ShapeDtypeStruct((total, width), BF16),
            jax.ShapeDtypeStruct((total, width), BF16),
        ],
        cost_estimate=TINY,
        compiler_params=pltpu.CompilerParams(vmem_limit_bytes=16 * MIB),
        name="merge_branch",
    )(spot, attended, x, cot, vectors, *outside(weight.arrays))


def make_mlp_kernel(which, pieces, more, blocks, size, weight_up, weight_down):
    up_count = len(weight_up.arrays)
    down_count = len(weight_down.arrays)
    deep = 768
    part = deep // pieces

    def load(spot_ref, ups, downs, up, down, sems):
        tile = spot_ref[TILES + which]
        hidden = weight_up.columns // pieces
        jobs = []
        for piece in range(pieces):
            column = pl.multiple_of(piece * hidden + tile * part, 128)
            jobs += weight_up.copies(ups, spot_ref, up, sems.at[0], column, part, piece * part)
        if down_count == 1:
            start = pl.multiple_of(tile * deep, 16)
            jobs.append(pltpu.make_async_copy(downs[0].at[pl.ds(start, deep)], down, sems.at[1]))
        else:
            y, me = spot_ref[0], spot_ref[1]
            start = pl.multiple_of(tile * part, 16)
            to = pl.multiple_of(y * part, 16)
            jobs.append(pltpu.make_async_copy(downs[0].at[pl.ds(start, part)], down.at[pl.ds(to, part)], sems.at[1]))
            to = pl.multiple_of((1 - y) * part, 16)
            for number, ref in enumerate(downs[1:]):

                @pl.when((me ^ number) == tile)
                def _():
                    run_copies([pltpu.make_async_copy(ref, down.at[pl.ds(to, part)], sems.at[2])])

        run_copies(jobs)

    def kernel(spot_ref, n_ref, d_ref, bias_ref, *refs):
        if more:
            old_out_ref, old_back_ref = refs[:2]
            refs = refs[2:]
        ups = refs[:up_count]
        downs = refs[up_count : up_count + down_count]
        out_ref, back_ref, grad_ref, sum_ref, up, down, normeds, dmlps, activs, duppers, sems = refs[
            up_count + down_count :
        ]
        block = pl.program_id(0)
        rows = pl.ds(block * size, size)

        @pl.when(block == 0)
        def _():
            load(spot_ref, ups, downs, up, down, sems)

        @pl.when(block < blocks)
        def _():
            normed = n_ref[...]
            dmlp = d_ref[...]
            normeds[rows] = normed
            dmlps[rows] = dmlp
            bias = bias_ref[0]
            value, slope = gelu_parts(dg(normed, up[...], NN) + bias)
            activ = value.astype(BF16)
            activs[rows] = activ
            dupper = (dg(dmlp, down[...], NT) * slope).astype(BF16)
            duppers[rows] = dupper
            out = dg(activ, down[...], NN)
            back = dg(dupper, up[...], NT)
            if more:
                out += old_out_ref[...]
                back += old_back_ref[...]
            out_ref[...] = out
            back_ref[...] = back
            sums = jnp.sum(dupper.astype(F32), axis=0, keepdims=True)

            @pl.when(block == 0)
            def _():
                sum_ref[...] = sums

            @pl.when(block > 0)
            def _():
                sum_ref[...] += sums

        @pl.when(block == blocks)
        def _():
            side = normeds.shape[1] // pieces

            @pl.loop(0, 3)
            def _(n):
                lanes = pl.ds(pl.multiple_of(n * 256, 256), 256)
                dup = dg(normeds[...], duppers[:, lanes], TN).astype(BF16)
                ddown = dg(activs[...], dmlps[:, lanes], TN).astype(BF16)
                for piece in range(pieces):
                    grad_ref[piece, :side, lanes] = dup[piece * side : (piece + 1) * side]
                    grad_ref[piece, side:, lanes] = ddown[piece * part : (piece + 1) * part]

    return kernel


def mlp(spot, which, normed, dmlp, old, bias_up, weight_up, weight_down, pieces):
    total, width = normed.shape
    deep = 768
    size = 256
    blocks = total // size
    more = old is not None
    row = pl.BlockSpec((size, width), lambda r, s: (jnp.minimum(r, blocks - 1), 0))
    arrays = outside(weight_up.arrays + weight_down.arrays)
    stack = (width + deep) // pieces
    return pl.pallas_call(
        make_mlp_kernel(which, pieces, more, blocks, size, weight_up, weight_down),
        grid_spec=pltpu.PrefetchScalarGridSpec(
            num_scalar_prefetch=1,
            grid=(blocks + 1,),
            in_specs=[row, row, pl.BlockSpec((1, 1, deep), lambda r, s: (s[TILES + which], 0, 0))]
            + ([row, row] if more else [])
            + [ANY] * len(arrays),
            out_specs=[
                row,
                row,
                pl.BlockSpec((pieces, stack, width), lambda r, s: (0, 0, 0)),
                pl.BlockSpec((1, deep), lambda r, s: (0, 0)),
            ],
            scratch_shapes=[
                pltpu.VMEM((width, deep), BF16),
                pltpu.VMEM((deep, width), BF16),
                pltpu.VMEM((total, width), BF16),
                pltpu.VMEM((total, width), BF16),
                pltpu.VMEM((total, deep), BF16),
                pltpu.VMEM((total, deep), BF16),
                pltpu.SemaphoreType.DMA((3,)),
            ],
        ),
        out_shape=[
            jax.ShapeDtypeStruct((total, width), F32),
            jax.ShapeDtypeStruct((total, width), F32),
            jax.ShapeDtypeStruct((pieces, stack, width), BF16),
            jax.ShapeDtypeStruct((1, deep), F32),
        ],
        cost_estimate=TINY,
        compiler_params=pltpu.CompilerParams(vmem_limit_bytes=16 * MIB),
        name="mlp",
    )(spot, normed, dmlp, bias_up, *(old or ()), *arrays)


def make_branch_kernel(pieces, blocks, weight):
    count = len(weight.arrays)

    def kernel(spot_ref, d_ref, x_ref, b_ref, c_ref, a_ref, vec_ref, *refs):
        resid_ref, datt_ref, grad_ref, sum_ref, acc, w, sem = refs[count:]
        block = pl.program_id(0)

        @pl.when(block == 0)
        def _():
            run_copies(weight.copies(refs[:count], spot_ref, w, sem))

        vec = lambda row: vec_ref[row : row + 1]
        dnormed = d_ref[...]
        branch = b_ref[...]
        unit, scale = norm_parts(x_ref[...].astype(F32) + vec(SCALE1) * branch)
        dresid = c_ref[...].astype(F32) + norm_back(dnormed, unit, scale, vec(GAIN2))
        resid_ref[...] = dresid
        dbranch = (vec(SCALE1) * dresid).astype(BF16)
        datt_ref[...] = dg(dbranch, w[...], NT).astype(BF16)
        part = dg(a_ref[...], dbranch, TN)
        rows = [dnormed * unit, dnormed, dresid * branch, dbranch.astype(F32)]
        sums = jnp.concatenate(
            [jnp.sum(row, axis=0, keepdims=True) for row in rows] + [jnp.zeros((4, dnormed.shape[1]), F32)], axis=0
        )

        @pl.when(block == 0)
        def _():
            acc[...] = part
            sum_ref[...] = sums

        @pl.when(block > 0)
        def _():
            acc[...] += part
            sum_ref[...] += sums

        @pl.when(block == blocks - 1)
        def _():
            side = acc.shape[0] // pieces
            for piece in range(pieces):
                grad_ref[piece] = acc[piece * side : (piece + 1) * side].astype(BF16)

    return kernel


def branch_back(spot, back, x, branch, cot, attended, vectors, weight, pieces):
    total, width = x.shape
    size = 256
    blocks = total // size
    block = pl.BlockSpec((size, width), lambda i, s: (i, 0))
    full = lambda i, s: (0, 0)
    return pl.pallas_call(
        make_branch_kernel(pieces, blocks, weight),
        grid_spec=pltpu.PrefetchScalarGridSpec(
            num_scalar_prefetch=1,
            grid=(blocks,),
            in_specs=[block] * 5 + [pl.BlockSpec((8, width), full)] + [ANY] * len(weight.arrays),
            out_specs=[
                block,
                block,
                pl.BlockSpec((pieces, width // pieces, width), lambda i, s: (0, 0, 0)),
                pl.BlockSpec((8, width), full),
            ],
            scratch_shapes=[
                pltpu.VMEM((width, width), F32),
                pltpu.VMEM((width, width), BF16),
                pltpu.SemaphoreType.DMA,
            ],
        ),
        out_shape=[
            jax.ShapeDtypeStruct((total, width), F32),
            jax.ShapeDtypeStruct((total, width), BF16),
            jax.ShapeDtypeStruct((pieces, width // pieces, width), BF16),
            jax.ShapeDtypeStruct((8, width), F32),
        ],
        cost_estimate=TINY,
        compiler_params=pltpu.CompilerParams(vmem_limit_bytes=16 * MIB),
        name="branch_back",
    )(spot, back, x, branch, cot, attended, vectors, *outside(weight.arrays))


def make_weight_kernel(pieces, parts, blocks, paired):
    def kernel(spot_ref, n_ref, *refs):
        columns, refs = refs[:parts], refs[parts:]
        block = pl.program_id(0)
        rows = jnp.concatenate([ref[0] for ref in columns], axis=1)
        part = dg(n_ref[...], rows, TN)
        acc = refs[-1]

        @pl.when(block == 0)
        def _():
            acc[...] = part

        @pl.when(block > 0)
        def _():
            acc[...] += part

        @pl.when(block == blocks - 1)
        def _():
            side = acc.shape[0] // pieces
            if not paired:
                for piece in range(pieces):
                    refs[0][piece] = acc[piece * side : (piece + 1) * side].astype(BF16)
                return
            other_ref, send_ref, keep_ref = refs[:3]
            half = side // 2
            core = spot_ref[CORE]
            for out_ref, which in ((send_ref, 1 - core), (keep_ref, core)):
                for piece in range(pieces):
                    start = pl.multiple_of(which * half, 16)
                    out_ref[piece, half:] = other_ref[piece, pl.ds(start, half)]
                    start = pl.multiple_of(piece * side + which * half, 16)
                    out_ref[piece, :half] = acc[pl.ds(start, half)].astype(BF16)

    return kernel


def weight_unit(spot, normed, columns, pieces, other=None):
    total, width = normed.shape
    parts = len(columns)
    wide = columns[0][0].shape[2]
    size = 512
    unit = (pieces, width // pieces, parts * wide)
    paired = other is not None
    full = pl.BlockSpec(unit, lambda i, s: (0, 0, 0))
    outs = 2 if paired else 1
    result = pl.pallas_call(
        make_weight_kernel(pieces, parts, total // size, paired),
        grid_spec=pltpu.PrefetchScalarGridSpec(
            num_scalar_prefetch=1,
            grid=(total // size,),
            in_specs=[pl.BlockSpec((size, width), lambda i, s: (i, 0))]
            + [pl.BlockSpec((1, size, wide), lambda i, s, n=n: (n, i, 0)) for _, n in columns]
            + [full] * paired,
            out_specs=[full] * outs,
            scratch_shapes=[pltpu.VMEM((width, parts * wide), F32)],
        ),
        out_shape=[jax.ShapeDtypeStruct(unit, BF16)] * outs,
        cost_estimate=TINY,
        compiler_params=pltpu.CompilerParams(vmem_limit_bytes=16 * MIB),
        name="weight_unit",
    )(spot, normed, *[array for array, _ in columns], *([other] if paired else []))
    return result if paired else result[0]


def make_finish_kernel(parts, weight):
    count = len(weight.arrays)

    def kernel(spot_ref, *refs):
        grads = refs[:parts]
        x_ref, r_ref, b_ref, m_ref, c_ref, d_ref, vec_ref = refs[parts : parts + 7]
        out_ref, sum_ref, w_ref, sem = refs[parts + 7 + count :]
        block = pl.program_id(0)

        @pl.when(block == 0)
        def _():
            run_copies(weight.copies(refs[parts + 7 : parts + 7 + count], spot_ref, w_ref, sem))

        vec = lambda row: vec_ref[row : row + 1]
        width = x_ref.shape[1]
        dnormed = None
        for i in range(3):
            rows = jnp.concatenate([ref[i] for ref in grads], axis=1)
            part = dg(rows, w_ref[:, i * width : (i + 1) * width], NT)
            dnormed = part if dnormed is None else dnormed + part
        x = x_ref[...].astype(F32)
        unit, scale = norm_parts(x)
        dx = r_ref[...] + norm_back(dnormed, unit, scale, vec(GAIN1))
        high = dx.astype(BF16)
        branch_m = m_ref[...] + vec(BIAS_LAST)
        out = x + vec(SCALE1) * b_ref[...] + vec(SCALE2) * branch_m
        out_ref[:, :width] = out.astype(BF16)
        out_ref[:, width : 2 * width] = high
        out_ref[:, 2 * width :] = (dx - high.astype(F32)).astype(BF16)
        rows = [dnormed * unit, dnormed, c_ref[...].astype(F32) * branch_m, d_ref[...].astype(F32)]
        sums = jnp.concatenate(
            [jnp.sum(row, axis=0, keepdims=True) for row in rows] + [jnp.zeros((4, width), F32)], axis=0
        )

        @pl.when(block == 0)
        def _():
            sum_ref[...] = sums

        @pl.when(block > 0)
        def _():
            sum_ref[...] += sums

    return kernel


def finish(spot, grads, x, dresid, branch, branch_m, cot, dmlp, vectors, weight, first, blocks):
    width = x.shape[1]
    size = 256
    block = pl.BlockSpec((size, width), lambda i, s: (first + i, 0))
    full = lambda i, s: (0, 0)
    return pl.pallas_call(
        make_finish_kernel(len(grads), weight),
        grid_spec=pltpu.PrefetchScalarGridSpec(
            num_scalar_prefetch=1,
            grid=(blocks,),
            in_specs=[pl.BlockSpec((3, size, grad.shape[2]), lambda i, s: (0, first + i, 0)) for grad in grads]
            + [block] * 6
            + [pl.BlockSpec((8, width), full)]
            + [ANY] * len(weight.arrays),
            out_specs=[pl.BlockSpec((size, 3 * width), lambda i, s: (i, 0)), pl.BlockSpec((8, width), full)],
            scratch_shapes=[pltpu.VMEM((width, weight.columns), BF16), pltpu.SemaphoreType.DMA],
        ),
        out_shape=[
            jax.ShapeDtypeStruct((size * blocks, 3 * width), BF16),
            jax.ShapeDtypeStruct((8, width), F32),
        ],
        cost_estimate=TINY,
        compiler_params=pltpu.CompilerParams(vmem_limit_bytes=16 * MIB),
        name="finish",
    )(spot, *grads, x, dresid, branch, branch_m, cot, dmlp, vectors, *outside(weight.arrays))


def page_start(page):
    total = page.shape[1]
    lane = lax.broadcasted_iota(jnp.int32, (1, total), 1)
    found = (page == pltpu.roll(page, total - (LONGEST - 1), 1)) & (lane <= total - LONGEST)
    return jnp.min(jnp.where(found, lane, total), axis=1, keepdims=True)


def unrotate_kernel(page_ref, a_ref, b_ref, o_ref, g_ref):
    size, width = o_ref.shape
    total = 2 * a_ref.shape[0]
    row = lax.broadcasted_iota(jnp.int32, (size, total), 0) + pl.program_id(0) * size
    col = lax.broadcasted_iota(jnp.int32, (size, total), 1)
    source = row - page_start(page_ref[...])
    source = jnp.where(source < 0, source + total, source)
    turn = jnp.where(col == source, 1.0, 0.0).astype(BF16)
    value = dg(turn[:, : total // 2], a_ref[...], NN) + dg(turn[:, total // 2 :], b_ref[...], NN)
    o_ref[...] = value[:, :width].astype(BF16)
    g_ref[...] = value[:, width : 2 * width] + value[:, 2 * width :]


def unrotate(page_ids, upper, lower):
    half, width3 = upper.shape
    total = 2 * half
    width = width3 // 3
    size = 256
    block = pl.BlockSpec((size, width), lambda i: (i, 0))
    full = lambda i: (0, 0)
    return pl.pallas_call(
        unrotate_kernel,
        grid=(total // size,),
        in_specs=[pl.BlockSpec((1, total), full)] + [pl.BlockSpec((half, width3), full)] * 2,
        out_specs=[block, block],
        out_shape=[
            jax.ShapeDtypeStruct((total, width), BF16),
            jax.ShapeDtypeStruct((total, width), F32),
        ],
        cost_estimate=TINY,
        compiler_params=pltpu.CompilerParams(vmem_limit_bytes=16 * MIB),
        name="unrotate",
    )(page_ids, upper, lower)


QV_ROW, UP_ROW, TABLE_ROW = 8, 10, 16


def pack_kernel(*refs):
    out_ref = refs[-1]
    lanes = out_ref.shape[1]
    out_ref[...] = jnp.zeros_like(out_ref)
    at = 0
    for ref in refs[:-1]:
        if len(ref.shape) == 1:
            for n in range(ref.shape[0] // lanes):
                out_ref[at : at + 1, :] = ref[n * lanes : (n + 1) * lanes].astype(F32).reshape(1, lanes)
                at += 1
        else:
            rows, columns = ref.shape
            out_ref[TABLE_ROW : TABLE_ROW + rows, :columns] = ref[...].astype(F32)


def pack_small(smalls):
    lanes = smalls[0].shape[0]
    return pl.pallas_call(
        pack_kernel, out_shape=jax.ShapeDtypeStruct((32, lanes), F32), cost_estimate=TINY, name="pack_small"
    )(*smalls)


def unpack_kernel(spot_ref, mine_ref, far_ref, vec_ref, qkv_ref, up_ref, mix_ref):
    first = spot_ref[Y] == 0
    low = jnp.where(first, mine_ref[...], far_ref[...])
    high = jnp.where(first, far_ref[...], mine_ref[...])
    lanes = low.shape[1]
    vec_ref[:, :lanes] = low[:8]
    vec_ref[:, lanes:] = high[:8]
    qkv_ref[...] = jnp.zeros_like(qkv_ref)
    for n in range(2):
        row = QV_ROW + n
        qkv_ref[:, n * lanes : (n + 1) * lanes] = low[row : row + 1]
        qkv_ref[:, (4 + n) * lanes : (5 + n) * lanes] = high[row : row + 1]
    for n in range(up_ref.shape[0]):
        row = UP_ROW + n
        up_ref[n, :, :lanes] = low[row : row + 1]
        up_ref[n, :, lanes:] = high[row : row + 1]
    row = lax.broadcasted_iota(jnp.int32, (128, 128), 0)
    col = lax.broadcasted_iota(jnp.int32, (128, 128), 1)
    inner = (row < ROWS) & (col < ROWS)
    bucket = jnp.where(inner, jnp.clip(row - col + NB // 2, 0, NB - 1), NB)
    keep = jnp.where((row == col) & (row >= ROWS) & (row < 112), 1.0, 0.0)
    for head in range(mix_ref.shape[0]):
        mix = keep
        for number in range(NB):
            half = low if number < NB // 2 else high
            at = TABLE_ROW + number % (NB // 2)
            mix = jnp.where(bucket == number, half[at : at + 1, head : head + 1], mix)
        mix_ref[head] = mix.astype(BF16)


def unpack_small(spot, mine, far):
    lanes = mine.shape[1]
    width = 2 * lanes
    smem = pl.BlockSpec(memory_space=pltpu.SMEM)
    vmem = pl.BlockSpec(memory_space=pltpu.VMEM)
    return pl.pallas_call(
        unpack_kernel,
        in_specs=[smem, vmem, vmem],
        out_shape=[
            jax.ShapeDtypeStruct((8, width), F32),
            jax.ShapeDtypeStruct((1, 3 * width), F32),
            jax.ShapeDtypeStruct((4, 1, width), F32),
            jax.ShapeDtypeStruct((HEADS, 128, 128), BF16),
        ],
        cost_estimate=TINY,
        compiler_params=pltpu.CompilerParams(vmem_limit_bytes=16 * MIB),
        name="unpack_small",
    )(spot, mine, far)


def pack_grads_kernel(spot_ref, *refs):
    a_ref, b_ref, two_ref = refs[:3]
    qv_refs, up_refs, tab_refs = refs[3:6], refs[6:10], refs[10:13]
    send_ref, keep_ref, both = refs[13:]
    lanes = both.shape[2]
    both[...] = jnp.zeros_like(both)
    one = a_ref[...] + b_ref[...]
    two = two_ref[...]
    rows = [one[0:1], one[1:2], two[2:3], two[3:4], two[0:1], two[1:2], one[2:3], one[3:4]]
    for n, row in enumerate(rows):
        for half in range(2):
            both[half, n : n + 1] = row[:, half * lanes : (half + 1) * lanes]
    for half in range(2):
        row = jnp.concatenate([ref[half : half + 1] for ref in qv_refs], axis=1)
        for n in range(2):
            both[half, QV_ROW + n : QV_ROW + n + 1] = row[:, n * lanes : (n + 1) * lanes]
    zero = spot_ref[CORE] == 0
    for chunk in range(2):
        first, second = up_refs[2 * chunk][...], up_refs[2 * chunk + 1][...]
        tiles = (jnp.where(zero, second, first), jnp.where(zero, first, second))
        for n, tile in enumerate(tiles):
            row = UP_ROW + 2 * chunk + n
            for half in range(2):
                both[half, row : row + 1] = tile[:, half * lanes : (half + 1) * lanes]
    sums = []
    lane = lax.broadcasted_iota(jnp.int32, (ROWS, 128), 1)
    line = lax.broadcasted_iota(jnp.int32, (ROWS, 128), 0)
    for ref in tab_refs:
        for n in range(ref.shape[0]):
            value = jnp.where(lane < ROWS, ref[n], 0.0)
            for bit in range(6):
                value = jnp.where((line >> bit) & 1 == 1, pltpu.roll(value, 128 - (1 << bit), 1), value)
            sums.append(jnp.sum(value, axis=0, keepdims=True))
    sums.append(jnp.zeros((16 - len(sums), 128), F32))
    sums = jnp.concatenate(sums, axis=0)
    number = lax.broadcasted_iota(jnp.int32, (NB, 128), 0)
    shift = lax.broadcasted_iota(jnp.int32, (NB, 128), 1)
    shift = jnp.where(shift < ROWS, shift, shift - 128)
    pick = jnp.where(jnp.clip(NB // 2 - shift, 0, NB - 1) == number, 1.0, 0.0).astype(BF16)
    table = None
    for piece in split3(sums):
        part = dg(pick, piece, NT)
        table = part if table is None else table + part
    for half in range(2):
        both[half, TABLE_ROW : TABLE_ROW + NB // 2, :16] = table[half * (NB // 2) : (half + 1) * (NB // 2)]
    y = spot_ref[Y]
    send_ref[...] = both[1 - y]
    keep_ref[...] = both[y]


def pack_grads(spot, sums_a, sums_b, sums2, sums_qv, up_sums, tabs):
    lanes = sums2.shape[1] // 2
    smem = pl.BlockSpec(memory_space=pltpu.SMEM)
    vmem = pl.BlockSpec(memory_space=pltpu.VMEM)
    return pl.pallas_call(
        pack_grads_kernel,
        in_specs=[smem] + [vmem] * 13,
        out_shape=[jax.ShapeDtypeStruct((32, lanes), F32)] * 2,
        scratch_shapes=[pltpu.VMEM((2, 32, lanes), F32)],
        cost_estimate=TINY,
        compiler_params=pltpu.CompilerParams(vmem_limit_bytes=16 * MIB),
        name="pack_grads",
    )(spot, sums_a, sums_b, sums2, *sums_qv, *up_sums, *tabs)


def unpack_grads_kernel(in_ref, *refs):
    lanes = in_ref.shape[1]
    for n in range(8):
        refs[n][...] = in_ref[n : n + 1].reshape(lanes)
    for n in range(2):
        refs[8][n * lanes : (n + 1) * lanes] = in_ref[QV_ROW + n : QV_ROW + n + 1].reshape(lanes)
    refs[9][...] = in_ref[TABLE_ROW:, :HEADS]
    for n in range(4):
        refs[10][n * lanes : (n + 1) * lanes] = in_ref[UP_ROW + n : UP_ROW + n + 1].reshape(lanes)


def unpack_grads(value):
    lanes = value.shape[1]
    return pl.pallas_call(
        unpack_grads_kernel,
        out_shape=[jax.ShapeDtypeStruct((lanes,), F32)] * 8
        + [
            jax.ShapeDtypeStruct((2 * lanes,), F32),
            jax.ShapeDtypeStruct((NB // 2, HEADS), F32),
            jax.ShapeDtypeStruct((4 * lanes,), F32),
        ],
        cost_estimate=TINY,
        compiler_params=pltpu.CompilerParams(vmem_limit_bytes=16 * MIB),
        name="unpack_grads",
    )(value)


def place_mlp_kernel(spot_ref, *refs):
    up_ref, down_ref = refs[8:]
    side = refs[0].shape[0]
    hidden = up_ref.shape[1] // 2
    core, x = spot_ref[CORE], spot_ref[X]
    for chunk in range(2):
        for n in range(4):
            ref = refs[4 * chunk + n]
            start = pl.multiple_of((2 * chunk + (core ^ (n // 2))) * side, 128)

            @pl.when((x ^ (n % 2)) == 0)
            def _():
                value = ref[...].astype(F32)
                up_ref[:, pl.ds(start, side)] = value[:, :side]
                up_ref[:, pl.ds(start + hidden, side)] = value[:, side:]

            @pl.when((x ^ (n % 2)) == 1)
            def _():
                down_ref[pl.ds(start, side)] = ref[...].astype(F32)


def place_mlp(spot, quarters, hidden):
    side, width = quarters[0].shape
    smem = pl.BlockSpec(memory_space=pltpu.SMEM)
    vmem = pl.BlockSpec(memory_space=pltpu.VMEM)
    return pl.pallas_call(
        place_mlp_kernel,
        in_specs=[smem] + [vmem] * 8,
        out_shape=[
            jax.ShapeDtypeStruct((side, hidden), F32),
            jax.ShapeDtypeStruct((hidden // 2, width), F32),
        ],
        cost_estimate=TINY,
        compiler_params=pltpu.CompilerParams(vmem_limit_bytes=16 * MIB),
        name="place_mlp",
    )(spot, *quarters)


def place_qkv_kernel(spot_ref, *refs):
    qkv_ref, proj_ref = refs[8:]
    half, width = refs[0].shape
    third = width // 3
    core, x = spot_ref[CORE], spot_ref[X]

    def put(rows, value, number):
        for n in range(3):
            start = n * width + number * third
            qkv_ref[rows, start : start + third] = value[:, n * third : (n + 1) * third]

    for n in range(4):
        rows = pl.ds(pl.multiple_of((core ^ (n // 2)) * half, 8), half)
        early, late = refs[n], refs[4 + n]

        @pl.when((x ^ (n % 2)) == 0)
        def _():
            put(rows, early[...].astype(F32), 0)
            put(rows, late[...].astype(F32), 2)

        @pl.when((x ^ (n % 2)) == 1)
        def _():
            proj_ref[rows] = early[...].astype(F32)
            put(rows, late[...].astype(F32), 1)


def place_qkv(spot, early, late):
    half, width = early[0].shape
    smem = pl.BlockSpec(memory_space=pltpu.SMEM)
    vmem = pl.BlockSpec(memory_space=pltpu.VMEM)
    return pl.pallas_call(
        place_qkv_kernel,
        in_specs=[smem] + [vmem] * 8,
        out_shape=[
            jax.ShapeDtypeStruct((2 * half, 3 * width), F32),
            jax.ShapeDtypeStruct((2 * half, width), F32),
        ],
        cost_estimate=TINY,
        compiler_params=pltpu.CompilerParams(vmem_limit_bytes=16 * MIB),
        name="place_qkv",
    )(spot, *early, *late)


def combine_kernel(spot_ref, *refs):
    total = None
    for ref in refs[:-1]:
        value = ref[...].astype(F32)
        value = value.reshape(value.shape[-2:])
        total = value if total is None else total + value
    refs[-1][...] = total.astype(BF16)


def combine(spot, terms, rows):
    width = terms[0][0].shape[-1]
    parts = 2 if rows % 32 == 0 else 1
    size = rows // parts
    specs = []
    for array, lead, start in terms:
        if array.ndim == 3:
            specs.append(
                pl.BlockSpec((1, size, width), lambda i, s, lead=lead, start=start: (lead(s), start(s) * parts + i, 0))
            )
        else:
            specs.append(pl.BlockSpec((size, width), lambda i, s, start=start: (start(s) * parts + i, 0)))
    return pl.pallas_call(
        combine_kernel,
        grid_spec=pltpu.PrefetchScalarGridSpec(
            num_scalar_prefetch=1,
            grid=(parts,),
            in_specs=specs,
            out_specs=pl.BlockSpec((size, width), lambda i, s: (i, 0)),
        ),
        out_shape=jax.ShapeDtypeStruct((rows, width), BF16),
        cost_estimate=TINY,
        compiler_params=pltpu.CompilerParams(vmem_limit_bytes=16 * MIB),
        name="combine",
    )(spot, *[array for array, _, _ in terms])


def narrow(terms, bit):
    return [(array, lead, lambda s, start=start: 2 * start(s) + bit(s)) for array, lead, start in terms]


def whole_term(array):
    return (array, None, lambda s: 0)


def join_kernel(spot_ref, a_ref, b_ref, o_ref):
    @pl.when(pl.program_id(0) == 0)
    def _():
        o_ref[...] = a_ref[...]

    @pl.when(pl.program_id(0) == 1)
    def _():
        o_ref[...] = b_ref[...]


def join(spot, bit, own, other):
    rows, width = own.shape
    full = pl.BlockSpec((rows, width), lambda i, s: (0, 0))
    return pl.pallas_call(
        join_kernel,
        grid_spec=pltpu.PrefetchScalarGridSpec(
            num_scalar_prefetch=1,
            grid=(2,),
            in_specs=[full, full],
            out_specs=pl.BlockSpec((rows, width), lambda i, s: (i ^ bit(s), 0)),
        ),
        out_shape=jax.ShapeDtypeStruct((2 * rows, width), BF16),
        cost_estimate=TINY,
        compiler_params=pltpu.CompilerParams(vmem_limit_bytes=16 * MIB),
        name="join",
    )(spot, own, other)


class Links:
    def __init__(self, dp, fsdp):
        self.dp, self.fsdp = dp, fsdp
        self.fast = fsdp == 2 and dp >= 4 and dp & (dp - 1) == 0
        here = lax.axis_index("dp")
        self.here = here
        self.core = here % 2
        self.x = (here // 2) % 2
        self.y = lax.axis_index("fsdp")
        self.masks = []
        mask = 4
        while mask < dp:
            self.masks.append(mask)
            mask *= 2

    def spot(self, tiles):
        values = [self.y, 2 * self.core + self.x, self.x, self.core] + tiles
        values += [(self.here // mask) % 2 for mask in self.masks]
        return jnp.stack(values).astype(jnp.int32)

    def swap(self, value, mask):
        return lax.ppermute(value, "dp", [(i, i ^ mask) for i in range(self.dp)])

    def swap_y(self, value):
        return lax.ppermute(value, "fsdp", [(0, 1), (1, 0)])

    def order(self, bit, own, other, axis=0):
        first = bit == 0
        return jnp.concatenate(
            [jnp.where(first, own, other), jnp.where(first, other, own)], axis=axis
        )

    def pieces(self, shards):
        rows = shards[0].shape[0]
        quarter = rows // 4
        start = (2 * self.core + self.x) * quarter
        return jnp.concatenate(
            [lax.dynamic_slice_in_dim(shard, start, quarter, 0) for shard in shards], axis=1
        )

    def weight_stages(self, shards):
        (first,) = yield [(self.pieces(shards), 0)]
        (second,) = yield [(first, 2)]
        rest = yield [(first, 1), (second, 1)]
        return (first, second) + tuple(rest)

    def small_gather(self, shard):
        (far,) = yield [(shard, 0)]
        return far

    def stages(self, spot, send, keep, halve):
        (near,) = yield [(send, 1)]
        keep = keep()
        half = keep.shape[1] // 2
        y, other_y = lambda s: s[Y], lambda s: 1 - s[Y]
        x, other_x = lambda s: s[X], lambda s: 1 - s[X]
        (far,) = yield [(combine(spot, [(keep, other_y, other_x), (near, other_y, other_x)], half), 0)]
        part = combine(spot, [(keep, y, other_x), (near, y, other_x), whole_term(far)], half)
        far = combine(spot, [(keep, other_y, x), (near, other_y, x)], half)
        got, far = yield [(part, 2), (far, 0)]
        terms = [(keep, y, x), (near, y, x), whole_term(far), whole_term(got)]
        masks = [(mask, lambda s, n=n: s[BITS + n]) for n, mask in enumerate(self.masks)]
        if halve:
            size = half
            for mask, bit in masks:
                size //= 2
                (got,) = yield [(combine(spot, narrow(terms, lambda s: 1 - bit(s)), size), mask)]
                terms = narrow(terms, bit) + [whole_term(got)]
            total = combine(spot, terms, size)
            for mask, bit in masks[::-1]:
                (got,) = yield [(total, mask)]
                total = join(spot, bit, total, got)
        else:
            total = combine(spot, terms, half)
            for mask, _ in masks:
                (got,) = yield [(total, mask)]
                total = combine(spot, [whole_term(total), whole_term(got)], half)
        (other,) = yield [(total, 2)]
        rest = yield [(total, 1), (other, 1)]
        return (total, other) + tuple(rest)

    def small_stages(self, send, keep):
        (got,) = yield [(send, 0)]
        total = keep + got
        mask = 1
        while mask < self.dp:
            (got,) = yield [(total, mask)]
            total = total + got
            mask *= 2
        return total

    def permute(self, value, mask):
        return self.swap(value, mask) if mask else self.swap_y(value)


class Flow:
    def __init__(self, links, run):
        self.links, self.run = links, run
        self.sends = next(run)
        self.got = None
        self.result = None

    def take(self, got):
        try:
            self.sends = self.run.send(got)
        except StopIteration as stop:
            self.result = stop.value

    def leave(self, values):
        self.got = [self.links.permute(value, mask) for value, (_, mask) in zip(values, self.sends)]


def advance(anchor, flows):
    flows = [flow for flow in flows if flow.result is None]
    if not flows:
        return anchor
    anchor, gots = lax.optimization_barrier((anchor, [flow.got for flow in flows]))
    for flow, got in zip(flows, gots):
        if got is not None:
            flow.take(got)
    going = [flow for flow in flows if flow.result is None]
    values = [[value for value, _ in flow.sends] for flow in going]
    anchor, values = lax.optimization_barrier((anchor, values))
    for flow, mine in zip(going, values):
        flow.leave(mine)
    return anchor


def make_body(dp, fsdp):
    def body(
        patches,
        page_ids,
        patch_rows,
        live_len,
        norm1_gain,
        norm1_bias,
        w_qkv,
        bias_qv,
        rel_table,
        w_proj,
        bias_proj,
        scale_attn,
        norm2_gain,
        norm2_bias,
        w_up,
        bias_up,
        w_down,
        bias_down,
        scale_mlp,
        cotangent,
    ):
        links = Links(dp, fsdp)
        smalls = (
            norm1_gain,
            norm1_bias,
            scale_attn,
            bias_proj,
            norm2_gain,
            norm2_bias,
            scale_mlp,
            bias_down,
            bias_qv,
            rel_table,
            bias_up,
        )
        total, width = patches.shape[1:]
        fast = links.fast
        pieces = 2 if fast else 1
        hidden = w_up.shape[1]
        tiles = [0, 1, 2, 3]
        if fast:
            tiles = [1 - links.core, links.core, 3 - links.core, 2 + links.core]
        spot = lax.optimization_barrier(links.spot(tiles))

        x, cot = patches[0], cotangent[0]
        if fast:
            loads = [
                Flow(links, links.weight_stages(group)) for group in ([w_qkv], [w_proj, w_up], [w_down])
            ]
            small = smalls[:9] + smalls[10:] + smalls[9:10]
            x, small = advance((x, small), loads[:1])
            mine = pack_small(small)
            far = Flow(links, links.small_gather(mine))
            x = advance(x, [far])
            x, query_side, key_side = rotate_ids(page_ids, patch_rows, live_len, x)
            x, cot = advance((x, cot), [far] + loads[:2])
            cot = rotate(page_ids, cot)
            vectors, bias_all, bias_hidden, mix = unpack_small(spot, mine, far.result)
            x, cot = lax.optimization_barrier((x, cot))
            (x, cot, mix) = advance((x, cot, mix), loads[:2])
            x, mix = advance((x, mix), loads[:1] + loads[2:])
            weight_qkv = Weight((w_qkv,) + loads[0].result, width, 3 * width)
        else:
            x, query_side, key_side = rotate_ids(page_ids, patch_rows, live_len, x)
            cot = rotate(page_ids, cot)
            mine = jnp.concatenate([small.reshape(-1) for small in smalls])
            packed = lax.all_gather(mine, "fsdp", axis=0, tiled=False)
            share = width // fsdp
            vectors = packed[:, : 8 * share].reshape(fsdp, 8, share).transpose(1, 0, 2).reshape(8, width).astype(F32)
            at = 8 * share
            whole = []
            for small in smalls[8:]:
                piece = packed[:, at : at + small.size]
                whole.append(piece.reshape((small.shape[0] * fsdp,) + small.shape[1:]).astype(F32))
                at += small.size
            bias_qv_f, table, bias_hidden = whole
            bias_all = jnp.concatenate([bias_qv_f[:width], jnp.zeros((width,), F32), bias_qv_f[width:]])[None]
            bias_hidden = bias_hidden.reshape(pieces, -1, 768 // pieces).transpose(1, 0, 2).reshape(-1, 1, 768)
            mix = bias_mix(table)
            weight_qkv, weight_proj, weight_up, weight_down = [
                Weight([lax.all_gather(shard, "fsdp", axis=0, tiled=True)], shard.shape[0] * fsdp, shard.shape[1])
                for shard in (w_qkv, w_proj, w_up, w_down)
            ]
        x, mix = lax.optimization_barrier((x, mix))
        normed1, qkv = project_qkv(spot, x, vectors, bias_all, weight_qkv)
        if fast:
            qkv = advance(qkv, loads)
        attended, lse = attention(qkv, query_side, key_side, mix)
        if fast:
            attended = advance(attended, loads)
            weight_proj = Weight((w_proj,) + loads[1].result, width, width)
            weight_up = Weight((w_up,) + loads[1].result, width, hidden, width)
        branch, normed2, dmlp = merge_branch(spot, attended, x, cot, vectors, weight_proj)
        if fast:
            normed2 = advance(normed2, loads)
            weight_down = Weight((w_down,) + loads[2].result, hidden, width)

        flows = []

        def launch(run):
            if links.fast:
                flows.append(Flow(links, run))

        def go(anchor):
            return advance(anchor, flows) if links.fast else anchor

        old = None
        mlp_grads, up_sums = [], []
        for number in range(4):
            chunk, second = divmod(number, 2)
            out, back, grad, sums = mlp(
                spot, number, normed2, dmlp, old, bias_hidden, weight_up, weight_down, pieces
            )
            mlp_grads.append(grad)
            up_sums.append(sums)
            if not second:
                launch(links.stages(spot, grad, lambda chunk=chunk: mlp_grads[2 * chunk + 1], True))
            old = go((out, back))
        branch_m, back = old
        dresid, datt, proj_grad, sums2 = branch_back(
            spot, back, x, branch, cot, attended, vectors, weight_proj, pieces
        )
        datt = go(datt)

        d_parts, sums_qv, tabs, units = [], [], [], []
        for number in range(3):
            d_part, sums, tab = attention_back(
                qkv, datt, attended, lse, query_side, key_side, mix, 2 * number, 2
            )
            sums_qv.append(sums)
            tabs.append(tab)
            datt, d_part = go((datt, d_part))
            d_parts.append(d_part)
            columns = [(d_part, 0), (d_part, 1), (d_part, 2)]
            other = (proj_grad, None, units[-1] if units else None)[number] if fast else None
            unit = weight_unit(spot, normed1, columns, pieces, other)
            if number == 0:
                if fast:
                    launch(links.stages(spot, unit[0], lambda unit=unit: unit[1], True))
                else:
                    first_unit = unit
                datt = go(datt)
            elif number == 1:
                units.append(unit)
                datt, units[0] = lax.optimization_barrier((datt, units[0]))
            elif fast:
                launch(links.stages(spot, unit[0], lambda unit=unit: unit[1], False))
                d_parts[2] = go(d_parts[2])
            else:
                units.append(unit)

        halves = []
        for first in range(0, total // 256, 2):
            half, sums = finish(
                spot, d_parts, x, dresid, branch, branch_m, cot, dmlp, vectors, weight_qkv, first, 2
            )
            half, dmlp = go((half, dmlp))
            halves.append((half, sums))
        (upper, sums_a), (lower, sums_b) = halves
        if fast:
            send, keep = pack_grads(spot, sums_a, sums_b, sums2, sums_qv, up_sums, tabs)
            launch(links.small_stages(send, keep))
            upper = advance(upper, flows[-1:])
            layer_out, grad_patches = unrotate(page_ids, upper, lower)
            layer_out, grad_patches = go((layer_out, grad_patches))
            out_w_up, out_w_down = place_mlp(spot, flows[0].result + flows[1].result, hidden)
            out_w_up, out_w_down = go((out_w_up, out_w_down))
            while any(flow.result is None for flow in flows):
                layer_out = go(layer_out)
            out_w_qkv, out_w_proj = place_qkv(spot, flows[2].result, flows[3].result)
            g = unpack_grads(flows[4].result)
            small_outs = [g[0], g[1], g[8], g[9], g[3], g[2], g[4], g[5], g[10], g[7], g[6]]
        else:
            layer_out, grad_patches = unrotate(page_ids, upper, lower)
            sums1 = sums_a + sums_b
            sums_qv = jnp.concatenate(sums_qv, axis=1)
            small_grads = [
                sums1[0],
                sums1[1],
                jnp.concatenate([sums_qv[0], sums_qv[1]]),
                table_gradient(jnp.concatenate(tabs, axis=0)),
                sums2[3],
                sums2[2],
                sums2[0],
                sums2[1],
                jnp.concatenate(up_sums, axis=0).reshape(-1),
                sums1[3],
                sums1[2],
            ]
            flat = jnp.concatenate([grad.reshape(fsdp, -1) for grad in small_grads], axis=1)
            summed = lax.psum_scatter(lax.psum(flat, "dp"), "fsdp", scatter_dimension=0, tiled=True)[0]
            small_outs = []
            at = 0
            for grad in small_grads:
                size = grad.size // fsdp
                small_outs.append(summed[at : at + size].reshape((grad.shape[0] // fsdp,) + grad.shape[1:]))
                at += size
            stacks = jnp.concatenate(mlp_grads, axis=1).astype(F32).reshape(-1, 2, width, width)
            qkv_units = [unit[0].astype(F32) for unit in (first_unit, units[0], units[1])]
            third = width // 3
            fulls = (
                jnp.concatenate([unit[:, n * third : (n + 1) * third] for n in range(3) for unit in qkv_units], axis=1),
                proj_grad[0].astype(F32),
                jnp.concatenate([stacks[t, 0] for t in range(stacks.shape[0])], axis=1),
                stacks[:, 1].reshape(-1, width),
            )
            out_w_qkv, out_w_proj, out_w_up, out_w_down = [
                lax.psum(lax.psum_scatter(grad, "fsdp", scatter_dimension=0, tiled=True), "dp") for grad in fulls
            ]
        return (
            layer_out[None],
            grad_patches[None],
            small_outs[0],
            small_outs[1],
            out_w_qkv,
            small_outs[2],
            small_outs[3],
            out_w_proj,
            small_outs[4],
            small_outs[5],
            small_outs[6],
            small_outs[7],
            out_w_up,
            small_outs[8],
            out_w_down,
            small_outs[9],
            small_outs[10],
        )

    return body


def solution(mesh):
    rows = P(("dp", "fsdp"), None, None)
    ids = P(("dp", "fsdp"), None)
    vector = P("fsdp")
    matrix = P("fsdp", None)
    in_specs = (
        rows,
        ids,
        ids,
        ids,
        vector,
        vector,
        matrix,
        vector,
        matrix,
        matrix,
        vector,
        vector,
        vector,
        vector,
        matrix,
        vector,
        matrix,
        vector,
        vector,
        rows,
    )
    out_specs = (
        rows,
        rows,
        vector,
        vector,
        matrix,
        vector,
        matrix,
        matrix,
        vector,
        vector,
        vector,
        vector,
        matrix,
        vector,
        matrix,
        vector,
        vector,
    )
    body = make_body(mesh.shape["dp"], mesh.shape["fsdp"])
    return jax.shard_map(body, mesh=mesh, in_specs=in_specs, out_specs=out_specs, check_vma=False)
```

```python
import jax
import jax.numpy as jnp
from jax import lax
from jax.experimental import pallas as pl
from jax.experimental.pallas import tpu as pltpu
from jax.sharding import PartitionSpec as P

HEADS = 12
HEAD = 64
NB = 32
ROWS = 64
PAGES = 16
LONGEST = 512
DEAD_SPAN = 256
EPSILON = 1e-06
BIG = 2.0**100
Y, ME, X, CORE, TILES, BITS = 0, 1, 2, 3, 4, 8
NN = (((1,), (0,)), ((), ()))
NT = (((1,), (1,)), ((), ()))
TN = (((0,), (0,)), ((), ()))
TINY = pl.CostEstimate(flops=1000, transcendentals=0, bytes_accessed=1000)
MIB = 2**20
F32 = jnp.float32
BF16 = jnp.bfloat16


def dg(left, right, dims):
    return lax.dot_general(left, right, dims, preferred_element_type=F32)


def split3(value):
    high = value.astype(BF16)
    rest = value - high.astype(F32)
    mid = rest.astype(BF16)
    low = (rest - mid.astype(F32)).astype(BF16)
    return high, mid, low


def mix_kernel(table_ref, mix_ref):
    head = pl.program_id(0)
    row = lax.broadcasted_iota(jnp.int32, (128, 128), 0)
    col = lax.broadcasted_iota(jnp.int32, (128, 128), 1)
    bucket = jnp.clip(row - col + NB // 2, 0, NB - 1)
    bias = jnp.zeros((128, 128), F32)
    for number in range(NB):
        bias = jnp.where(bucket == number, table_ref[number, head], bias)
    keep = (row == col) & (row >= ROWS) & (row < 112)
    mix = jnp.where((row < ROWS) & (col < ROWS), bias, jnp.where(keep, 1.0, 0.0))
    mix_ref[0] = mix.astype(BF16)


def bias_mix(table):
    return pl.pallas_call(
        mix_kernel,
        grid=(HEADS,),
        in_specs=[pl.BlockSpec(memory_space=pltpu.SMEM)],
        out_specs=pl.BlockSpec((1, 128, 128), lambda head: (head, 0, 0)),
        out_shape=jax.ShapeDtypeStruct((HEADS, 128, 128), BF16),
        compiler_params=pltpu.CompilerParams(vmem_limit_bytes=14 * MIB),
        name="bias_mix",
    )(table.astype(F32))


def attention_kernel(q_ref, k_ref, v_ref, f_ref, g_ref, m_ref, o_ref, l_ref):
    pair = pl.program_id(1)
    size = q_ref.shape[0]
    q = q_ref[...].astype(F32) * HEAD**-0.5
    v = v_ref[...]
    lane = lax.broadcasted_iota(jnp.int32, (size, 128), 1)
    keys = jnp.concatenate([k_ref[...], g_ref[...]], axis=1)
    f = f_ref[...]

    @pl.when(pair == 0)
    def _():
        l_ref[...] = jnp.zeros_like(l_ref)

    lse = l_ref[...]
    out = None
    mines = [(lane // HEAD) == h for h in range(2)]
    scores = []
    for h in range(2):
        extra = dg(f, m_ref[h], NN).astype(BF16)
        queries = jnp.concatenate([jnp.where(mines[h], q, 0.0).astype(BF16), extra], axis=1)
        scores.append(dg(queries, keys, NT))
    for h, score in enumerate(scores):
        top = jnp.max(score, axis=1, keepdims=True)
        expo = jnp.exp(score - top)
        denom = jnp.sum(expo, axis=1, keepdims=True)
        part = dg(expo.astype(BF16), jnp.where(mines[h], v, jnp.zeros_like(v)), NN) / denom
        out = part if out is None else out + part
        lse = jnp.where(lane == 2 * pair + h, top + jnp.log(denom), lse)
    o_ref[...] = out.astype(BF16)
    l_ref[...] = lse


def attention(qkv, query_side, key_side, mix):
    total, width3 = qkv.shape
    width = width3 // 3
    pairs = width // 128
    size = LONGEST
    blocks = total // size
    area = blocks * size * size
    return pl.pallas_call(
        attention_kernel,
        grid=(blocks, pairs),
        in_specs=[
            pl.BlockSpec((size, 128), lambda b, h: (b, h)),
            pl.BlockSpec((size, 128), lambda b, h: (b, pairs + h)),
            pl.BlockSpec((size, 128), lambda b, h: (b, 2 * pairs + h)),
            pl.BlockSpec((size, 128), lambda b, h: (b, 0)),
            pl.BlockSpec((size, 128), lambda b, h: (b, 0)),
            pl.BlockSpec((2, 128, 128), lambda b, h: (h, 0, 0)),
        ],
        out_specs=[
            pl.BlockSpec((size, 128), lambda b, h: (b, h)),
            pl.BlockSpec((size, 128), lambda b, h: (b, 0)),
        ],
        out_shape=[
            jax.ShapeDtypeStruct((total, width), BF16),
            jax.ShapeDtypeStruct((total, 128), F32),
        ],
        cost_estimate=TINY,
        compiler_params=pltpu.CompilerParams(vmem_limit_bytes=14 * MIB),
        name="attention",
    )(qkv, qkv, qkv, query_side, key_side, mix)


def make_attention_back_kernel(first):
    def kernel(q_ref, k_ref, v_ref, da_ref, o_ref, l_ref, f_ref, g_ref, m_ref, d_ref, sum_ref, tab_ref):
        pair = pl.program_id(0) + first
        block = pl.program_id(1)
        size = q_ref.shape[0]
        lane = lax.broadcasted_iota(jnp.int32, (size, 128), 1)
        q = q_ref[...].astype(F32) * HEAD**-0.5
        v = v_ref[...]
        da = da_ref[...]
        product = da.astype(F32) * o_ref[...].astype(F32)
        f = f_ref[...]
        keys = jnp.concatenate([k_ref[...], g_ref[...]], axis=1)
        values = jnp.concatenate([v, jnp.where(lane < 3, 1.0, 0.0).astype(BF16)], axis=1)
        lse_all = l_ref[...]
        dq, dk, dv = None, None, None
        saved = []
        for h in range(2):
            mine = (lane // HEAD) == h
            extra = dg(f, m_ref[h], NN)
            lse = jnp.sum(jnp.where(lane == 2 * pair + h, lse_all, 0.0), axis=1, keepdims=True)
            for place, piece in enumerate(split3(-lse)):
                extra = jnp.where(lane == 112 + place, piece.astype(F32), extra)
            qm = jnp.where(mine, q, 0.0).astype(BF16)
            queries = jnp.concatenate([qm, extra.astype(BF16)], axis=1)
            delta = jnp.sum(jnp.where(mine, product, 0.0), axis=1, keepdims=True)
            columns = jnp.zeros((size, 128), F32)
            for place, piece in enumerate(split3(-delta)):
                columns = jnp.where(lane == place, piece.astype(F32), columns)
            dam = jnp.where(mine, da, jnp.zeros_like(da))
            dax = jnp.concatenate([dam, columns.astype(BF16)], axis=1)
            saved.append((mine, qm, dam, dg(keys, queries, NT), dg(values, dax, NT)))
        for h in range(2):
            mine, qm, dam, score, dprob = saved[h]
            prob = jnp.exp(score)
            dscore = (prob * dprob).astype(BF16)
            dvh = dg(prob.astype(BF16), dam, NN)
            dkh = dg(dscore, qm, NN)
            both = dg(dscore, keys, TN)
            dv = dvh if dv is None else dv + dvh
            dk = dkh if dk is None else dk + dkh
            dq = both[:, :128] if dq is None else jnp.where(mine, both[:, :128], dq)
            rows = both[:, 128:]
            rows_high = rows.astype(BF16)
            rows_low = (rows - rows_high.astype(F32)).astype(BF16)
            grid = dg(f, jnp.concatenate([rows_high, rows_low], axis=1), TN)
            grid = grid[:ROWS, :128] + grid[:ROWS, 128:]

            @pl.when(block == 0)
            def _():
                tab_ref[h] = grid

            @pl.when(block > 0)
            def _():
                tab_ref[h] += grid

        dq = (dq * HEAD**-0.5).astype(BF16)
        dk = dk.astype(BF16)
        dv = dv.astype(BF16)
        d_ref[0] = dq
        d_ref[1] = dk
        d_ref[2] = dv
        sums = jnp.concatenate(
            [
                jnp.sum(dq.astype(F32), axis=0, keepdims=True),
                jnp.sum(dv.astype(F32), axis=0, keepdims=True),
                jnp.zeros((6, 128), F32),
            ],
            axis=0,
        )

        @pl.when(block == 0)
        def _():
            sum_ref[...] = sums

        @pl.when(block > 0)
        def _():
            sum_ref[...] += sums

    return kernel


def attention_back(qkv, d_attended, attended, lse, query_side, key_side, mix, first, count):
    total, width3 = qkv.shape
    pairs = width3 // 3 // 128
    size = LONGEST
    blocks = total // size
    wide = lambda h, b: (b, first + h)
    side = lambda h, b: (b, 0)
    return pl.pallas_call(
        make_attention_back_kernel(first),
        grid=(count, blocks),
        in_specs=[
            pl.BlockSpec((size, 128), wide),
            pl.BlockSpec((size, 128), lambda h, b: (b, pairs + first + h)),
            pl.BlockSpec((size, 128), lambda h, b: (b, 2 * pairs + first + h)),
            pl.BlockSpec((size, 128), wide),
            pl.BlockSpec((size, 128), wide),
            pl.BlockSpec((size, 128), side),
            pl.BlockSpec((size, 128), side),
            pl.BlockSpec((size, 128), side),
            pl.BlockSpec((2, 128, 128), lambda h, b: (first + h, 0, 0)),
        ],
        out_specs=[
            pl.BlockSpec((3, size, 128), lambda h, b: (0, b, h)),
            pl.BlockSpec((8, 128), lambda h, b: (0, h)),
            pl.BlockSpec((2, ROWS, 128), lambda h, b: (h, 0, 0)),
        ],
        out_shape=[
            jax.ShapeDtypeStruct((3, total, 128 * count), BF16),
            jax.ShapeDtypeStruct((8, 128 * count), F32),
            jax.ShapeDtypeStruct((2 * count, ROWS, 128), F32),
        ],
        cost_estimate=TINY,
        compiler_params=pltpu.CompilerParams(vmem_limit_bytes=14 * MIB),
        name="attention_back",
    )(qkv, qkv, qkv, d_attended, attended, lse, query_side, key_side, mix)


def table_gradient(tab):
    row = jnp.arange(ROWS, dtype=jnp.int32)
    bucket = jnp.clip(row[:, None] - row[None, :] + NB // 2, 0, NB - 1)
    onehot = (bucket[:, :, None] == jnp.arange(NB, dtype=jnp.int32)).astype(F32)
    return jnp.einsum("hij,ijb->bh", tab[:, :, :ROWS], onehot, precision=lax.Precision.HIGHEST)


def turn_rows(page, size, total):
    row = lax.broadcasted_iota(jnp.int32, (size, total), 0) + pl.program_id(0) * size
    col = lax.broadcasted_iota(jnp.int32, (size, total), 1)
    source = row + page_start(page)
    source = jnp.where(source >= total, source - total, source)
    return jnp.where(col == source, 1.0, 0.0).astype(BF16)


def rotate_kernel(page_ref, x_ref, xo_ref):
    turn = turn_rows(page_ref[...], xo_ref.shape[0], x_ref.shape[0])
    xo_ref[...] = dg(turn, x_ref[...], NN).astype(BF16)


def rotate_ids_kernel(page_ref, place_ref, live_ref, x_ref, xo_ref, f_ref, g_ref):
    total = x_ref.shape[0]
    page = page_ref[...]
    place = place_ref[...]
    turn = turn_rows(page, xo_ref.shape[0], total)
    xo_ref[...] = dg(turn, x_ref[...], NN).astype(BF16)
    line = lax.broadcasted_iota(jnp.int32, (128, total), 0)
    pos = lax.broadcasted_iota(jnp.int32, (128, total), 1)
    span = pos & (DEAD_SPAN - 1)
    high = 80 + (span >> 4)
    low = 96 + (span & 15)
    early = pos < total - DEAD_SPAN
    in_high = (line >= 80) & (line < 96)
    in_low = (line >= 96) & (line < 112)
    select = (
        (line == place)
        | (line == 64 + page)
        | (line == high)
        | (line == low)
        | (early & (in_high | in_low))
    )
    dead = pos >= live_ref[0, 0]
    other_page = jnp.logical_not(dead) & (line >= 64) & (line < 80) & (line != 64 + page)
    other_place = dead & ((in_high & (line != high)) | (in_low & (line != low)))
    one = (line == place) | ((line >= 112) & (line < 115))
    query_side = jnp.where(select, 1.0, 0.0).astype(BF16)
    key_side = jnp.where(other_page | other_place, -BIG, jnp.where(one, 1.0, 0.0)).astype(BF16)
    f_ref[...] = dg(turn, query_side, NT).astype(BF16)
    g_ref[...] = dg(turn, key_side, NT).astype(BF16)


def rotate(page_ids, values):
    total, width = values.shape
    size = 256
    full = lambda i: (0, 0)
    return pl.pallas_call(
        rotate_kernel,
        grid=(total // size,),
        in_specs=[pl.BlockSpec((1, total), full), pl.BlockSpec((total, width), full)],
        out_specs=pl.BlockSpec((size, width), lambda i: (i, 0)),
        out_shape=jax.ShapeDtypeStruct((total, width), BF16),
        cost_estimate=TINY,
        compiler_params=pltpu.CompilerParams(vmem_limit_bytes=14 * MIB),
        name="rotate",
    )(page_ids, values)


def rotate_ids(page_ids, patch_rows, live_len, values):
    total, width = values.shape
    size = 256
    full = lambda i: (0, 0)
    rows = lambda i: (i, 0)
    return pl.pallas_call(
        rotate_ids_kernel,
        grid=(total // size,),
        in_specs=[
            pl.BlockSpec((1, total), full),
            pl.BlockSpec((1, total), full),
            pl.BlockSpec(memory_space=pltpu.SMEM),
            pl.BlockSpec((total, width), full),
        ],
        out_specs=[
            pl.BlockSpec((size, width), rows),
            pl.BlockSpec((size, 128), rows),
            pl.BlockSpec((size, 128), rows),
        ],
        out_shape=[
            jax.ShapeDtypeStruct((total, width), BF16),
            jax.ShapeDtypeStruct((total, 128), BF16),
            jax.ShapeDtypeStruct((total, 128), BF16),
        ],
        cost_estimate=TINY,
        compiler_params=pltpu.CompilerParams(vmem_limit_bytes=14 * MIB),
        name="rotate_ids",
    )(page_ids, patch_rows, live_len, values)


def norm_parts(values):
    center = values - jnp.mean(values, axis=-1, keepdims=True)
    spread = jnp.mean(center * center, axis=-1, keepdims=True)
    scale = lax.rsqrt(spread + EPSILON)
    return center * scale, scale


def norm_back(grad, unit, scale, gain):
    inner = grad * gain
    mean = jnp.mean(inner, axis=-1, keepdims=True)
    mixed = jnp.mean(inner * unit, axis=-1, keepdims=True)
    return scale * (inner - mean - unit * mixed)


def gelu_parts(upper):
    c = 0.7978845608028654
    square = upper * upper
    wave = jnp.tanh(upper * (c + (c * 0.044715) * square))
    half = 0.5 + 0.5 * wave
    value = upper * half
    slope = half + (value * (1.0 - wave)) * (c + (3 * c * 0.044715) * square)
    return value, slope


GAIN1, SHIFT1, SCALE1, BIAS_OUT, GAIN2, SHIFT2, SCALE2, BIAS_LAST = range(8)


ANY = pl.BlockSpec(memory_space=pl.ANY)


class Weight:
    def __init__(self, arrays, rows, columns, at=0):
        self.arrays, self.rows, self.columns, self.at = tuple(arrays), rows, columns, at

    def copies(self, refs, spot_ref, target, sem, column=0, columns=None, to=0):
        columns = columns or self.columns
        lanes = pl.ds(to, columns)
        if len(refs) == 1:
            return [pltpu.make_async_copy(refs[0].at[:, pl.ds(column, columns)], target.at[:, lanes], sem)]
        y, me = spot_ref[0], spot_ref[1]
        size = self.rows // 2
        quarter = size // 4
        start = pl.multiple_of(y * size, 16)
        jobs = [
            pltpu.make_async_copy(refs[0].at[:, pl.ds(column, columns)], target.at[pl.ds(start, size), lanes], sem)
        ]
        for number, ref in enumerate(refs[1:]):
            start = pl.multiple_of((1 - y) * size + (me ^ number) * quarter, 16)
            jobs.append(
                pltpu.make_async_copy(
                    ref.at[:, pl.ds(self.at + column, columns)], target.at[pl.ds(start, quarter), lanes], sem
                )
            )
        return jobs


def outside(arrays):
    return [pltpu.with_memory_space_constraint(array, pltpu.HBM) for array in arrays]


def run_copies(jobs):
    for job in jobs:
        job.start()
    for job in jobs:
        job.wait()


def make_qkv_kernel(weight):
    count = len(weight.arrays)

    def kernel(spot_ref, x_ref, vec_ref, bias_ref, *refs):
        normed_ref, qkv_ref, w, sem = refs[count:]

        @pl.when(pl.program_id(0) == 0)
        def _():
            run_copies(weight.copies(refs[:count], spot_ref, w, sem))

        unit, _ = norm_parts(x_ref[...].astype(F32))
        normed = (unit * vec_ref[GAIN1 : GAIN1 + 1] + vec_ref[SHIFT1 : SHIFT1 + 1]).astype(BF16)
        normed_ref[...] = normed
        qkv_ref[...] = (dg(normed, w[...], NN) + bias_ref[...]).astype(BF16)

    return kernel


def project_qkv(spot, x, vectors, bias, weight):
    total, width = x.shape
    size = 256
    wide = weight.columns
    full = lambda i, s: (0, 0)
    rows = lambda i, s: (i, 0)
    return pl.pallas_call(
        make_qkv_kernel(weight),
        grid_spec=pltpu.PrefetchScalarGridSpec(
            num_scalar_prefetch=1,
            grid=(total // size,),
            in_specs=[
                pl.BlockSpec((size, width), rows),
                pl.BlockSpec((8, width), full),
                pl.BlockSpec((1, wide), full),
            ]
            + [ANY] * len(weight.arrays),
            out_specs=[pl.BlockSpec((size, width), rows), pl.BlockSpec((size, wide), rows)],
            scratch_shapes=[pltpu.VMEM((width, wide), BF16), pltpu.SemaphoreType.DMA],
        ),
        out_shape=[
            jax.ShapeDtypeStruct((total, width), BF16),
            jax.ShapeDtypeStruct((total, wide), BF16),
        ],
        cost_estimate=TINY,
        compiler_params=pltpu.CompilerParams(vmem_limit_bytes=14 * MIB),
        name="project_qkv",
    )(spot, x, vectors, bias, *outside(weight.arrays))


def make_merge_kernel(weight):
    count = len(weight.arrays)

    def kernel(spot_ref, a_ref, x_ref, c_ref, vec_ref, *refs):
        branch_ref, normed_ref, dmlp_ref, w, sem = refs[count:]

        @pl.when(pl.program_id(0) == 0)
        def _():
            run_copies(weight.copies(refs[:count], spot_ref, w, sem))

        vec = lambda row: vec_ref[row : row + 1]
        branch = dg(a_ref[...], w[...], NN) + vec(BIAS_OUT)
        branch_ref[...] = branch
        unit, _ = norm_parts(x_ref[...].astype(F32) + vec(SCALE1) * branch)
        normed_ref[...] = (unit * vec(GAIN2) + vec(SHIFT2)).astype(BF16)
        dmlp_ref[...] = (vec(SCALE2) * c_ref[...].astype(F32)).astype(BF16)

    return kernel


def merge_branch(spot, attended, x, cot, vectors, weight):
    total, width = x.shape
    size = 256
    full = lambda i, s: (0, 0)
    block = pl.BlockSpec((size, width), lambda i, s: (i, 0))
    return pl.pallas_call(
        make_merge_kernel(weight),
        grid_spec=pltpu.PrefetchScalarGridSpec(
            num_scalar_prefetch=1,
            grid=(total // size,),
            in_specs=[block, block, block, pl.BlockSpec((8, width), full)] + [ANY] * len(weight.arrays),
            out_specs=[block, block, block],
            scratch_shapes=[pltpu.VMEM((width, width), BF16), pltpu.SemaphoreType.DMA],
        ),
        out_shape=[
            jax.ShapeDtypeStruct((total, width), F32),
            jax.ShapeDtypeStruct((total, width), BF16),
            jax.ShapeDtypeStruct((total, width), BF16),
        ],
        cost_estimate=TINY,
        compiler_params=pltpu.CompilerParams(vmem_limit_bytes=14 * MIB),
        name="merge_branch",
    )(spot, attended, x, cot, vectors, *outside(weight.arrays))


def make_mlp_kernel(which, pieces, more, blocks, size, weight_up, weight_down):
    up_count = len(weight_up.arrays)
    down_count = len(weight_down.arrays)
    deep = 768
    part = deep // pieces

    def load(spot_ref, ups, downs, up, down, sems):
        tile = spot_ref[TILES + which]
        hidden = weight_up.columns // pieces
        jobs = []
        for piece in range(pieces):
            column = pl.multiple_of(piece * hidden + tile * part, 128)
            jobs += weight_up.copies(ups, spot_ref, up, sems.at[0], column, part, piece * part)
        if down_count == 1:
            start = pl.multiple_of(tile * deep, 16)
            jobs.append(pltpu.make_async_copy(downs[0].at[pl.ds(start, deep)], down, sems.at[1]))
        else:
            y, me = spot_ref[0], spot_ref[1]
            start = pl.multiple_of(tile * part, 16)
            to = pl.multiple_of(y * part, 16)
            jobs.append(pltpu.make_async_copy(downs[0].at[pl.ds(start, part)], down.at[pl.ds(to, part)], sems.at[1]))
            to = pl.multiple_of((1 - y) * part, 16)
            for number, ref in enumerate(downs[1:]):

                @pl.when((me ^ number) == tile)
                def _():
                    run_copies([pltpu.make_async_copy(ref, down.at[pl.ds(to, part)], sems.at[2])])

        run_copies(jobs)

    def kernel(spot_ref, n_ref, d_ref, bias_ref, *refs):
        if more:
            old_out_ref, old_back_ref = refs[:2]
            refs = refs[2:]
        ups = refs[:up_count]
        downs = refs[up_count : up_count + down_count]
        out_ref, back_ref, grad_ref, sum_ref, up, down, normeds, dmlps, activs, duppers, sems = refs[
            up_count + down_count :
        ]
        block = pl.program_id(0)
        rows = pl.ds(block * size, size)

        @pl.when(block == 0)
        def _():
            load(spot_ref, ups, downs, up, down, sems)

        @pl.when(block < blocks)
        def _():
            normed = n_ref[...]
            dmlp = d_ref[...]
            normeds[rows] = normed
            dmlps[rows] = dmlp
            bias = bias_ref[0]
            value, slope = gelu_parts(dg(normed, up[...], NN) + bias)
            activ = value.astype(BF16)
            activs[rows] = activ
            dupper = (dg(dmlp, down[...], NT) * slope).astype(BF16)
            duppers[rows] = dupper
            out = dg(activ, down[...], NN)
            back = dg(dupper, up[...], NT)
            if more:
                out += old_out_ref[...]
                back += old_back_ref[...]
            out_ref[...] = out
            back_ref[...] = back
            sums = jnp.sum(dupper.astype(F32), axis=0, keepdims=True)

            @pl.when(block == 0)
            def _():
                sum_ref[...] = sums

            @pl.when(block > 0)
            def _():
                sum_ref[...] += sums

        @pl.when(block == blocks)
        def _():
            side = normeds.shape[1] // pieces

            @pl.loop(0, 3)
            def _(n):
                lanes = pl.ds(pl.multiple_of(n * 256, 256), 256)
                dup = dg(normeds[...], duppers[:, lanes], TN).astype(BF16)
                ddown = dg(activs[...], dmlps[:, lanes], TN).astype(BF16)
                for piece in range(pieces):
                    grad_ref[piece, :side, lanes] = dup[piece * side : (piece + 1) * side]
                    grad_ref[piece, side:, lanes] = ddown[piece * part : (piece + 1) * part]

    return kernel


def mlp(spot, which, normed, dmlp, old, bias_up, weight_up, weight_down, pieces):
    total, width = normed.shape
    deep = 768
    size = 256
    blocks = total // size
    more = old is not None
    row = pl.BlockSpec((size, width), lambda r, s: (jnp.minimum(r, blocks - 1), 0))
    arrays = outside(weight_up.arrays + weight_down.arrays)
    stack = (width + deep) // pieces
    return pl.pallas_call(
        make_mlp_kernel(which, pieces, more, blocks, size, weight_up, weight_down),
        grid_spec=pltpu.PrefetchScalarGridSpec(
            num_scalar_prefetch=1,
            grid=(blocks + 1,),
            in_specs=[row, row, pl.BlockSpec((1, 1, deep), lambda r, s: (s[TILES + which], 0, 0))]
            + ([row, row] if more else [])
            + [ANY] * len(arrays),
            out_specs=[
                row,
                row,
                pl.BlockSpec((pieces, stack, width), lambda r, s: (0, 0, 0)),
                pl.BlockSpec((1, deep), lambda r, s: (0, 0)),
            ],
            scratch_shapes=[
                pltpu.VMEM((width, deep), BF16),
                pltpu.VMEM((deep, width), BF16),
                pltpu.VMEM((total, width), BF16),
                pltpu.VMEM((total, width), BF16),
                pltpu.VMEM((total, deep), BF16),
                pltpu.VMEM((total, deep), BF16),
                pltpu.SemaphoreType.DMA((3,)),
            ],
        ),
        out_shape=[
            jax.ShapeDtypeStruct((total, width), F32),
            jax.ShapeDtypeStruct((total, width), F32),
            jax.ShapeDtypeStruct((pieces, stack, width), BF16),
            jax.ShapeDtypeStruct((1, deep), F32),
        ],
        cost_estimate=TINY,
        compiler_params=pltpu.CompilerParams(vmem_limit_bytes=14 * MIB),
        name="mlp",
    )(spot, normed, dmlp, bias_up, *(old or ()), *arrays)


def make_branch_kernel(pieces, blocks, weight):
    count = len(weight.arrays)

    def kernel(spot_ref, d_ref, x_ref, b_ref, c_ref, a_ref, vec_ref, *refs):
        resid_ref, datt_ref, grad_ref, sum_ref, acc, w, sem = refs[count:]
        block = pl.program_id(0)

        @pl.when(block == 0)
        def _():
            run_copies(weight.copies(refs[:count], spot_ref, w, sem))

        vec = lambda row: vec_ref[row : row + 1]
        dnormed = d_ref[...]
        branch = b_ref[...]
        unit, scale = norm_parts(x_ref[...].astype(F32) + vec(SCALE1) * branch)
        dresid = c_ref[...].astype(F32) + norm_back(dnormed, unit, scale, vec(GAIN2))
        resid_ref[...] = dresid
        dbranch = (vec(SCALE1) * dresid).astype(BF16)
        datt_ref[...] = dg(dbranch, w[...], NT).astype(BF16)
        part = dg(a_ref[...], dbranch, TN)
        rows = [dnormed * unit, dnormed, dresid * branch, dbranch.astype(F32)]
        sums = jnp.concatenate(
            [jnp.sum(row, axis=0, keepdims=True) for row in rows] + [jnp.zeros((4, dnormed.shape[1]), F32)], axis=0
        )

        @pl.when(block == 0)
        def _():
            acc[...] = part
            sum_ref[...] = sums

        @pl.when(block > 0)
        def _():
            acc[...] += part
            sum_ref[...] += sums

        @pl.when(block == blocks - 1)
        def _():
            side = acc.shape[0] // pieces
            for piece in range(pieces):
                grad_ref[piece] = acc[piece * side : (piece + 1) * side].astype(BF16)

    return kernel


def branch_back(spot, back, x, branch, cot, attended, vectors, weight, pieces):
    total, width = x.shape
    size = 256
    blocks = total // size
    block = pl.BlockSpec((size, width), lambda i, s: (i, 0))
    full = lambda i, s: (0, 0)
    return pl.pallas_call(
        make_branch_kernel(pieces, blocks, weight),
        grid_spec=pltpu.PrefetchScalarGridSpec(
            num_scalar_prefetch=1,
            grid=(blocks,),
            in_specs=[block] * 5 + [pl.BlockSpec((8, width), full)] + [ANY] * len(weight.arrays),
            out_specs=[
                block,
                block,
                pl.BlockSpec((pieces, width // pieces, width), lambda i, s: (0, 0, 0)),
                pl.BlockSpec((8, width), full),
            ],
            scratch_shapes=[
                pltpu.VMEM((width, width), F32),
                pltpu.VMEM((width, width), BF16),
                pltpu.SemaphoreType.DMA,
            ],
        ),
        out_shape=[
            jax.ShapeDtypeStruct((total, width), F32),
            jax.ShapeDtypeStruct((total, width), BF16),
            jax.ShapeDtypeStruct((pieces, width // pieces, width), BF16),
            jax.ShapeDtypeStruct((8, width), F32),
        ],
        cost_estimate=TINY,
        compiler_params=pltpu.CompilerParams(vmem_limit_bytes=14 * MIB),
        name="branch_back",
    )(spot, back, x, branch, cot, attended, vectors, *outside(weight.arrays))


def make_weight_kernel(pieces, parts, blocks, split, paired):
    def kernel(spot_ref, n_ref, *refs):
        columns, refs = refs[:parts], refs[parts:]
        block = pl.program_id(0)
        rows = jnp.concatenate([ref[0] for ref in columns], axis=1)
        part = dg(n_ref[...], rows, TN)
        acc = refs[-1]

        @pl.when(block == 0)
        def _():
            acc[...] = part

        @pl.when(block > 0)
        def _():
            acc[...] += part

        @pl.when(block == blocks - 1)
        def _():
            side = acc.shape[0] // pieces
            if not split:
                for piece in range(pieces):
                    refs[0][piece] = acc[piece * side : (piece + 1) * side].astype(BF16)
                return
            half = side // 2
            core = spot_ref[CORE]
            for out_ref, which in ((refs[-3], 1 - core), (refs[-2], core)):
                for piece in range(pieces):
                    start = pl.multiple_of(piece * side + which * half, 16)
                    out_ref[piece, :half] = acc[pl.ds(start, half)].astype(BF16)
                    if paired:
                        start = pl.multiple_of(which * half, 16)
                        out_ref[piece, half:] = refs[0][piece, pl.ds(start, half)]

    return kernel


def weight_unit(spot, normed, columns, pieces, split, other=None):
    total, width = normed.shape
    parts = len(columns)
    wide = columns[0][0].shape[2]
    size = 512
    paired = other is not None
    unit = (pieces, width // pieces, parts * wide)
    out = (pieces, width // pieces // (2 if split and not paired else 1), parts * wide)
    outs = 2 if split else 1
    result = pl.pallas_call(
        make_weight_kernel(pieces, parts, total // size, split, paired),
        grid_spec=pltpu.PrefetchScalarGridSpec(
            num_scalar_prefetch=1,
            grid=(total // size,),
            in_specs=[pl.BlockSpec((size, width), lambda i, s: (i, 0))]
            + [pl.BlockSpec((1, size, wide), lambda i, s, n=n: (n, i, 0)) for _, n in columns]
            + [pl.BlockSpec(unit, lambda i, s: (0, 0, 0))] * paired,
            out_specs=[pl.BlockSpec(out, lambda i, s: (0, 0, 0))] * outs,
            scratch_shapes=[pltpu.VMEM((width, parts * wide), F32)],
        ),
        out_shape=[jax.ShapeDtypeStruct(out, BF16)] * outs,
        cost_estimate=TINY,
        compiler_params=pltpu.CompilerParams(vmem_limit_bytes=14 * MIB),
        name="weight_unit",
    )(spot, normed, *[array for array, _ in columns], *([other] if paired else []))
    return result if split else result[0]


def make_finish_kernel(parts, weight):
    count = len(weight.arrays)

    def kernel(spot_ref, *refs):
        grads = refs[:parts]
        x_ref, r_ref, b_ref, m_ref, c_ref, d_ref, vec_ref = refs[parts : parts + 7]
        out_ref, sum_ref, w_ref, sem = refs[parts + 7 + count :]
        block = pl.program_id(0)

        @pl.when(block == 0)
        def _():
            run_copies(weight.copies(refs[parts + 7 : parts + 7 + count], spot_ref, w_ref, sem))

        vec = lambda row: vec_ref[row : row + 1]
        width = x_ref.shape[1]
        dnormed = None
        for i in range(3):
            rows = jnp.concatenate([ref[i] for ref in grads], axis=1)
            part = dg(rows, w_ref[:, i * width : (i + 1) * width], NT)
            dnormed = part if dnormed is None else dnormed + part
        x = x_ref[...].astype(F32)
        unit, scale = norm_parts(x)
        dx = r_ref[...] + norm_back(dnormed, unit, scale, vec(GAIN1))
        high = dx.astype(BF16)
        branch_m = m_ref[...] + vec(BIAS_LAST)
        out = x + vec(SCALE1) * b_ref[...] + vec(SCALE2) * branch_m
        out_ref[:, :width] = out.astype(BF16)
        out_ref[:, width : 2 * width] = high
        out_ref[:, 2 * width :] = (dx - high.astype(F32)).astype(BF16)
        rows = [dnormed * unit, dnormed, c_ref[...].astype(F32) * branch_m, d_ref[...].astype(F32)]
        sums = jnp.concatenate(
            [jnp.sum(row, axis=0, keepdims=True) for row in rows] + [jnp.zeros((4, width), F32)], axis=0
        )

        @pl.when(block == 0)
        def _():
            sum_ref[...] = sums

        @pl.when(block > 0)
        def _():
            sum_ref[...] += sums

    return kernel


def finish(spot, grads, x, dresid, branch, branch_m, cot, dmlp, vectors, weight, first, blocks):
    width = x.shape[1]
    size = 256
    block = pl.BlockSpec((size, width), lambda i, s: (first + i, 0))
    full = lambda i, s: (0, 0)
    return pl.pallas_call(
        make_finish_kernel(len(grads), weight),
        grid_spec=pltpu.PrefetchScalarGridSpec(
            num_scalar_prefetch=1,
            grid=(blocks,),
            in_specs=[pl.BlockSpec((3, size, grad.shape[2]), lambda i, s: (0, first + i, 0)) for grad in grads]
            + [block] * 6
            + [pl.BlockSpec((8, width), full)]
            + [ANY] * len(weight.arrays),
            out_specs=[pl.BlockSpec((size, 3 * width), lambda i, s: (i, 0)), pl.BlockSpec((8, width), full)],
            scratch_shapes=[pltpu.VMEM((width, weight.columns), BF16), pltpu.SemaphoreType.DMA],
        ),
        out_shape=[
            jax.ShapeDtypeStruct((size * blocks, 3 * width), BF16),
            jax.ShapeDtypeStruct((8, width), F32),
        ],
        cost_estimate=TINY,
        compiler_params=pltpu.CompilerParams(vmem_limit_bytes=14 * MIB),
        name="finish",
    )(spot, *grads, x, dresid, branch, branch_m, cot, dmlp, vectors, *outside(weight.arrays))


def page_start(page):
    total = page.shape[1]
    lane = lax.broadcasted_iota(jnp.int32, (1, total), 1)
    found = (page == pltpu.roll(page, total - (LONGEST - 1), 1)) & (lane <= total - LONGEST)
    return jnp.min(jnp.where(found, lane, total), axis=1, keepdims=True)


def unrotate_kernel(page_ref, a_ref, b_ref, o_ref, g_ref):
    size, width = o_ref.shape
    total = 2 * a_ref.shape[0]
    row = lax.broadcasted_iota(jnp.int32, (size, total), 0) + pl.program_id(0) * size
    col = lax.broadcasted_iota(jnp.int32, (size, total), 1)
    source = row - page_start(page_ref[...])
    source = jnp.where(source < 0, source + total, source)
    turn = jnp.where(col == source, 1.0, 0.0).astype(BF16)
    value = dg(turn[:, : total // 2], a_ref[...], NN) + dg(turn[:, total // 2 :], b_ref[...], NN)
    o_ref[...] = value[:, :width].astype(BF16)
    g_ref[...] = value[:, width : 2 * width] + value[:, 2 * width :]


def unrotate(page_ids, upper, lower):
    half, width3 = upper.shape
    total = 2 * half
    width = width3 // 3
    size = 256
    block = pl.BlockSpec((size, width), lambda i: (i, 0))
    full = lambda i: (0, 0)
    return pl.pallas_call(
        unrotate_kernel,
        grid=(total // size,),
        in_specs=[pl.BlockSpec((1, total), full)] + [pl.BlockSpec((half, width3), full)] * 2,
        out_specs=[block, block],
        out_shape=[
            jax.ShapeDtypeStruct((total, width), BF16),
            jax.ShapeDtypeStruct((total, width), F32),
        ],
        cost_estimate=TINY,
        compiler_params=pltpu.CompilerParams(vmem_limit_bytes=14 * MIB),
        name="unrotate",
    )(page_ids, upper, lower)


QV_ROW, UP_ROW, TABLE_ROW = 8, 10, 16


def pack_kernel(*refs):
    out_ref = refs[-1]
    lanes = out_ref.shape[1]
    out_ref[...] = jnp.zeros_like(out_ref)
    at = 0
    for ref in refs[:-1]:
        if len(ref.shape) == 1:
            for n in range(ref.shape[0] // lanes):
                out_ref[at : at + 1, :] = ref[n * lanes : (n + 1) * lanes].astype(F32).reshape(1, lanes)
                at += 1
        else:
            rows, columns = ref.shape
            out_ref[TABLE_ROW : TABLE_ROW + rows, :columns] = ref[...].astype(F32)


def pack_small(smalls):
    lanes = smalls[0].shape[0]
    return pl.pallas_call(
        pack_kernel, out_shape=jax.ShapeDtypeStruct((32, lanes), F32), cost_estimate=TINY, name="pack_small"
    )(*smalls)


def unpack_kernel(spot_ref, mine_ref, far_ref, vec_ref, qkv_ref, up_ref, mix_ref):
    first = spot_ref[Y] == 0
    low = jnp.where(first, mine_ref[...], far_ref[...])
    high = jnp.where(first, far_ref[...], mine_ref[...])
    lanes = low.shape[1]
    vec_ref[:, :lanes] = low[:8]
    vec_ref[:, lanes:] = high[:8]
    qkv_ref[...] = jnp.zeros_like(qkv_ref)
    for n in range(2):
        row = QV_ROW + n
        qkv_ref[:, n * lanes : (n + 1) * lanes] = low[row : row + 1]
        qkv_ref[:, (4 + n) * lanes : (5 + n) * lanes] = high[row : row + 1]
    for n in range(up_ref.shape[0]):
        row = UP_ROW + n
        up_ref[n, :, :lanes] = low[row : row + 1]
        up_ref[n, :, lanes:] = high[row : row + 1]
    row = lax.broadcasted_iota(jnp.int32, (128, 128), 0)
    col = lax.broadcasted_iota(jnp.int32, (128, 128), 1)
    inner = (row < ROWS) & (col < ROWS)
    bucket = jnp.where(inner, jnp.clip(row - col + NB // 2, 0, NB - 1), NB)
    keep = jnp.where((row == col) & (row >= ROWS) & (row < 112), 1.0, 0.0)
    for head in range(mix_ref.shape[0]):
        mix = keep
        for number in range(NB):
            half = low if number < NB // 2 else high
            at = TABLE_ROW + number % (NB // 2)
            mix = jnp.where(bucket == number, half[at : at + 1, head : head + 1], mix)
        mix_ref[head] = mix.astype(BF16)


def unpack_small(spot, mine, far):
    lanes = mine.shape[1]
    width = 2 * lanes
    smem = pl.BlockSpec(memory_space=pltpu.SMEM)
    vmem = pl.BlockSpec(memory_space=pltpu.VMEM)
    return pl.pallas_call(
        unpack_kernel,
        in_specs=[smem, vmem, vmem],
        out_shape=[
            jax.ShapeDtypeStruct((8, width), F32),
            jax.ShapeDtypeStruct((1, 3 * width), F32),
            jax.ShapeDtypeStruct((4, 1, width), F32),
            jax.ShapeDtypeStruct((HEADS, 128, 128), BF16),
        ],
        cost_estimate=TINY,
        compiler_params=pltpu.CompilerParams(vmem_limit_bytes=14 * MIB),
        name="unpack_small",
    )(spot, mine, far)


def pack_grads_kernel(spot_ref, *refs):
    a_ref, b_ref, two_ref = refs[:3]
    qv_refs, up_refs, tab_refs = refs[3:6], refs[6:10], refs[10:13]
    send_ref, keep_ref, both = refs[13:]
    lanes = both.shape[2]
    both[...] = jnp.zeros_like(both)
    one = a_ref[...] + b_ref[...]
    two = two_ref[...]
    rows = [one[0:1], one[1:2], two[2:3], two[3:4], two[0:1], two[1:2], one[2:3], one[3:4]]
    for n, row in enumerate(rows):
        for half in range(2):
            both[half, n : n + 1] = row[:, half * lanes : (half + 1) * lanes]
    for half in range(2):
        row = jnp.concatenate([ref[half : half + 1] for ref in qv_refs], axis=1)
        for n in range(2):
            both[half, QV_ROW + n : QV_ROW + n + 1] = row[:, n * lanes : (n + 1) * lanes]
    zero = spot_ref[CORE] == 0
    for chunk in range(2):
        first, second = up_refs[2 * chunk][...], up_refs[2 * chunk + 1][...]
        tiles = (jnp.where(zero, second, first), jnp.where(zero, first, second))
        for n, tile in enumerate(tiles):
            row = UP_ROW + 2 * chunk + n
            for half in range(2):
                both[half, row : row + 1] = tile[:, half * lanes : (half + 1) * lanes]
    sums = []
    lane = lax.broadcasted_iota(jnp.int32, (ROWS, 128), 1)
    line = lax.broadcasted_iota(jnp.int32, (ROWS, 128), 0)
    for ref in tab_refs:
        for n in range(ref.shape[0]):
            value = jnp.where(lane < ROWS, ref[n], 0.0)
            for bit in range(6):
                value = jnp.where((line >> bit) & 1 == 1, pltpu.roll(value, 128 - (1 << bit), 1), value)
            sums.append(jnp.sum(value, axis=0, keepdims=True))
    sums.append(jnp.zeros((16 - len(sums), 128), F32))
    sums = jnp.concatenate(sums, axis=0)
    number = lax.broadcasted_iota(jnp.int32, (NB, 128), 0)
    shift = lax.broadcasted_iota(jnp.int32, (NB, 128), 1)
    shift = jnp.where(shift < ROWS, shift, shift - 128)
    pick = jnp.where(jnp.clip(NB // 2 - shift, 0, NB - 1) == number, 1.0, 0.0).astype(BF16)
    table = None
    for piece in split3(sums):
        part = dg(pick, piece, NT)
        table = part if table is None else table + part
    for half in range(2):
        both[half, TABLE_ROW : TABLE_ROW + NB // 2, :16] = table[half * (NB // 2) : (half + 1) * (NB // 2)]
    y = spot_ref[Y]
    send_ref[...] = both[1 - y]
    keep_ref[...] = both[y]


def pack_grads(spot, sums_a, sums_b, sums2, sums_qv, up_sums, tabs):
    lanes = sums2.shape[1] // 2
    smem = pl.BlockSpec(memory_space=pltpu.SMEM)
    vmem = pl.BlockSpec(memory_space=pltpu.VMEM)
    return pl.pallas_call(
        pack_grads_kernel,
        in_specs=[smem] + [vmem] * 13,
        out_shape=[jax.ShapeDtypeStruct((32, lanes), F32)] * 2,
        scratch_shapes=[pltpu.VMEM((2, 32, lanes), F32)],
        cost_estimate=TINY,
        compiler_params=pltpu.CompilerParams(vmem_limit_bytes=14 * MIB),
        name="pack_grads",
    )(spot, sums_a, sums_b, sums2, *sums_qv, *up_sums, *tabs)


def unpack_grads_kernel(in_ref, *refs):
    lanes = in_ref.shape[1]
    for n in range(8):
        refs[n][...] = in_ref[n : n + 1].reshape(lanes)
    for n in range(2):
        refs[8][n * lanes : (n + 1) * lanes] = in_ref[QV_ROW + n : QV_ROW + n + 1].reshape(lanes)
    refs[9][...] = in_ref[TABLE_ROW:, :HEADS]
    for n in range(4):
        refs[10][n * lanes : (n + 1) * lanes] = in_ref[UP_ROW + n : UP_ROW + n + 1].reshape(lanes)


def unpack_grads(value):
    lanes = value.shape[1]
    return pl.pallas_call(
        unpack_grads_kernel,
        out_shape=[jax.ShapeDtypeStruct((lanes,), F32)] * 8
        + [
            jax.ShapeDtypeStruct((2 * lanes,), F32),
            jax.ShapeDtypeStruct((NB // 2, HEADS), F32),
            jax.ShapeDtypeStruct((4 * lanes,), F32),
        ],
        cost_estimate=TINY,
        compiler_params=pltpu.CompilerParams(vmem_limit_bytes=14 * MIB),
        name="unpack_grads",
    )(value)


def place_mlp_kernel(spot_ref, *refs):
    up_ref, down_ref = refs[8:]
    side = refs[0].shape[0]
    hidden = up_ref.shape[1] // 2
    core, x = spot_ref[CORE], spot_ref[X]
    for chunk in range(2):
        for n in range(4):
            ref = refs[4 * chunk + n]
            start = pl.multiple_of((2 * chunk + (core ^ (n // 2))) * side, 128)

            @pl.when((x ^ (n % 2)) == 0)
            def _():
                @pl.loop(0, side // 64)
                def _(m):
                    rows = pl.ds(pl.multiple_of(m * 64, 64), 64)
                    value = ref[rows].astype(F32)
                    up_ref[rows, pl.ds(start, side)] = value[:, :side]
                    up_ref[rows, pl.ds(start + hidden, side)] = value[:, side:]

            @pl.when((x ^ (n % 2)) == 1)
            def _():
                @pl.loop(0, side // 64)
                def _(m):
                    rows = pl.ds(pl.multiple_of(m * 64, 64), 64)
                    down_ref[pl.ds(pl.multiple_of(start + m * 64, 64), 64)] = ref[rows].astype(F32)


def place_mlp(spot, quarters, hidden):
    side, width = quarters[0].shape
    smem = pl.BlockSpec(memory_space=pltpu.SMEM)
    vmem = pl.BlockSpec(memory_space=pltpu.VMEM)
    return pl.pallas_call(
        place_mlp_kernel,
        in_specs=[smem] + [vmem] * 8,
        out_shape=[
            jax.ShapeDtypeStruct((side, hidden), F32),
            jax.ShapeDtypeStruct((hidden // 2, width), F32),
        ],
        cost_estimate=TINY,
        compiler_params=pltpu.CompilerParams(vmem_limit_bytes=14 * MIB),
        name="place_mlp",
    )(spot, *quarters)


def place_qkv_kernel(spot_ref, *refs):
    qkv_ref, proj_ref = refs[8:]
    half, width = refs[0].shape
    third = width // 3
    core, x = spot_ref[CORE], spot_ref[X]

    def put(rows, value, number):
        for n in range(3):
            start = n * width + number * third
            qkv_ref[rows, start : start + third] = value[:, n * third : (n + 1) * third]

    qkv_ref[...] = jnp.zeros_like(qkv_ref)
    for n in range(4):
        start = (core ^ (n // 2)) * half
        rows = pl.ds(pl.multiple_of(start, 8), half)
        early = refs[n]

        @pl.when((x ^ (n % 2)) == 0)
        def _():
            put(rows, early[...].astype(F32), 0)

        @pl.when((x ^ (n % 2)) == 1)
        def _():
            proj_ref[rows] = early[...].astype(F32)

        rows = pl.ds(pl.multiple_of(start + (x ^ (n % 2)) * (half // 2), 8), half // 2)
        put(rows, refs[4 + n][...].astype(F32), 1)


def place_qkv(spot, early, middle):
    half, width = early[0].shape
    smem = pl.BlockSpec(memory_space=pltpu.SMEM)
    vmem = pl.BlockSpec(memory_space=pltpu.VMEM)
    return pl.pallas_call(
        place_qkv_kernel,
        in_specs=[smem] + [vmem] * 8,
        out_shape=[
            jax.ShapeDtypeStruct((2 * half, 3 * width), F32),
            jax.ShapeDtypeStruct((2 * half, width), F32),
        ],
        cost_estimate=TINY,
        compiler_params=pltpu.CompilerParams(vmem_limit_bytes=14 * MIB),
        name="place_qkv",
    )(spot, *early, *middle)


def place_late_kernel(spot_ref, qkv_in_ref, *refs):
    pieces, (qkv_ref, wide, sem) = refs[:4], refs[4:]
    rows, width = pieces[0].shape
    third = width // 3
    core, x = spot_ref[CORE], spot_ref[X]
    jobs = []
    for n, ref in enumerate(pieces):
        wide[n] = ref[...].astype(F32)
        start = pl.multiple_of(((core ^ (n // 2)) * 2 + (x ^ (n % 2))) * rows, 8)
        for m in range(3):
            to = pl.ds(m * width + 2 * third, third)
            jobs.append(
                pltpu.make_async_copy(
                    wide.at[n, :, pl.ds(m * third, third)], qkv_ref.at[pl.ds(start, rows), to], sem
                )
            )
    run_copies(jobs)


def place_late(spot, qkv, late):
    smem = pl.BlockSpec(memory_space=pltpu.SMEM)
    vmem = pl.BlockSpec(memory_space=pltpu.VMEM)
    (qkv,) = outside([qkv])
    return pl.pallas_call(
        place_late_kernel,
        in_specs=[smem, ANY] + [vmem] * 4,
        out_specs=ANY,
        out_shape=jax.ShapeDtypeStruct(qkv.shape, F32),
        scratch_shapes=[pltpu.VMEM((4,) + late[0].shape, F32), pltpu.SemaphoreType.DMA],
        input_output_aliases={1: 0},
        cost_estimate=TINY,
        compiler_params=pltpu.CompilerParams(vmem_limit_bytes=14 * MIB),
        name="place_late",
    )(spot, qkv, *late)


def combine_kernel(spot_ref, *refs):
    total = None
    for ref in refs[:-1]:
        value = ref[...].astype(F32)
        value = value.reshape(value.shape[-2:])
        total = value if total is None else total + value
    refs[-1][...] = total.astype(BF16)


def combine(spot, terms, rows):
    width = terms[0][0].shape[-1]
    parts = 2 if rows % 32 == 0 else 1
    size = rows // parts
    specs = []
    for array, lead, start in terms:
        if array.ndim == 3:
            specs.append(
                pl.BlockSpec((1, size, width), lambda i, s, lead=lead, start=start: (lead(s), start(s) * parts + i, 0))
            )
        else:
            specs.append(pl.BlockSpec((size, width), lambda i, s, start=start: (start(s) * parts + i, 0)))
    return pl.pallas_call(
        combine_kernel,
        grid_spec=pltpu.PrefetchScalarGridSpec(
            num_scalar_prefetch=1,
            grid=(parts,),
            in_specs=specs,
            out_specs=pl.BlockSpec((size, width), lambda i, s: (i, 0)),
        ),
        out_shape=jax.ShapeDtypeStruct((rows, width), BF16),
        cost_estimate=TINY,
        compiler_params=pltpu.CompilerParams(vmem_limit_bytes=14 * MIB),
        name="combine",
    )(spot, *[array for array, _, _ in terms])


def narrow(terms, bit):
    return [(array, lead, lambda s, start=start: 2 * start(s) + bit(s)) for array, lead, start in terms]


def whole_term(array):
    return (array, None, lambda s: 0)


def join_kernel(spot_ref, a_ref, b_ref, o_ref):
    @pl.when(pl.program_id(0) == 0)
    def _():
        o_ref[...] = a_ref[...]

    @pl.when(pl.program_id(0) == 1)
    def _():
        o_ref[...] = b_ref[...]


def join(spot, bit, own, other):
    rows, width = own.shape
    full = pl.BlockSpec((rows, width), lambda i, s: (0, 0))
    return pl.pallas_call(
        join_kernel,
        grid_spec=pltpu.PrefetchScalarGridSpec(
            num_scalar_prefetch=1,
            grid=(2,),
            in_specs=[full, full],
            out_specs=pl.BlockSpec((rows, width), lambda i, s: (i ^ bit(s), 0)),
        ),
        out_shape=jax.ShapeDtypeStruct((2 * rows, width), BF16),
        cost_estimate=TINY,
        compiler_params=pltpu.CompilerParams(vmem_limit_bytes=14 * MIB),
        name="join",
    )(spot, own, other)


class Links:
    def __init__(self, dp, fsdp):
        self.dp, self.fsdp = dp, fsdp
        self.fast = fsdp == 2 and dp >= 4 and dp & (dp - 1) == 0
        here = lax.axis_index("dp")
        self.here = here
        self.core = here % 2
        self.x = (here // 2) % 2
        self.y = lax.axis_index("fsdp")
        self.masks = []
        mask = 4
        while mask < dp:
            self.masks.append(mask)
            mask *= 2

    def spot(self, tiles):
        values = [self.y, 2 * self.core + self.x, self.x, self.core] + tiles
        values += [(self.here // mask) % 2 for mask in self.masks]
        return jnp.stack(values).astype(jnp.int32)

    def swap(self, value, mask):
        return lax.ppermute(value, "dp", [(i, i ^ mask) for i in range(self.dp)])

    def swap_y(self, value):
        return lax.ppermute(value, "fsdp", [(0, 1), (1, 0)])

    def order(self, bit, own, other, axis=0):
        first = bit == 0
        return jnp.concatenate(
            [jnp.where(first, own, other), jnp.where(first, other, own)], axis=axis
        )

    def pieces(self, shards):
        rows = shards[0].shape[0]
        quarter = rows // 4
        start = (2 * self.core + self.x) * quarter
        return jnp.concatenate(
            [lax.dynamic_slice_in_dim(shard, start, quarter, 0) for shard in shards], axis=1
        )

    def weight_stages(self, shards):
        (first,) = yield [(self.pieces(shards), 0)]
        (second,) = yield [(first, 2)]
        rest = yield [(first, 1), (second, 1)]
        return (first, second) + tuple(rest)

    def small_gather(self, shard):
        (far,) = yield [(shard, 0)]
        return far

    def stages(self, spot, send, keep, halve):
        (near,) = yield [(send, 1)]
        keep = keep()
        half = keep.shape[1] // 2
        y, other_y = lambda s: s[Y], lambda s: 1 - s[Y]
        x, other_x = lambda s: s[X], lambda s: 1 - s[X]
        (far,) = yield [(combine(spot, [(keep, other_y, other_x), (near, other_y, other_x)], half), 0)]
        part = combine(spot, [(keep, y, other_x), (near, y, other_x), whole_term(far)], half)
        far = combine(spot, [(keep, other_y, x), (near, other_y, x)], half)
        got, far = yield [(part, 2), (far, 0)]
        terms = [(keep, y, x), (near, y, x), whole_term(far), whole_term(got)]
        masks = [(mask, lambda s, n=n: s[BITS + n]) for n, mask in enumerate(self.masks)]
        if halve:
            size = half
            for mask, bit in masks:
                size //= 2
                (got,) = yield [(combine(spot, narrow(terms, lambda s: 1 - bit(s)), size), mask)]
                terms = narrow(terms, bit) + [whole_term(got)]
            total = combine(spot, terms, size)
            for mask, bit in masks[::-1]:
                (got,) = yield [(total, mask)]
                total = join(spot, bit, total, got)
        else:
            total = combine(spot, terms, half)
            for mask, _ in masks:
                (got,) = yield [(total, mask)]
                total = combine(spot, [whole_term(total), whole_term(got)], half)
        (other,) = yield [(total, 2)]
        rest = yield [(total, 1), (other, 1)]
        return (total, other) + tuple(rest)

    def small_stages(self, send, keep):
        (got,) = yield [(send, 0)]
        total = keep + got
        for mask in [1, 2] + self.masks:
            (got,) = yield [(total, mask)]
            total = total + got
        return total

    def permute(self, value, mask):
        return self.swap(value, mask) if mask else self.swap_y(value)


class Flow:
    def __init__(self, links, run):
        self.links, self.run = links, run
        self.sends = next(run)
        self.got = None
        self.result = None

    def take(self, got):
        try:
            self.sends = self.run.send(got)
        except StopIteration as stop:
            self.result = stop.value

    def leave(self, values):
        self.got = [self.links.permute(value, mask) for value, (_, mask) in zip(values, self.sends)]


def advance(anchor, flows):
    flows = [flow for flow in flows if flow.result is None]
    if not flows:
        return anchor
    anchor, gots = lax.optimization_barrier((anchor, [flow.got for flow in flows]))
    for flow, got in zip(flows, gots):
        if got is not None:
            flow.take(got)
    going = [flow for flow in flows if flow.result is None]
    values = [[value for value, _ in flow.sends] for flow in going]
    anchor, values = lax.optimization_barrier((anchor, values))
    for flow, mine in zip(going, values):
        flow.leave(mine)
    return anchor


def make_body(dp, fsdp):
    def body(
        patches,
        page_ids,
        patch_rows,
        live_len,
        norm1_gain,
        norm1_bias,
        w_qkv,
        bias_qv,
        rel_table,
        w_proj,
        bias_proj,
        scale_attn,
        norm2_gain,
        norm2_bias,
        w_up,
        bias_up,
        w_down,
        bias_down,
        scale_mlp,
        cotangent,
    ):
        links = Links(dp, fsdp)
        smalls = (
            norm1_gain,
            norm1_bias,
            scale_attn,
            bias_proj,
            norm2_gain,
            norm2_bias,
            scale_mlp,
            bias_down,
            bias_qv,
            rel_table,
            bias_up,
        )
        total, width = patches.shape[1:]
        fast = links.fast
        pieces = 2 if fast else 1
        hidden = w_up.shape[1]
        tiles = [0, 1, 2, 3]
        if fast:
            tiles = [1 - links.core, links.core, 3 - links.core, 2 + links.core]
        spot = lax.optimization_barrier(links.spot(tiles))

        x, cot = patches[0], cotangent[0]
        if fast:
            loads = [
                Flow(links, links.weight_stages(group)) for group in ([w_qkv], [w_proj, w_up], [w_down])
            ]
            small = smalls[:9] + smalls[10:] + smalls[9:10]
            x, small = advance((x, small), loads[:1])
            mine = pack_small(small)
            far = Flow(links, links.small_gather(mine))
            x = advance(x, [far])
            x, query_side, key_side = rotate_ids(page_ids, patch_rows, live_len, x)
            x, cot = advance((x, cot), [far] + loads[:2])
            cot = rotate(page_ids, cot)
            vectors, bias_all, bias_hidden, mix = unpack_small(spot, mine, far.result)
            x, cot = lax.optimization_barrier((x, cot))
            (x, cot, mix) = advance((x, cot, mix), loads[:2])
            x, mix = advance((x, mix), loads[:1] + loads[2:])
            weight_qkv = Weight((w_qkv,) + loads[0].result, width, 3 * width)
        else:
            x, query_side, key_side = rotate_ids(page_ids, patch_rows, live_len, x)
            cot = rotate(page_ids, cot)
            mine = jnp.concatenate([small.reshape(-1) for small in smalls])
            packed = lax.all_gather(mine, "fsdp", axis=0, tiled=False)
            share = width // fsdp
            vectors = packed[:, : 8 * share].reshape(fsdp, 8, share).transpose(1, 0, 2).reshape(8, width).astype(F32)
            at = 8 * share
            whole = []
            for small in smalls[8:]:
                piece = packed[:, at : at + small.size]
                whole.append(piece.reshape((small.shape[0] * fsdp,) + small.shape[1:]).astype(F32))
                at += small.size
            bias_qv_f, table, bias_hidden = whole
            bias_all = jnp.concatenate([bias_qv_f[:width], jnp.zeros((width,), F32), bias_qv_f[width:]])[None]
            bias_hidden = bias_hidden.reshape(pieces, -1, 768 // pieces).transpose(1, 0, 2).reshape(-1, 1, 768)
            mix = bias_mix(table)
            weight_qkv, weight_proj, weight_up, weight_down = [
                Weight([lax.all_gather(shard, "fsdp", axis=0, tiled=True)], shard.shape[0] * fsdp, shard.shape[1])
                for shard in (w_qkv, w_proj, w_up, w_down)
            ]
        x, mix = lax.optimization_barrier((x, mix))
        normed1, qkv = project_qkv(spot, x, vectors, bias_all, weight_qkv)
        if fast:
            qkv = advance(qkv, loads)
        attended, lse = attention(qkv, query_side, key_side, mix)
        if fast:
            attended = advance(attended, loads)
            weight_proj = Weight((w_proj,) + loads[1].result, width, width)
            weight_up = Weight((w_up,) + loads[1].result, width, hidden, width)
        branch, normed2, dmlp = merge_branch(spot, attended, x, cot, vectors, weight_proj)
        if fast:
            normed2 = advance(normed2, loads)
            weight_down = Weight((w_down,) + loads[2].result, hidden, width)

        flows = []

        def launch(run):
            if links.fast:
                flows.append(Flow(links, run))

        def go(anchor):
            return advance(anchor, flows) if links.fast else anchor

        old = None
        mlp_grads, up_sums = [], []
        for number in range(4):
            chunk, second = divmod(number, 2)
            out, back, grad, sums = mlp(
                spot, number, normed2, dmlp, old, bias_hidden, weight_up, weight_down, pieces
            )
            mlp_grads.append(grad)
            up_sums.append(sums)
            if not second:
                launch(links.stages(spot, grad, lambda chunk=chunk: mlp_grads[2 * chunk + 1], True))
            old = go((out, back))
        branch_m, back = old
        dresid, datt, proj_grad, sums2 = branch_back(
            spot, back, x, branch, cot, attended, vectors, weight_proj, pieces
        )
        datt = go(datt)

        d_parts, sums_qv, tabs, units = [], [], [], []
        for number in range(3):
            d_part, sums, tab = attention_back(
                qkv, datt, attended, lse, query_side, key_side, mix, 2 * number, 2
            )
            sums_qv.append(sums)
            tabs.append(tab)
            datt, d_part = go((datt, d_part))
            d_parts.append(d_part)
            columns = [(d_part, 0), (d_part, 1), (d_part, 2)]
            unit = weight_unit(spot, normed1, columns, pieces, fast, proj_grad if fast and number == 0 else None)
            if fast:
                launch(links.stages(spot, unit[0], lambda unit=unit: unit[1], number == 0))
            units.append(unit)
            anchor = d_part if number == 2 else datt
            anchor = advance(anchor, flows[-1:] if number == 1 else flows) if fast else anchor
            if number == 2:
                d_parts[2] = anchor
            else:
                datt = anchor

        halves = []
        for first in range(0, total // 256, 2):
            half, sums = finish(
                spot, d_parts, x, dresid, branch, branch_m, cot, dmlp, vectors, weight_qkv, first, 2
            )
            half, dmlp = go((half, dmlp))
            halves.append((half, sums))
        (upper, sums_a), (lower, sums_b) = halves
        if fast:
            send, keep = pack_grads(spot, sums_a, sums_b, sums2, sums_qv, up_sums, tabs)
            launch(links.small_stages(send, keep))
            upper = advance(upper, flows[-1:])
            layer_out, grad_patches = unrotate(page_ids, upper, lower)
            layer_out, grad_patches = go((layer_out, grad_patches))
            out_w_up, out_w_down = place_mlp(spot, flows[0].result + flows[1].result, hidden)
            out_w_up, out_w_down = go((out_w_up, out_w_down))
            out_w_qkv = None
            while any(flow.result is None for flow in flows):
                if out_w_qkv is None and flows[2].result and flows[3].result:
                    out_w_qkv, out_w_proj = place_qkv(spot, flows[2].result, flows[3].result)
                    layer_out, out_w_qkv, out_w_proj = lax.optimization_barrier((layer_out, out_w_qkv, out_w_proj))
                layer_out = go(layer_out)
            if out_w_qkv is None:
                out_w_qkv, out_w_proj = place_qkv(spot, flows[2].result, flows[3].result)
            out_w_qkv = place_late(spot, out_w_qkv, flows[4].result)
            g = unpack_grads(flows[5].result)
            small_outs = [g[0], g[1], g[8], g[9], g[3], g[2], g[4], g[5], g[10], g[7], g[6]]
        else:
            layer_out, grad_patches = unrotate(page_ids, upper, lower)
            sums1 = sums_a + sums_b
            sums_qv = jnp.concatenate(sums_qv, axis=1)
            small_grads = [
                sums1[0],
                sums1[1],
                jnp.concatenate([sums_qv[0], sums_qv[1]]),
                table_gradient(jnp.concatenate(tabs, axis=0)),
                sums2[3],
                sums2[2],
                sums2[0],
                sums2[1],
                jnp.concatenate(up_sums, axis=0).reshape(-1),
                sums1[3],
                sums1[2],
            ]
            flat = jnp.concatenate([grad.reshape(fsdp, -1) for grad in small_grads], axis=1)
            summed = lax.psum_scatter(lax.psum(flat, "dp"), "fsdp", scatter_dimension=0, tiled=True)[0]
            small_outs = []
            at = 0
            for grad in small_grads:
                size = grad.size // fsdp
                small_outs.append(summed[at : at + size].reshape((grad.shape[0] // fsdp,) + grad.shape[1:]))
                at += size
            stacks = jnp.concatenate(mlp_grads, axis=1).astype(F32).reshape(-1, 2, width, width)
            qkv_units = [unit[0].astype(F32) for unit in units]
            third = width // 3
            fulls = (
                jnp.concatenate([unit[:, n * third : (n + 1) * third] for n in range(3) for unit in qkv_units], axis=1),
                proj_grad[0].astype(F32),
                jnp.concatenate([stacks[t, 0] for t in range(stacks.shape[0])], axis=1),
                stacks[:, 1].reshape(-1, width),
            )
            out_w_qkv, out_w_proj, out_w_up, out_w_down = [
                lax.psum(lax.psum_scatter(grad, "fsdp", scatter_dimension=0, tiled=True), "dp") for grad in fulls
            ]
        return (
            layer_out[None],
            grad_patches[None],
            small_outs[0],
            small_outs[1],
            out_w_qkv,
            small_outs[2],
            small_outs[3],
            out_w_proj,
            small_outs[4],
            small_outs[5],
            small_outs[6],
            small_outs[7],
            out_w_up,
            small_outs[8],
            out_w_down,
            small_outs[9],
            small_outs[10],
        )

    return body


def solution(mesh):
    rows = P(("dp", "fsdp"), None, None)
    ids = P(("dp", "fsdp"), None)
    vector = P("fsdp")
    matrix = P("fsdp", None)
    in_specs = (
        rows,
        ids,
        ids,
        ids,
        vector,
        vector,
        matrix,
        vector,
        matrix,
        matrix,
        vector,
        vector,
        vector,
        vector,
        matrix,
        vector,
        matrix,
        vector,
        vector,
        rows,
    )
    out_specs = (
        rows,
        rows,
        vector,
        vector,
        matrix,
        vector,
        matrix,
        matrix,
        vector,
        vector,
        vector,
        vector,
        matrix,
        vector,
        matrix,
        vector,
        vector,
    )
    body = make_body(mesh.shape["dp"], mesh.shape["fsdp"])
    return jax.shard_map(body, mesh=mesh, in_specs=in_specs, out_specs=out_specs, check_vma=False)
```
